512 devices in a mesh: row: 16 (over x, y_hi, core), col: 8 (over z), tp: 4 (over y_lo).
Axes of the slice: x: 4, y: 8 (y_hi: 2, y_lo: 4; y = y_hi * 4 + y_lo), z: 8, core: 2. Of those that a mesh axis runs over, the one named last changes fastest.
Arguments:
- latent: bfloat16 [256, 128, 1024], P('row', 'col'), may hold values from -6 to 6
- norm_gain: float32 [1024], replicated, may hold values from 0.1 to 1.9
- qkv_weight: bfloat16 [1024, 3, 1024], P(None, None, 'tp'), may hold values from -4 to 4
- out_weight: bfloat16 [1024, 1024], P('tp'), may hold values from -0.1875 to 0.1875
- cotangent: bfloat16 [256, 128, 1024], P('row', 'col'), may hold values from -6 to 6
Outputs:
- latent_grad: float32 [256, 128, 1024], P(('row', 'tp'), 'col')
The draws below stay inside these ranges and needn't reach their ends.
All inputs are finite; a program needn't handle non-finite values.
Results may differ from the reference program's by a relative error of at most 0.009.
Values may be sent and summed in bfloat16 or wider, within the bound.
No kernel may reach another device: no remote copies, remote signals or barrier semaphores. Data moves between devices by JAX's collectives and lax.ppermute only.
A program may use at most 64 MiB of HBM per device.

```python
import jax
import jax.numpy as jnp
from jax import lax

D = 1024
HEADS = 16
HEAD_DIM = 64
RADIUS = 3
IMG_H = 256
IMG_W = 128
N_TP = 4


def draw_qkv_weight(key, part):
    first_key = jax.random.fold_in(key, 0)
    base = jax.random.truncated_normal(first_key, -6.0, 6.0, (D, 3, HEADS * HEAD_DIM), jnp.float32) * D ** (-0.5)
    return base.astype(jnp.bfloat16)


def levels(key, shape, cuts, low, top_value):
    def one(axis_at, shards_of):
        steps = jax.random.uniform(jax.random.fold_in(jax.random.fold_in(key, 6), axis_at), (shards_of,), jnp.float32, low / len(cuts), top_value / len(cuts))
        return jnp.repeat(jnp.exp(steps), shape[axis_at] // shards_of).reshape((-1,) + (1,) * (len(shape) - axis_at - 1))

    level = one(*cuts[0])
    for cut in cuts[1:]:
        level = level * one(*cut)
    return level


def gaussian(stream_key, dims, scale, most, cuts=(), kind=jnp.bfloat16):
    result = jax.random.normal(stream_key, dims, jnp.float32) * scale
    if len(cuts) > 0:
        result = levels(stream_key, dims, cuts, -0.22, 0.18) * result
    return jnp.clip(result, min=-most, max=most).astype(kind)


def setup_inputs(seed: int = 0) -> dict:
    arg_keys = jax.random.split(jax.random.key(seed), 6)
    return {
        "latent": gaussian(arg_keys[0], (IMG_H, IMG_W, D), 1.0, 6.0, ((0, 16), (1, 8))),
        "norm_gain": jnp.clip(1.0 + 0.18 * jax.random.normal(arg_keys[1], (D,), jnp.float32), 0.1, 1.9),
        "qkv_weight": draw_qkv_weight(jax.random.fold_in(arg_keys[5], 71), 0),
        "out_weight": gaussian(arg_keys[3], (HEADS * HEAD_DIM, D), (HEADS * HEAD_DIM) ** -0.5, 0.1875, ((0, 4),)),
        "cotangent": gaussian(arg_keys[4], (IMG_H, IMG_W, D), 1.0, 6.0, ((0, 16), (1, 8))),
    }


block_side = 8

def to_regions(field, block_rows, block_cols):
    region_side = block_side + 2 * RADIUS
    grow = block_side - 2 * RADIUS
    padded = jnp.pad(field, ((0, grow), (0, grow), (0, 0)))
    wide_cols = padded.shape[1]
    channels = padded.shape[2]
    span_rows = block_rows * block_side
    upper = padded[:span_rows].reshape(block_rows, block_side, wide_cols, channels)
    lower = padded[block_side:span_rows + block_side].reshape(block_rows, block_side, wide_cols, channels)[:, :2 * RADIUS]
    banded = jnp.concatenate([upper, lower], axis=1)
    span_cols = block_cols * block_side
    left_part = banded[:, :, :span_cols].reshape(block_rows, region_side, block_cols, block_side, channels)
    right_part = banded[:, :, block_side:span_cols + block_side].reshape(block_rows, region_side, block_cols, block_side, channels)[:, :, :, :2 * RADIUS]
    tiles = jnp.concatenate([left_part, right_part], axis=3).transpose(0, 2, 1, 3, 4)
    return tiles.reshape(block_rows, block_cols, region_side * region_side, channels)

def fold_lead(grads):
    block_count = grads.shape[0]
    middle = grads[:, RADIUS:RADIUS + block_side]
    top_rim = grads[:, :RADIUS]
    bottom_rim = grads[:, RADIUS + block_side:]
    middle = middle.at[1:, :RADIUS].add(bottom_rim[:-1])
    middle = middle.at[:-1, block_side - RADIUS:].add(top_rim[1:])
    rest = grads.shape[2:]
    return jnp.concatenate([top_rim[0], middle.reshape((block_count * block_side,) + rest), bottom_rim[-1]], axis=0)

def from_regions(grads, block_rows, block_cols):
    region_side = block_side + 2 * RADIUS
    channels = grads.shape[-1]
    shaped = grads.reshape(block_rows, block_cols, region_side, region_side, channels).transpose(1, 3, 0, 2, 4)
    folded = fold_lead(shaped).transpose(1, 2, 0, 3)
    return fold_lead(folded)

def window_mask():
    region_side = block_side + 2 * RADIUS
    spots = jnp.arange(block_side, dtype=jnp.int32)[:, None]
    cells = jnp.arange(region_side, dtype=jnp.int32)[None, :]
    near = (cells >= spots) & (cells <= spots + 2 * RADIUS)
    both = near[:, None, :, None] & near[None, :, None, :]
    return both.reshape(block_side * block_side, region_side * region_side)

def core(query_blocks, upstream_blocks, key_regions, value_regions, allowed):
    scale = HEAD_DIM ** (-0.5)
    highest = lax.Precision.HIGHEST
    raw = jnp.einsum('nqhd,nkhd->nhqk', query_blocks.astype(jnp.float32), key_regions.astype(jnp.float32))
    scores = jnp.where(allowed[:, None], raw * scale, -1e+30)
    peak = lax.optimization_barrier(jnp.max(scores, axis=-1, keepdims=True))
    exponent = jnp.exp(scores - peak)
    weights = exponent / lax.optimization_barrier(jnp.sum(exponent, axis=-1, keepdims=True))
    value_dots = jnp.einsum('nqhd,nkhd->nhqk', upstream_blocks.astype(jnp.float32), value_regions.astype(jnp.float32))
    centre = lax.optimization_barrier(jnp.sum(weights * value_dots, axis=-1, keepdims=True))
    score_grads = weights * (value_dots - centre)
    query_grad = jnp.einsum('nhqk,nkhd->nqhd', score_grads, key_regions.astype(jnp.float32), precision=highest) * scale
    key_grad = jnp.einsum('nhqk,nqhd->nkhd', score_grads, query_blocks.astype(jnp.float32), precision=highest) * scale
    value_grad = jnp.einsum('nhqk,nqhd->nkhd', weights, upstream_blocks.astype(jnp.float32), precision=highest)
    return (query_grad, key_grad, value_grad)

def attend(query, grad_out, neighbours, valid_cells):
    tile_rows, tile_cols, head_cols = query.shape
    head_count = head_cols // HEAD_DIM
    block_rows = tile_rows // block_side
    block_cols = tile_cols // block_side
    cells = block_side * block_side

    def to_blocks(field):
        shaped = field.reshape(block_rows, block_side, block_cols, block_side, head_count, HEAD_DIM)
        return shaped.transpose(0, 2, 1, 3, 4, 5).reshape(block_rows, block_cols, cells, head_count, HEAD_DIM)
    query_blocks = to_blocks(query)
    upstream_blocks = to_blocks(grad_out)
    regions = to_regions(neighbours, block_rows, block_cols)
    region_cells = regions.shape[2]
    key_regions = regions[..., :head_cols].reshape(block_rows, block_cols, region_cells, head_count, HEAD_DIM)
    value_regions = regions[..., head_cols:].reshape(block_rows, block_cols, region_cells, head_count, HEAD_DIM)
    valid_regions = to_regions(valid_cells[:, :, None], block_rows, block_cols)[..., 0]
    allowed = window_mask()[None, None] & valid_regions[:, :, None, :]

    def one_band(pieces):
        return core(pieces[0], pieces[1], pieces[2], pieces[3], pieces[4])
    query_grad, key_grad, value_grad = lax.map(one_band, (query_blocks, upstream_blocks, key_regions, value_regions, allowed))
    query_grad = query_grad.reshape(block_rows, block_cols, block_side, block_side, head_cols)
    query_grad = query_grad.transpose(0, 2, 1, 3, 4).reshape(tile_rows, tile_cols, head_cols)
    pair_grad = jnp.concatenate([key_grad.reshape(block_rows, block_cols, region_cells, head_cols), value_grad.reshape(block_rows, block_cols, region_cells, head_cols)], axis=-1)
    spread = from_regions(pair_grad, block_rows, block_cols)
    return (query_grad, spread)

def reference(latent, norm_gain, qkv_weight, out_weight, cotangent):
    image_rows, image_cols, model_width = latent.shape
    token_count = image_rows * image_cols
    head_cols = HEADS * HEAD_DIM // N_TP
    latent_f32 = latent.astype(jnp.float32)
    inverse = lax.rsqrt(lax.optimization_barrier(jnp.mean(latent_f32 * latent_f32, axis=-1, keepdims=True)) + 1e-06)
    unit = latent_f32 * inverse
    normed = (unit * norm_gain).astype(jnp.bfloat16).reshape(token_count, model_width)
    upstream_flat = cotangent.reshape(token_count, model_width)
    valid_cells = jnp.pad(jnp.ones((image_rows, image_cols), jnp.bool_), RADIUS)

    def one_group(summed, group_index):
        begin = (group_index * head_cols).astype(jnp.int32)
        projection = lax.dynamic_slice_in_dim(qkv_weight, begin, head_cols, 2).reshape(model_width, 3 * head_cols)
        back_weight = lax.dynamic_slice_in_dim(out_weight, begin, head_cols, 0)
        projected = jnp.dot(normed, projection, preferred_element_type=jnp.float32).astype(jnp.bfloat16)
        projected = projected.reshape(token_count, 3, head_cols)
        query = projected[:, 0].reshape(image_rows, image_cols, head_cols)
        pairs = jnp.concatenate([projected[:, 1], projected[:, 2]], axis=-1).reshape(image_rows, image_cols, 2 * head_cols)
        neighbours = jnp.pad(pairs, ((RADIUS, RADIUS), (RADIUS, RADIUS), (0, 0)))
        grad_out = jnp.dot(upstream_flat, back_weight.T, preferred_element_type=jnp.float32).astype(jnp.bfloat16)
        grad_out = grad_out.reshape(image_rows, image_cols, head_cols)
        query_grad, spread = attend(query, grad_out, neighbours, valid_cells)
        inner = spread[RADIUS:RADIUS + image_rows, RADIUS:RADIUS + image_cols]
        stacked = jnp.stack([query_grad, inner[..., :head_cols], inner[..., head_cols:]], axis=2)
        stacked = stacked.astype(jnp.bfloat16).reshape(token_count, 3 * head_cols)
        partial_sum = jnp.dot(stacked, projection.T, preferred_element_type=jnp.float32)
        rounded = lax.optimization_barrier(partial_sum.astype(jnp.bfloat16))
        return (summed + rounded.astype(jnp.float32), None)
    summed, ignored = lax.scan(one_group, jnp.zeros((token_count, model_width), jnp.float32), jnp.arange(N_TP, dtype=jnp.int32))
    scaled = summed.reshape(image_rows, image_cols, model_width) * norm_gain
    stat = lax.optimization_barrier(jnp.mean(scaled * unit, axis=-1, keepdims=True))
    return cotangent.astype(jnp.float32) + inverse * (scaled - unit * stat)
```

```python
import jax
import jax.numpy as jnp
import numpy as np
from jax import lax
from jax.experimental import pallas as pl
from jax.experimental.pallas import tpu as pltpu
from jax.sharding import PartitionSpec as P

HEAD_DIM = 64
RADIUS = 3
REACH = 2 * RADIUS
SIDE = 16
WIDE = SIDE + 2 * REACH
TALL = SIDE + 2 * RADIUS
KV_ROWS = REACH * SIDE
QG_ROWS = RADIUS * SIDE
KV_EDGE = 176
QG_EDGE = 80
KEYS = WIDE * SIDE + 2 * KV_EDGE
QUERIES = TALL * SIDE + 2 * QG_EDGE
FAR = 1000.0
bf16 = jnp.bfloat16
f32 = jnp.float32
VMEM = pl.BlockSpec(memory_space=pltpu.VMEM)
SMEM = pl.BlockSpec(memory_space=pltpu.SMEM)
PARAMS = pltpu.CompilerParams(vmem_limit_bytes=56 * 1024 * 1024)


def nt(a, b):
    return lax.dot_general(a, b, (((1,), (1,)), ((), ())), preferred_element_type=f32)


def nn(a, b):
    return jnp.dot(a, b, preferred_element_type=f32)


def edge_picks():
    def pick(out_rows, in_rows, count, lines, first):
        table = np.zeros((out_rows, in_rows), np.float32)
        for line in range(lines):
            for step in range(count):
                table[line * count + step, line * SIDE + first + step] = 1.0
        return table

    kv_low = pick(KV_EDGE, WIDE * SIDE, REACH, WIDE, 0)
    kv_high = pick(KV_EDGE, WIDE * SIDE, REACH, WIDE, SIDE - REACH)
    qg_low = pick(QG_EDGE, TALL * SIDE, RADIUS, TALL, 0)
    qg_high = pick(QG_EDGE, TALL * SIDE, RADIUS, TALL, SIDE - RADIUS)
    return [jnp.asarray(t, bf16) for t in (kv_low, kv_high, qg_low, qg_high)]


def places():
    def coords(lines, reach, edge_rows):
        ys, xs = [], []
        for line in range(lines):
            for x in range(SIDE):
                ys.append(line - reach)
                xs.append(x)
        for first in (-reach, SIDE):
            begin = len(ys)
            for line in range(lines):
                for step in range(reach):
                    ys.append(line - reach)
                    xs.append(first + step)
            while len(ys) < begin + edge_rows:
                ys.append(FAR)
                xs.append(FAR)
        return np.asarray(ys, np.float32), np.asarray(xs, np.float32)

    key_y, key_x = coords(WIDE, REACH, KV_EDGE)
    query_y, query_x = coords(TALL, RADIUS, QG_EDGE)
    keys = np.stack([key_y, key_x], axis=1)
    queries = np.stack([query_y, query_x], axis=0)
    queries = np.where(queries == FAR, -FAR, queries)
    return jnp.asarray(keys), jnp.asarray(queries)


def project_kernel(latent, gain, weight, out_weight, cotangent, kv, qg, upper, lower):
    tokens = latent[...].astype(f32)
    inverse = lax.rsqrt(jnp.mean(tokens * tokens, axis=-1, keepdims=True) + 1e-06)
    normed = (tokens * inverse * gain[...]).astype(bf16)
    width = out_weight.shape[0]
    grad_out = nt(cotangent[...], out_weight[...]).astype(bf16)
    query = nn(normed, weight[0]).astype(bf16)
    qg[:, :width] = query * jnp.asarray(HEAD_DIM ** (-0.5), bf16)
    kv[:, :width] = nn(normed, weight[1]).astype(bf16)
    kv[:, width:] = nn(normed, weight[2]).astype(bf16)
    qg[:, width:] = grad_out
    count = latent.shape[0]
    upper[:KV_ROWS] = kv[:KV_ROWS]
    upper[KV_ROWS:] = qg[:QG_ROWS]
    lower[:KV_ROWS] = kv[count - KV_ROWS :]
    lower[KV_ROWS:] = qg[count - QG_ROWS :]


def edges_kernel(kv, qg, above, below, kv_low, kv_high, qg_low, qg_high, left, right):
    kv_all = jnp.concatenate([above[:KV_ROWS], kv[...], below[:KV_ROWS]], axis=0)
    qg_all = jnp.concatenate([above[KV_ROWS:], qg[...], below[KV_ROWS:]], axis=0)
    left[:KV_EDGE] = nn(kv_low[...], kv_all).astype(bf16)
    left[KV_EDGE:] = nn(qg_low[...], qg_all).astype(bf16)
    right[:KV_EDGE] = nn(kv_high[...], kv_all).astype(bf16)
    right[KV_EDGE:] = nn(qg_high[...], qg_all).astype(bf16)


def attend_kernel(
    limits, kv, qg, above, below, from_left, from_right, keys, queries, weight, partial, bias
):
    width = kv.shape[1] // 2
    count = kv.shape[0]
    key_y, key_x = keys[:, 0:1], keys[:, 1:2]
    query_y, query_x = queries[0:1, :], queries[1:2, :]
    top, bottom = limits[0].astype(f32), limits[1].astype(f32)
    left, right = limits[2].astype(f32), limits[3].astype(f32)
    inside = (key_y >= top) & (key_y <= bottom) & (key_x >= left) & (key_x <= right)
    key_y = jnp.where(inside, key_y, FAR)
    near = (jnp.abs(key_y - query_y) <= RADIUS) & (jnp.abs(key_x - query_x) <= RADIUS)
    bias[...] = jnp.where(near, 0.0, -1e30)

    kv_all = jnp.concatenate(
        [above[:KV_ROWS], kv[...], below[:KV_ROWS], from_left[:KV_EDGE], from_right[:KV_EDGE]],
        axis=0,
    )
    qg_all = jnp.concatenate(
        [above[KV_ROWS:], qg[...], below[KV_ROWS:], from_left[KV_EDGE:], from_right[KV_EDGE:]],
        axis=0,
    )
    key, value = kv_all[:, :width], kv_all[:, width:]
    query, upstream = qg_all[:, :width], qg_all[:, width:]
    key_t = key.astype(f32).T.astype(bf16)
    lanes = lax.broadcasted_iota(jnp.int32, (1, width), 1) // HEAD_DIM
    own = slice(KV_ROWS, KV_ROWS + count)
    key_grad = jnp.zeros((count, width), f32)
    value_grad = jnp.zeros((count, width), f32)
    query_parts = []
    for head in range(width // HEAD_DIM):
        mine = lanes == head
        query_h = jnp.where(mine, query, jnp.zeros_like(query))
        upstream_h = jnp.where(mine, upstream, jnp.zeros_like(upstream))
        scores = nt(key, query_h) + bias[...]
        dots = nt(value, upstream_h)
        exponent = jnp.exp(scores - jnp.max(scores, axis=0, keepdims=True))
        scale = 1.0 / jnp.sum(exponent, axis=0, keepdims=True)
        weights = exponent * scale
        centre = jnp.sum(weights * dots, axis=0, keepdims=True)
        score_grads = (weights * (dots - centre)).astype(bf16)
        value_grad += nn(weights[own].astype(bf16), upstream_h)
        key_grad += nn(score_grads[own], query_h)
        query_parts.append(nn(key_t[head * HEAD_DIM : (head + 1) * HEAD_DIM], score_grads))
    query_grad = jnp.concatenate(query_parts, axis=0).T[QG_ROWS : QG_ROWS + count]
    query_grad = query_grad * (HEAD_DIM ** (-0.5))
    total = nt(query_grad.astype(bf16), weight[0])
    total += nt(key_grad.astype(bf16), weight[1])
    total += nt(value_grad.astype(bf16), weight[2])
    partial[...] = total.astype(bf16)


def finish_kernel(place, received, latent, gain, cotangent, result):
    count = received.shape[1]
    first = pl.multiple_of(place[0] * count, count)
    tokens = latent[pl.ds(first, count), :].astype(f32)
    upstream = cotangent[pl.ds(first, count), :].astype(f32)
    summed = received[0].astype(f32)
    for part in range(1, received.shape[0]):
        summed += received[part].astype(f32)
    inverse = lax.rsqrt(jnp.mean(tokens * tokens, axis=-1, keepdims=True) + 1e-06)
    unit = tokens * inverse
    scaled = summed * gain[...]
    stat = jnp.mean(scaled * unit, axis=-1, keepdims=True)
    result[...] = upstream + inverse * (scaled - unit * stat)


def moved(block, axis, distance):
    count = lax.axis_size(axis)
    route = [(i, i + distance) for i in range(count) if 0 <= i + distance < count]
    return lax.ppermute(block, axis, route)


def per_device(latent, norm_gain, qkv_weight, out_weight, cotangent):
    tile_rows, tile_cols, model_width = latent.shape
    head_cols = out_weight.shape[0]
    count = tile_rows * tile_cols
    tp = lax.axis_size("tp")
    flat_latent = latent.reshape(count, model_width)
    flat_cotangent = cotangent.reshape(count, model_width)
    gain = norm_gain.reshape(1, model_width)
    weight = qkv_weight.transpose(1, 0, 2)
    shape = jax.ShapeDtypeStruct
    edge = shape((KV_ROWS + QG_ROWS, 2 * head_cols), bf16)
    kv, qg, upper, lower = pl.pallas_call(
        project_kernel,
        out_shape=[shape((count, 2 * head_cols), bf16)] * 2 + [edge] * 2,
        in_specs=[VMEM] * 5,
        out_specs=[VMEM] * 4,
        compiler_params=PARAMS,
        name="project",
    )(flat_latent, gain, weight, out_weight, flat_cotangent)
    above = moved(lower, "row", 1)
    below = moved(upper, "row", -1)
    side = shape((KV_EDGE + QG_EDGE, 2 * head_cols), bf16)
    leftward, rightward = pl.pallas_call(
        edges_kernel,
        out_shape=[side] * 2,
        in_specs=[VMEM] * 8,
        out_specs=[VMEM] * 2,
        compiler_params=PARAMS,
        name="edges",
    )(kv, qg, above, below, *edge_picks())
    from_left = moved(rightward, "col", 1)
    from_right = moved(leftward, "col", -1)
    row, col = lax.axis_index("row"), lax.axis_index("col")
    limits = jnp.stack(
        [
            -row * tile_rows,
            (lax.axis_size("row") - row) * tile_rows - 1,
            -col * tile_cols,
            (lax.axis_size("col") - col) * tile_cols - 1,
        ]
    ).astype(jnp.int32)
    partial = pl.pallas_call(
        attend_kernel,
        out_shape=shape((count, model_width), bf16),
        in_specs=[SMEM] + [VMEM] * 9,
        out_specs=VMEM,
        scratch_shapes=[pltpu.VMEM((KEYS, QUERIES), f32)],
        compiler_params=PARAMS,
        name="attend",
    )(limits, kv, qg, above, below, from_left, from_right, *places(), weight)
    own = count // tp
    received = lax.all_to_all(partial.reshape(tp, own, model_width), "tp", 0, 0)
    place = lax.axis_index("tp").astype(jnp.int32).reshape(1)
    result = pl.pallas_call(
        finish_kernel,
        out_shape=shape((own, model_width), f32),
        in_specs=[SMEM] + [VMEM] * 4,
        out_specs=VMEM,
        compiler_params=PARAMS,
        name="finish",
    )(place, received, flat_latent, gain, flat_cotangent)
    return result.reshape(own // tile_cols, tile_cols, model_width)


def solution(mesh):
    placed = (P("row", "col", None), P(), P(None, None, "tp"), P("tp", None), P("row", "col", None))
    return jax.shard_map(
        per_device,
        mesh=mesh,
        in_specs=placed,
        out_specs=P(("row", "tp"), "col", None),
        check_vma=False,
    )
```

```python
import jax
import jax.numpy as jnp
import numpy as np
from jax import lax
from jax.experimental import pallas as pl
from jax.experimental.pallas import tpu as pltpu
from jax.sharding import PartitionSpec as P

HEAD_DIM = 64
RADIUS = 3
REACH = 2 * RADIUS
SIDE = 16
WIDE = SIDE + 2 * REACH
TALL = SIDE + 2 * RADIUS
KV_ROWS = REACH * SIDE
QG_ROWS = RADIUS * SIDE
KV_EDGE = 176
QG_EDGE = 80
MIDDLE = SIDE - 2 * RADIUS
MID_QUERIES = 224
OWN_FROM = 32
OWN_EDGE = 112
FAR = 1000.0
bf16 = jnp.bfloat16
f32 = jnp.float32
VMEM = pl.BlockSpec(memory_space=pltpu.VMEM)
SMEM = pl.BlockSpec(memory_space=pltpu.SMEM)
PARAMS = pltpu.CompilerParams(vmem_limit_bytes=56 * 1024 * 1024)


def nt(a, b):
    return lax.dot_general(a, b, (((1,), (1,)), ((), ())), preferred_element_type=f32)


def nn(a, b):
    return jnp.dot(a, b, preferred_element_type=f32)


def table(out_rows, in_rows, pairs):
    filled = np.zeros((out_rows, in_rows), np.float32)
    for target, source in pairs:
        filled[target, source] = 1.0
    return jnp.asarray(filled, bf16)


def strip_pairs(lines, count, first):
    return [
        (line * count + step, line * SIDE + first + step)
        for line in range(lines)
        for step in range(count)
    ]


def edge_picks():
    return [
        table(KV_EDGE, WIDE * SIDE, strip_pairs(WIDE, REACH, 0)),
        table(KV_EDGE, WIDE * SIDE, strip_pairs(WIDE, REACH, SIDE - REACH)),
        table(QG_EDGE, TALL * SIDE, strip_pairs(TALL, RADIUS, 0)),
        table(QG_EDGE, TALL * SIDE, strip_pairs(TALL, RADIUS, SIDE - RADIUS)),
    ]


def middle_picks():
    pairs = strip_pairs(TALL, MIDDLE, RADIUS)
    gather = table(MID_QUERIES, TALL * SIDE, pairs)
    own = [
        (source - QG_ROWS, target)
        for target, source in pairs
        if 0 <= source - QG_ROWS < SIDE * SIDE
    ]
    return gather, table(SIDE * SIDE, MID_QUERIES, own)


def side_spreads():
    key_pairs, query_pairs = [], []
    for part, first in enumerate((0, SIDE - REACH)):
        for target, source in strip_pairs(WIDE, REACH, first):
            if 0 <= source - KV_ROWS < SIDE * SIDE:
                key_pairs.append((source - KV_ROWS, part * OWN_EDGE + target - OWN_FROM))
    for part, first in enumerate((0, SIDE - RADIUS)):
        for target, source in strip_pairs(TALL, RADIUS, first):
            if 0 <= source - QG_ROWS < SIDE * SIDE:
                query_pairs.append((source - QG_ROWS, part * QG_EDGE + target))
    return (
        table(SIDE * SIDE, 2 * OWN_EDGE, key_pairs),
        table(SIDE * SIDE, 2 * QG_EDGE, query_pairs),
    )


def coords(lines, reach, first, count, total, pad):
    ys = [float(line - reach) for line in range(lines) for _ in range(count)]
    xs = [float(first + step) for _ in range(lines) for step in range(count)]
    spare = [pad] * (total - len(ys))
    return np.asarray([ys + spare, xs + spare], np.float32)


def middle_places(heads):
    keys = coords(WIDE, REACH, 0, SIDE, WIDE * SIDE, FAR)
    queries = coords(TALL, RADIUS, RADIUS, MIDDLE, MID_QUERIES, -FAR)
    return jnp.asarray(keys.T), jnp.asarray(np.tile(queries, (1, heads)))


def side_places(heads):
    spots = []
    for key_firsts, query_firsts in (
        ((0, -REACH), (0, -RADIUS)),
        ((SIDE - REACH, SIDE), (SIDE - RADIUS, SIDE)),
    ):
        keys = [coords(WIDE, REACH, f, REACH, KV_EDGE, FAR) for f in key_firsts]
        queries = [coords(TALL, RADIUS, f, RADIUS, QG_EDGE, -FAR) for f in query_firsts]
        spots.append(jnp.asarray(np.concatenate(keys, axis=1).T))
        spots.append(jnp.asarray(np.tile(np.concatenate(queries, axis=1), (1, heads))))
    return spots


def project_kernel(latent, gain, weight, out_weight, cotangent, kv, qg, upper, lower):
    tokens = latent[...].astype(f32)
    inverse = lax.rsqrt(jnp.mean(tokens * tokens, axis=-1, keepdims=True) + 1e-06)
    normed = (tokens * inverse * gain[...]).astype(bf16)
    width = out_weight.shape[0]
    grad_out = nt(cotangent[...], out_weight[...]).astype(bf16)
    query = nn(normed, weight[0]).astype(bf16)
    qg[:, :width] = query * jnp.asarray(HEAD_DIM ** (-0.5), bf16)
    kv[:, :width] = nn(normed, weight[1]).astype(bf16)
    kv[:, width:] = nn(normed, weight[2]).astype(bf16)
    qg[:, width:] = grad_out
    count = latent.shape[0]
    upper[:KV_ROWS] = kv[:KV_ROWS]
    upper[KV_ROWS:] = qg[:QG_ROWS]
    lower[:KV_ROWS] = kv[count - KV_ROWS :]
    lower[KV_ROWS:] = qg[count - QG_ROWS :]


def edges_kernel(kv, qg, above, below, kv_low, kv_high, qg_low, qg_high, left, right):
    kv_all = jnp.concatenate([above[:KV_ROWS], kv[...], below[:KV_ROWS]], axis=0)
    qg_all = jnp.concatenate([above[KV_ROWS:], qg[...], below[KV_ROWS:]], axis=0)
    left[:KV_EDGE] = nn(kv_low[...], kv_all).astype(bf16)
    left[KV_EDGE:] = nn(qg_low[...], qg_all).astype(bf16)
    right[:KV_EDGE] = nn(kv_high[...], kv_all).astype(bf16)
    right[KV_EDGE:] = nn(qg_high[...], qg_all).astype(bf16)


def window_bias(limits, keys, queries):
    key_y, key_x = keys[:, 0:1], keys[:, 1:2]
    top, bottom = limits[0].astype(f32), limits[1].astype(f32)
    left, right = limits[2].astype(f32), limits[3].astype(f32)
    inside = (key_y >= top) & (key_y <= bottom) & (key_x >= left) & (key_x <= right)
    key_y = jnp.where(inside, key_y, FAR)
    apart = jnp.maximum(jnp.abs(key_y - queries[0:1, :]), jnp.abs(key_x - queries[1:2, :]))
    return jnp.where(apart <= RADIUS, 0.0, -1e30)


def by_head(block):
    width = block.shape[1]
    lanes = lax.broadcasted_iota(jnp.int32, (1, width), 1) // HEAD_DIM
    return [jnp.where(lanes == head, block, jnp.zeros_like(block)) for head in range(width // HEAD_DIM)]


def attention(bias, kv, qg, own):
    width = kv.shape[1] // 2
    count = qg.shape[0]
    key, value = kv[:, :width], kv[:, width:]
    query = jnp.concatenate(by_head(qg[:, :width]), axis=0)
    upstream = jnp.concatenate(by_head(qg[:, width:]), axis=0)
    scores = nt(key, query) + bias
    dots = nt(value, upstream)
    exponent = jnp.exp(scores - jnp.max(scores, axis=0, keepdims=True))
    scale = 1.0 / jnp.sum(exponent, axis=0, keepdims=True)
    weights = exponent * scale
    centre = jnp.sum(weights * dots, axis=0, keepdims=True)
    score_grads = (weights * (dots - centre)).astype(bf16)
    value_grad = nn(weights[own].astype(bf16), upstream)
    key_grad = nn(score_grads[own], query)
    stacked = nn(key.astype(f32).T.astype(bf16), score_grads).T
    parts = [stacked[first : first + count] for first in range(0, stacked.shape[0], count)]
    lanes = lax.broadcasted_iota(jnp.int32, (1, width), 1) // HEAD_DIM
    query_grad = parts[0]
    for head in range(1, len(parts)):
        query_grad = jnp.where(lanes == head, parts[head], query_grad)
    return query_grad * (HEAD_DIM ** (-0.5)), key_grad, value_grad


def middle_kernel(
    limits, kv, qg, above, below, keys, queries, gather, spread, query_out, pair_out
):
    width = kv.shape[1] // 2
    count = kv.shape[0]
    kv_all = jnp.concatenate([above[:KV_ROWS], kv[...], below[:KV_ROWS]], axis=0)
    qg_all = jnp.concatenate([above[KV_ROWS:], qg[...], below[KV_ROWS:]], axis=0)
    qg_mid = nn(gather[...], qg_all).astype(bf16)
    bias = window_bias(limits, keys, queries)
    own = slice(KV_ROWS, KV_ROWS + count)
    query_grad, key_grad, value_grad = attention(bias, kv_all, qg_mid, own)
    query_out[...] = nn(spread[...], query_grad.astype(bf16)).astype(bf16)
    pair_out[:, :width] = key_grad
    pair_out[:, width:] = value_grad


def sides_kernel(
    limits, leftward, from_left, rightward, from_right, query_mid, pair_mid, left_keys,
    left_queries, right_keys, right_queries, key_spread, query_spread, weight, partial
):
    width = query_mid.shape[1]
    own = slice(OWN_FROM, OWN_FROM + OWN_EDGE)
    query_parts, pair_parts = [], []
    for mine, theirs, keys, queries in (
        (leftward, from_left, left_keys, left_queries),
        (rightward, from_right, right_keys, right_queries),
    ):
        kv = jnp.concatenate([mine[:KV_EDGE], theirs[:KV_EDGE]], axis=0)
        qg = jnp.concatenate([mine[KV_EDGE:], theirs[KV_EDGE:]], axis=0)
        bias = window_bias(limits, keys, queries)
        query_grad, key_grad, value_grad = attention(bias, kv, qg, own)
        query_parts.append(query_grad[:QG_EDGE])
        pair_parts.append(jnp.concatenate([key_grad, value_grad], axis=1))
    query_side = jnp.concatenate(query_parts, axis=0).astype(bf16)
    pair_side = jnp.concatenate(pair_parts, axis=0)
    coarse = pair_side.astype(bf16)
    fine = (pair_side - coarse.astype(f32)).astype(bf16)
    pair = pair_mid[...] + (nn(key_spread[...], coarse) + nn(key_spread[...], fine))
    query_grad = query_mid[...].astype(f32) + nn(query_spread[...], query_side)
    pair = pair.astype(bf16)
    total = nt(query_grad.astype(bf16), weight[0])
    total += nt(pair[:, :width], weight[1])
    total += nt(pair[:, width:], weight[2])
    partial[...] = total.astype(bf16)


def finish_kernel(place, received, latent, gain, cotangent, result):
    count = received.shape[1]
    first = pl.multiple_of(place[0] * count, count)
    tokens = latent[pl.ds(first, count), :].astype(f32)
    upstream = cotangent[pl.ds(first, count), :].astype(f32)
    summed = received[0].astype(f32)
    for part in range(1, received.shape[0]):
        summed += received[part].astype(f32)
    inverse = lax.rsqrt(jnp.mean(tokens * tokens, axis=-1, keepdims=True) + 1e-06)
    unit = tokens * inverse
    scaled = summed * gain[...]
    stat = jnp.mean(scaled * unit, axis=-1, keepdims=True)
    result[...] = upstream + inverse * (scaled - unit * stat)


def moved(block, axis, distance):
    count = lax.axis_size(axis)
    route = [(i, i + distance) for i in range(count) if 0 <= i + distance < count]
    return lax.ppermute(block, axis, route)


def per_device(latent, norm_gain, qkv_weight, out_weight, cotangent):
    tile_rows, tile_cols, model_width = latent.shape
    head_cols = out_weight.shape[0]
    count = tile_rows * tile_cols
    tp = lax.axis_size("tp")
    flat_latent = latent.reshape(count, model_width)
    flat_cotangent = cotangent.reshape(count, model_width)
    gain = norm_gain.reshape(1, model_width)
    weight = qkv_weight.transpose(1, 0, 2)
    shape = jax.ShapeDtypeStruct
    edge = shape((KV_ROWS + QG_ROWS, 2 * head_cols), bf16)
    row, col = lax.axis_index("row"), lax.axis_index("col")
    limits = jnp.stack(
        [
            -row * tile_rows,
            (lax.axis_size("row") - row) * tile_rows - 1,
            -col * tile_cols,
            (lax.axis_size("col") - col) * tile_cols - 1,
        ]
    ).astype(jnp.int32)
    kv, qg, upper, lower = pl.pallas_call(
        project_kernel,
        out_shape=[shape((count, 2 * head_cols), bf16)] * 2 + [edge] * 2,
        in_specs=[VMEM] * 5,
        out_specs=[VMEM] * 4,
        compiler_params=PARAMS,
        name="project",
    )(flat_latent, gain, weight, out_weight, flat_cotangent)
    above = moved(lower, "row", 1)
    below = moved(upper, "row", -1)
    side = shape((KV_EDGE + QG_EDGE, 2 * head_cols), bf16)
    leftward, rightward = pl.pallas_call(
        edges_kernel,
        out_shape=[side] * 2,
        in_specs=[VMEM] * 8,
        out_specs=[VMEM] * 2,
        compiler_params=PARAMS,
        name="edges",
    )(kv, qg, above, below, *edge_picks())
    from_left = moved(rightward, "col", 1)
    from_right = moved(leftward, "col", -1)
    heads = head_cols // HEAD_DIM
    query_mid, pair_mid = pl.pallas_call(
        middle_kernel,
        out_shape=[shape((count, head_cols), bf16), shape((count, 2 * head_cols), f32)],
        in_specs=[SMEM] + [VMEM] * 8,
        out_specs=[VMEM] * 2,
        compiler_params=PARAMS,
        name="middle",
    )(limits, kv, qg, above, below, *middle_places(heads), *middle_picks())
    partial = pl.pallas_call(
        sides_kernel,
        out_shape=shape((count, model_width), bf16),
        in_specs=[SMEM] + [VMEM] * 13,
        out_specs=VMEM,
        compiler_params=PARAMS,
        name="sides",
    )(
        limits, leftward, from_left, rightward, from_right, query_mid, pair_mid,
        *side_places(heads), *side_spreads(), weight,
    )
    own = count // tp
    received = lax.all_to_all(partial.reshape(tp, own, model_width), "tp", 0, 0)
    place = lax.axis_index("tp").astype(jnp.int32).reshape(1)
    result = pl.pallas_call(
        finish_kernel,
        out_shape=shape((own, model_width), f32),
        in_specs=[SMEM] + [VMEM] * 4,
        out_specs=VMEM,
        compiler_params=PARAMS,
        name="finish",
    )(place, received, flat_latent, gain, flat_cotangent)
    return result.reshape(own // tile_cols, tile_cols, model_width)


def solution(mesh):
    placed = (P("row", "col", None), P(), P(None, None, "tp"), P("tp", None), P("row", "col", None))
    return jax.shard_map(
        per_device,
        mesh=mesh,
        in_specs=placed,
        out_specs=P(("row", "tp"), "col", None),
        check_vma=False,
    )
```

```python
import functools

import jax
import jax.numpy as jnp
import numpy as np
from jax import lax
from jax.experimental import pallas as pl
from jax.experimental.pallas import tpu as pltpu
from jax.sharding import PartitionSpec as P

HEAD_DIM = 64
RADIUS = 3
REACH = 2 * RADIUS
SIDE = 16
WIDE = SIDE + 2 * REACH
TALL = SIDE + 2 * RADIUS
KV_ROWS = REACH * SIDE
QG_ROWS = RADIUS * SIDE
KV_EDGE = 176
QG_EDGE = 80
MIDDLE = SIDE - 2 * RADIUS
MID_QUERIES = 224
OWN_FROM = 32
OWN_EDGE = 112
FAR = 1000.0
bf16 = jnp.bfloat16
f32 = jnp.float32
VMEM = pl.BlockSpec(memory_space=pltpu.VMEM)
HERE = pl.BlockSpec(memory_space=pltpu.VMEM)
SMEM = pl.BlockSpec(memory_space=pltpu.SMEM)
FAR_SPACE = pl.BlockSpec(memory_space=pltpu.HBM)
PARAMS = pltpu.CompilerParams(vmem_limit_bytes=32 * 1024 * 1024)


def in_hbm(block):
    return pltpu.with_memory_space_constraint(block, pltpu.HBM)


def near_call(kernel, name, outs, specs, *operands):
    fixed = [
        pltpu.with_memory_space_constraint(x, pltpu.VMEM) if spec is VMEM else x
        for x, spec in zip(operands, specs)
    ]
    places = [VMEM if spec is HERE else spec for spec in specs]
    return pl.pallas_call(
        kernel,
        out_shape=outs,
        in_specs=places,
        out_specs=jax.tree.map(lambda _: VMEM, outs),
        compiler_params=PARAMS,
        name=name,
    )(*fixed)


def nt(a, b):
    return lax.dot_general(a, b, (((1,), (1,)), ((), ())), preferred_element_type=f32)


def nn(a, b):
    return jnp.dot(a, b, preferred_element_type=f32)


def table(out_rows, in_rows, pairs):
    filled = np.zeros((out_rows, in_rows), np.float32)
    for target, source in pairs:
        filled[target, source] = 1.0
    return jnp.asarray(filled, bf16)


def strip_pairs(lines, count, first):
    return [
        (line * count + step, line * SIDE + first + step)
        for line in range(lines)
        for step in range(count)
    ]


GATHERS = {
    "kv_edges": (0, 2 * KV_EDGE, WIDE * SIDE),
    "qg_edges": (2 * KV_EDGE, 2 * QG_EDGE, TALL * SIDE),
    "middle": (2 * KV_EDGE + 2 * QG_EDGE, MID_QUERIES, TALL * SIDE),
}
SPREADS = {
    "middle": (0, SIDE * SIDE, MID_QUERIES),
    "keys": (SIDE * SIDE, SIDE * SIDE, 2 * OWN_EDGE),
    "queries": (2 * SIDE * SIDE, SIDE * SIDE, 2 * QG_EDGE),
}


def part_of(ref, spot):
    first, rows, cols = spot
    return ref[first : first + rows, :cols]


def gathers():
    pairs = []
    for part, first in enumerate((0, SIDE - REACH)):
        pairs += [(part * KV_EDGE + t, f) for t, f in strip_pairs(WIDE, REACH, first)]
    begin = GATHERS["qg_edges"][0]
    for part, first in enumerate((0, SIDE - RADIUS)):
        pairs += [(begin + part * QG_EDGE + t, f) for t, f in strip_pairs(TALL, RADIUS, first)]
    begin = GATHERS["middle"][0]
    pairs += [(begin + t, f) for t, f in strip_pairs(TALL, MIDDLE, RADIUS)]
    return table(begin + MID_QUERIES, WIDE * SIDE, pairs)


def spreads():
    pairs = []

    def add(name, halo, column, target):
        token = target - halo * SIDE
        if 0 <= token < SIDE * SIDE:
            pairs.append((SPREADS[name][0] + token, column))

    for t, f in strip_pairs(TALL, MIDDLE, RADIUS):
        add("middle", RADIUS, t, f)
    for part, first in enumerate((0, SIDE - REACH)):
        for t, f in strip_pairs(WIDE, REACH, first):
            add("keys", REACH, part * OWN_EDGE + t - OWN_FROM, f)
    for part, first in enumerate((0, SIDE - RADIUS)):
        for t, f in strip_pairs(TALL, RADIUS, first):
            add("queries", RADIUS, part * QG_EDGE + t, f)
    return table(3 * SIDE * SIDE, SIDE * SIDE, pairs)


def coords(lines, reach, first, count, total, pad):
    ys = [float(line - reach) for line in range(lines) for _ in range(count)]
    xs = [float(first + step) for _ in range(lines) for step in range(count)]
    spare = [pad] * (total - len(ys))
    return np.asarray([ys + spare, xs + spare], np.float32)


def places(heads):
    keys = [coords(WIDE, REACH, 0, SIDE, WIDE * SIDE, FAR)]
    queries = [np.tile(coords(TALL, RADIUS, RADIUS, MIDDLE, MID_QUERIES, -FAR), (1, heads))]
    for key_firsts, query_firsts in (
        ((0, -REACH), (0, -RADIUS)),
        ((SIDE - REACH, SIDE), (SIDE - RADIUS, SIDE)),
    ):
        keys += [coords(WIDE, REACH, f, REACH, KV_EDGE, FAR) for f in key_firsts]
        both = [coords(TALL, RADIUS, f, RADIUS, QG_EDGE, -FAR) for f in query_firsts]
        queries.append(np.tile(np.concatenate(both, axis=1), (1, heads)))
    keys, queries = np.concatenate(keys, axis=1), np.concatenate(queries, axis=1)
    joined = np.full((8, queries.shape[1]), FAR, np.float32)
    joined[:2, : keys.shape[1]] = keys
    joined[2:4] = queries
    return jnp.asarray(joined)


def project_kernel(
    row, col, place, latent_any, gain, weight_any, out_weight_any, cotangent_any, kv, qg, far, near,
    latent, weight, out_weight, cotangent, sems
):
    copies = [
        pltpu.make_async_copy(source, target, sems.at[i])
        for i, (source, target) in enumerate(
            (
                (latent_any, latent),
                (weight_any.at[1], weight.at[1]),
                (weight_any.at[2], weight.at[2]),
                (weight_any.at[0], weight.at[0]),
                (cotangent_any, cotangent),
                (out_weight_any, out_weight),
            )
        )
    ]
    for copy in copies:
        copy.start()
    width = out_weight.shape[0]
    copies[0].wait()
    tokens = latent[...].astype(f32)
    inverse = lax.rsqrt(jnp.mean(tokens * tokens, axis=-1, keepdims=True) + 1e-06)
    normed = (tokens * inverse * gain[...]).astype(bf16)
    copies[1].wait()
    copies[2].wait()
    kv[:, :width] = nn(normed, weight[1]).astype(bf16)
    kv[:, width:] = nn(normed, weight[2]).astype(bf16)
    for copy in copies[3:]:
        copy.wait()
    query = nn(normed, weight[0]).astype(bf16)
    qg[:, :width] = query * jnp.asarray(HEAD_DIM ** (-0.5), bf16)
    qg[:, width:] = nt(cotangent[...], out_weight[...]).astype(bf16)
    count = latent.shape[0]
    odd = lax.rem(row[0], 2)
    for strip, at_end in ((far, odd), (near, 1 - odd)):
        first = pl.multiple_of(at_end * (count - KV_ROWS), SIDE)
        strip[:KV_ROWS] = kv[pl.ds(first, KV_ROWS), :]
        first = pl.multiple_of(at_end * (count - QG_ROWS), SIDE)
        strip[KV_ROWS:] = qg[pl.ds(first, QG_ROWS), :]


def tall_blocks(row, kv, qg, far, near):
    odd = lax.rem(row[0], 2) == 1
    above = jnp.where(odd, near[...], far[...])
    below = jnp.where(odd, far[...], near[...])
    kv_all = jnp.concatenate([above[:KV_ROWS], kv[...], below[:KV_ROWS]], axis=0)
    qg_all = jnp.concatenate([above[KV_ROWS:], qg[...], below[KV_ROWS:]], axis=0)
    return kv_all, qg_all


def edges_kernel(row, kv, qg, far, near, gather, left, right, kv_tall, qg_tall):
    kv_all, qg_all = tall_blocks(row, kv, qg, far, near)
    kv_tall[...] = kv_all
    qg_tall[...] = qg_all
    kv_edges = nn(part_of(gather, GATHERS["kv_edges"]), kv_all).astype(bf16)
    qg_edges = nn(part_of(gather, GATHERS["qg_edges"]), qg_all).astype(bf16)
    left[:KV_EDGE] = kv_edges[:KV_EDGE]
    left[KV_EDGE:] = qg_edges[:QG_EDGE]
    right[:KV_EDGE] = kv_edges[KV_EDGE:]
    right[KV_EDGE:] = qg_edges[QG_EDGE:]


def window_bias(spot, extent, keys, queries):
    key_y, key_x = keys[:, 0:1], keys[:, 1:2]
    top, left = (-(at * SIDE).astype(f32) for at in spot)
    bottom, right = ((((n - at) * SIDE) - 1).astype(f32) for at, n in zip(spot, extent))
    inside = (key_y >= top) & (key_y <= bottom) & (key_x >= left) & (key_x <= right)
    key_y = jnp.where(inside, key_y, FAR)
    apart = jnp.maximum(jnp.abs(key_y - queries[0:1, :]), jnp.abs(key_x - queries[1:2, :]))
    return jnp.where(apart <= RADIUS, 0.0, -1e30)


def by_head(block):
    width = block.shape[1]
    lanes = lax.broadcasted_iota(jnp.int32, (1, width), 1) // HEAD_DIM
    return [jnp.where(lanes == head, block, jnp.zeros_like(block)) for head in range(width // HEAD_DIM)]


def attention(bias, kv, qg, own):
    width = kv.shape[1] // 2
    count = qg.shape[0]
    key, value = kv[:, :width], kv[:, width:]
    query = jnp.concatenate(by_head(qg[:, :width]), axis=0)
    upstream = jnp.concatenate(by_head(qg[:, width:]), axis=0)
    scores = nt(key, query) + bias
    dots = nt(value, upstream)
    exponent = jnp.exp(scores - jnp.max(scores, axis=0, keepdims=True))
    scale = 1.0 / jnp.sum(exponent, axis=0, keepdims=True)
    weights = exponent * scale
    centre = jnp.sum(weights * dots, axis=0, keepdims=True)
    score_grads = (weights * (dots - centre)).astype(bf16)
    value_grad = nn(weights[own].astype(bf16), upstream)
    key_grad = nn(score_grads[own], query)
    stacked = nn(key.astype(f32).T.astype(bf16), score_grads).T
    parts = [stacked[first : first + count] for first in range(0, stacked.shape[0], count)]
    lanes = lax.broadcasted_iota(jnp.int32, (1, width), 1) // HEAD_DIM
    query_grad = parts[0]
    for head in range(1, len(parts)):
        query_grad = jnp.where(lanes == head, parts[head], query_grad)
    return query_grad * (HEAD_DIM ** (-0.5)), key_grad, value_grad


def middle_kernel(
    extent, row, col, kv, qg, points, gather, spread, query_out, pair_out, left_bias, right_bias
):
    count, width = query_out.shape
    spot = (row[0], col[0])
    keys, queries = points[...].T, points[2:4]
    qg_mid = nn(part_of(gather, GATHERS["middle"]), qg[...]).astype(bf16)
    first_key, first_query = kv.shape[0], MID_QUERIES * width // HEAD_DIM
    bias = window_bias(spot, extent, keys[:first_key], queries[:, :first_query])
    own = slice(KV_ROWS, KV_ROWS + count)
    query_grad, key_grad, value_grad = attention(bias, kv[...], qg_mid, own)
    scattered = nn(part_of(spread, SPREADS["middle"]), query_grad.astype(bf16))
    query_out[...] = scattered.astype(bf16)
    pair_out[:, :width] = key_grad
    pair_out[:, width:] = value_grad
    for side in (left_bias, right_bias):
        last_key, last_query = first_key + side.shape[0], first_query + side.shape[1]
        side[...] = window_bias(
            spot, extent, keys[first_key:last_key], queries[:, first_query:last_query]
        )
        first_key, first_query = last_key, last_query


def sides_kernel(
    leftward, from_left, rightward, from_right, query_mid, pair_mid, left_bias, right_bias,
    spread, weight, partial
):
    width = query_mid.shape[1]
    own = slice(OWN_FROM, OWN_FROM + OWN_EDGE)
    query_parts, pair_parts = [], []
    for mine, theirs, bias in (
        (leftward, from_left, left_bias),
        (rightward, from_right, right_bias),
    ):
        kv = jnp.concatenate([mine[:KV_EDGE], theirs[:KV_EDGE]], axis=0)
        qg = jnp.concatenate([mine[KV_EDGE:], theirs[KV_EDGE:]], axis=0)
        query_grad, key_grad, value_grad = attention(bias[...], kv, qg, own)
        query_parts.append(query_grad[:QG_EDGE])
        pair_parts.append(jnp.concatenate([key_grad, value_grad], axis=1))
    query_side = jnp.concatenate(query_parts, axis=0).astype(bf16)
    pair_side = jnp.concatenate(pair_parts, axis=0)
    coarse = pair_side.astype(bf16)
    fine = (pair_side - coarse.astype(f32)).astype(bf16)
    key_spread, query_spread = (part_of(spread, SPREADS[name]) for name in ("keys", "queries"))
    pair = pair_mid[...] + (nn(key_spread, coarse) + nn(key_spread, fine))
    query_grad = query_mid[...].astype(f32) + nn(query_spread, query_side)
    pair = pair.astype(bf16)
    total = nt(query_grad.astype(bf16), weight[0])
    total += nt(pair[:, :width], weight[1])
    total += nt(pair[:, width:], weight[2])
    partial[...] = total.astype(bf16)


def finish_kernel(place, received, latent, gain, cotangent, result):
    count = received.shape[1]
    first = pl.multiple_of(place[0] * count, count)
    tokens = latent[pl.ds(first, count), :].astype(f32)
    upstream = cotangent[pl.ds(first, count), :].astype(f32)
    summed = received[0].astype(f32)
    for part in range(1, received.shape[0]):
        summed += received[part].astype(f32)
    inverse = lax.rsqrt(jnp.mean(tokens * tokens, axis=-1, keepdims=True) + 1e-06)
    unit = tokens * inverse
    scaled = summed * gain[...]
    stat = jnp.mean(scaled * unit, axis=-1, keepdims=True)
    result[...] = upstream + inverse * (scaled - unit * stat)


def paired(block, axis, first):
    count = lax.axis_size(axis)
    route = []
    for low in range(first, count - 1, 2):
        route += [(low, low + 1), (low + 1, low)]
    return lax.ppermute(block, axis, route)


def moved(block, axis, distance):
    count = lax.axis_size(axis)
    route = [(i, i + distance) for i in range(count) if 0 <= i + distance < count]
    return lax.ppermute(block, axis, route)


def per_device(latent, norm_gain, qkv_weight, out_weight, cotangent):
    tile_rows, tile_cols, model_width = latent.shape
    head_cols = out_weight.shape[0]
    count = tile_rows * tile_cols
    tp = lax.axis_size("tp")
    flat_latent = latent.reshape(count, model_width)
    flat_cotangent = cotangent.reshape(count, model_width)
    gain = norm_gain.reshape(1, model_width)
    weight = qkv_weight.transpose(1, 0, 2)
    shape = pltpu.VMEM
    heads = head_cols // HEAD_DIM
    row = lax.axis_index("row").astype(jnp.int32).reshape(1)
    col = lax.axis_index("col").astype(jnp.int32).reshape(1)
    place = lax.axis_index("tp").astype(jnp.int32).reshape(1)
    extent = (lax.axis_size("row"), lax.axis_size("col"))
    edge = shape((KV_ROWS + QG_ROWS, 2 * head_cols), bf16)
    kv, qg, far, near = pl.pallas_call(
        project_kernel,
        out_shape=[shape((count, 2 * head_cols), bf16)] * 2 + [edge] * 2,
        in_specs=[SMEM, SMEM, SMEM, FAR_SPACE, HERE, FAR_SPACE, FAR_SPACE, FAR_SPACE],
        out_specs=[HERE] * 4,
        scratch_shapes=[
            pltpu.VMEM(flat_latent.shape, bf16),
            pltpu.VMEM(weight.shape, bf16),
            pltpu.VMEM(out_weight.shape, bf16),
            pltpu.VMEM(flat_cotangent.shape, bf16),
            pltpu.SemaphoreType.DMA((6,)),
        ],
        compiler_params=PARAMS,
        name="project",
    )(
        row,
        col,
        place,
        in_hbm(flat_latent),
        in_hbm(gain),
        in_hbm(weight),
        in_hbm(out_weight),
        in_hbm(flat_cotangent),
    )
    far = paired(far, "row", 1)
    near = paired(near, "row", 0)
    side = shape((KV_EDGE + QG_EDGE, 2 * head_cols), bf16)
    gather, spread = gathers(), spreads()
    tall = [shape((lines * SIDE, 2 * head_cols), bf16) for lines in (WIDE, TALL)]
    leftward, rightward, kv_tall, qg_tall = near_call(
        edges_kernel,
        "edges",
        [side] * 2 + tall,
        [SMEM] + [VMEM] * 5,
        row, kv, qg, far, near, gather,
    )
    from_left = moved(rightward, "col", 1)
    from_right = moved(leftward, "col", -1)
    bias = shape((2 * KV_EDGE, 2 * QG_EDGE * heads), f32)
    query_mid, pair_mid, left_bias, right_bias = near_call(
        functools.partial(middle_kernel, extent),
        "middle",
        [shape((count, head_cols), bf16), shape((count, 2 * head_cols), f32), bias, bias],
        [SMEM] * 2 + [VMEM] * 5,
        row, col, kv_tall, qg_tall, places(heads), gather, spread,
    )
    partial = near_call(
        sides_kernel,
        "sides",
        shape((count, model_width), bf16),
        [VMEM] * 10,
        leftward, from_left, rightward, from_right, query_mid, pair_mid, left_bias, right_bias,
        spread, weight,
    )
    own = count // tp
    received = lax.all_to_all(partial.reshape(tp, own, model_width), "tp", 0, 0)
    result = near_call(
        finish_kernel,
        "finish",
        jax.ShapeDtypeStruct((own, model_width), f32),
        [SMEM] + [VMEM] * 4,
        place, received, flat_latent, gain, flat_cotangent,
    )
    return result.reshape(own // tile_cols, tile_cols, model_width)


def solution(mesh):
    placed = (P("row", "col", None), P(), P(None, None, "tp"), P("tp", None), P("row", "col", None))
    return jax.shard_map(
        per_device,
        mesh=mesh,
        in_specs=placed,
        out_specs=P(("row", "tp"), "col", None),
        check_vma=False,
    )
```

```python
import functools

import jax
import jax.numpy as jnp
import numpy as np
from jax import lax
from jax.experimental import pallas as pl
from jax.experimental.pallas import tpu as pltpu
from jax.sharding import PartitionSpec as P

HEAD_DIM = 64
RADIUS = 3
REACH = 2 * RADIUS
SIDE = 16
WIDE = SIDE + 2 * REACH
TALL = SIDE + 2 * RADIUS
KV_ROWS = REACH * SIDE
QG_ROWS = RADIUS * SIDE
KV_EDGE = 176
QG_EDGE = 80
MIDDLE = SIDE - 2 * RADIUS
MID_QUERIES = 224
OWN_FROM = 32
OWN_EDGE = 112
FAR = 1000.0
bf16 = jnp.bfloat16
f32 = jnp.float32
VMEM = pl.BlockSpec(memory_space=pltpu.VMEM)
HERE = pl.BlockSpec(memory_space=pltpu.VMEM)
SMEM = pl.BlockSpec(memory_space=pltpu.SMEM)
FAR_SPACE = pl.BlockSpec(memory_space=pltpu.HBM)
PARAMS = pltpu.CompilerParams(vmem_limit_bytes=32 * 1024 * 1024)


def in_hbm(block):
    return pltpu.with_memory_space_constraint(block, pltpu.HBM)


def near_call(kernel, name, outs, specs, *operands, scratch=()):
    fixed = [
        pltpu.with_memory_space_constraint(x, pltpu.VMEM) if spec is VMEM else x
        for x, spec in zip(operands, specs)
    ]
    places = [VMEM if spec is HERE else spec for spec in specs]
    return pl.pallas_call(
        kernel,
        out_shape=outs,
        in_specs=places,
        out_specs=jax.tree.map(lambda _: VMEM, outs),
        scratch_shapes=scratch,
        compiler_params=PARAMS,
        name=name,
    )(*fixed)


def nt(a, b):
    return lax.dot_general(a, b, (((1,), (1,)), ((), ())), preferred_element_type=f32)


def nn(a, b):
    return jnp.dot(a, b, preferred_element_type=f32)


def table(out_rows, in_rows, pairs):
    filled = np.zeros((out_rows, in_rows), np.float32)
    for target, source in pairs:
        filled[target, source] = 1.0
    return jnp.asarray(filled, bf16)


def strip_pairs(lines, count, first):
    return [
        (line * count + step, line * SIDE + first + step)
        for line in range(lines)
        for step in range(count)
    ]


GATHERS = {
    "kv_edges": (0, 2 * KV_EDGE, WIDE * SIDE),
    "qg_edges": (2 * KV_EDGE, 2 * QG_EDGE, TALL * SIDE),
    "middle": (2 * KV_EDGE + 2 * QG_EDGE, MID_QUERIES, TALL * SIDE),
}
HALF = SIDE // 2
HALF_TOKENS = SIDE * HALF
SPREADS = {
    "middle": (0, 2 * HALF_TOKENS, MID_QUERIES),
    "keys": ((2 * HALF_TOKENS, HALF_TOKENS, OWN_EDGE), (3 * HALF_TOKENS, HALF_TOKENS, OWN_EDGE)),
    "queries": ((4 * HALF_TOKENS, HALF_TOKENS, QG_EDGE), (5 * HALF_TOKENS, HALF_TOKENS, QG_EDGE)),
}


def part_of(ref, spot):
    first, rows, cols = spot
    return ref[first : first + rows, :cols]


def gathers():
    pairs = []
    for part, first in enumerate((0, SIDE - REACH)):
        pairs += [(part * KV_EDGE + t, f) for t, f in strip_pairs(WIDE, REACH, first)]
    begin = GATHERS["qg_edges"][0]
    for part, first in enumerate((0, SIDE - RADIUS)):
        pairs += [(begin + part * QG_EDGE + t, f) for t, f in strip_pairs(TALL, RADIUS, first)]
    begin = GATHERS["middle"][0]
    pairs += [(begin + t, f) for t, f in strip_pairs(TALL, MIDDLE, RADIUS)]
    return table(begin + MID_QUERIES, WIDE * SIDE, pairs)


def spreads():
    pairs = []

    def add(first, halo, column, target):
        token = target - halo * SIDE
        if 0 <= token < SIDE * SIDE:
            y, x = divmod(token, SIDE)
            pairs.append((first + x // HALF * HALF_TOKENS + y * HALF + x % HALF, column))

    for t, f in strip_pairs(TALL, MIDDLE, RADIUS):
        add(0, RADIUS, t, f)
    for first in (0, SIDE - REACH):
        for t, f in strip_pairs(WIDE, REACH, first):
            add(SPREADS["keys"][0][0], REACH, t - OWN_FROM, f)
    for first in (0, SIDE - RADIUS):
        for t, f in strip_pairs(TALL, RADIUS, first):
            add(SPREADS["queries"][0][0], RADIUS, t, f)
    return table(6 * HALF_TOKENS, SIDE * SIDE, pairs)


def coords(lines, reach, first, count, total, pad):
    ys = [float(line - reach) for line in range(lines) for _ in range(count)]
    xs = [float(first + step) for _ in range(lines) for step in range(count)]
    spare = [pad] * (total - len(ys))
    return np.asarray([ys + spare, xs + spare], np.float32)


def places(heads):
    keys = [coords(WIDE, REACH, 0, SIDE, WIDE * SIDE, FAR)]
    queries = [np.tile(coords(TALL, RADIUS, RADIUS, MIDDLE, MID_QUERIES, -FAR), (1, heads))]
    for key_firsts, query_firsts in (
        ((0, -REACH), (0, -RADIUS)),
        ((SIDE - REACH, SIDE), (SIDE - RADIUS, SIDE)),
    ):
        keys += [coords(WIDE, REACH, f, REACH, KV_EDGE, FAR) for f in key_firsts]
        both = [coords(TALL, RADIUS, f, RADIUS, QG_EDGE, -FAR) for f in query_firsts]
        queries.append(np.tile(np.concatenate(both, axis=1), (1, heads)))
    keys, queries = np.concatenate(keys, axis=1), np.concatenate(queries, axis=1)
    joined = np.full((8, queries.shape[1]), FAR, np.float32)
    joined[:2, : keys.shape[1]] = keys
    joined[2:4] = queries
    return jnp.asarray(joined)


def project_kernel(
    row, col, place, latent_any, gain, weight_any, out_weight_any, cotangent_any, kv, qg, far, near,
    latent, weight, out_weight, cotangent, sems
):
    copies = [
        pltpu.make_async_copy(source, target, sems.at[i])
        for i, (source, target) in enumerate(
            (
                (latent_any, latent),
                (weight_any.at[1], weight.at[1]),
                (weight_any.at[2], weight.at[2]),
                (weight_any.at[0], weight.at[0]),
                (cotangent_any, cotangent),
                (out_weight_any, out_weight),
            )
        )
    ]
    for copy in copies:
        copy.start()
    width = out_weight.shape[0]
    copies[0].wait()
    tokens = latent[...].astype(f32)
    inverse = lax.rsqrt(jnp.mean(tokens * tokens, axis=-1, keepdims=True) + 1e-06)
    normed = (tokens * inverse * gain[...]).astype(bf16)
    copies[1].wait()
    copies[2].wait()
    kv[:, :width] = nn(normed, weight[1]).astype(bf16)
    kv[:, width:] = nn(normed, weight[2]).astype(bf16)
    for copy in copies[3:]:
        copy.wait()
    query = nn(normed, weight[0]).astype(bf16)
    qg[:, :width] = query * jnp.asarray(HEAD_DIM ** (-0.5), bf16)
    qg[:, width:] = nt(cotangent[...], out_weight[...]).astype(bf16)
    count = latent.shape[0]
    odd = lax.rem(row[0], 2)
    for strip, at_end in ((far, odd), (near, 1 - odd)):
        first = pl.multiple_of(at_end * (count - KV_ROWS), SIDE)
        strip[:KV_ROWS] = kv[pl.ds(first, KV_ROWS), :]
        first = pl.multiple_of(at_end * (count - QG_ROWS), SIDE)
        strip[KV_ROWS:] = qg[pl.ds(first, QG_ROWS), :]


def tall_blocks(row, kv, qg, far, near):
    odd = lax.rem(row[0], 2) == 1
    above = jnp.where(odd, near[...], far[...])
    below = jnp.where(odd, far[...], near[...])
    kv_all = jnp.concatenate([above[:KV_ROWS], kv[...], below[:KV_ROWS]], axis=0)
    qg_all = jnp.concatenate([above[KV_ROWS:], qg[...], below[KV_ROWS:]], axis=0)
    return kv_all, qg_all


def edges_kernel(row, kv, qg, far, near, gather, left, right, kv_tall, qg_tall):
    kv_all, qg_all = tall_blocks(row, kv, qg, far, near)
    kv_tall[...] = kv_all
    qg_tall[...] = qg_all
    kv_edges = nn(part_of(gather, GATHERS["kv_edges"]), kv_all).astype(bf16)
    qg_edges = nn(part_of(gather, GATHERS["qg_edges"]), qg_all).astype(bf16)
    left[:KV_EDGE] = kv_edges[:KV_EDGE]
    left[KV_EDGE:] = qg_edges[:QG_EDGE]
    right[:KV_EDGE] = kv_edges[KV_EDGE:]
    right[KV_EDGE:] = qg_edges[QG_EDGE:]


def window_bias(spot, extent, keys, queries):
    key_y, key_x = keys[:, 0:1], keys[:, 1:2]
    top, left = (-(at * SIDE).astype(f32) for at in spot)
    bottom, right = ((((n - at) * SIDE) - 1).astype(f32) for at, n in zip(spot, extent))
    inside = (key_y >= top) & (key_y <= bottom) & (key_x >= left) & (key_x <= right)
    key_y = jnp.where(inside, key_y, FAR)
    apart = jnp.maximum(jnp.abs(key_y - queries[0:1, :]), jnp.abs(key_x - queries[1:2, :]))
    return jnp.where(apart <= RADIUS, 0.0, -1e30)


def by_head(block):
    width = block.shape[1]
    lanes = lax.broadcasted_iota(jnp.int32, (1, width), 1) // HEAD_DIM
    return [jnp.where(lanes == head, block, jnp.zeros_like(block)) for head in range(width // HEAD_DIM)]


def attention(bias, kv, qg, own):
    width = kv.shape[1] // 2
    count = qg.shape[0]
    key, value = kv[:, :width], kv[:, width:]
    query = jnp.concatenate(by_head(qg[:, :width]), axis=0)
    upstream = jnp.concatenate(by_head(qg[:, width:]), axis=0)
    scores = nt(key, query) + bias
    dots = nt(value, upstream)
    exponent = jnp.exp(scores - jnp.max(scores, axis=0, keepdims=True))
    scale = 1.0 / jnp.sum(exponent, axis=0, keepdims=True)
    weights = exponent * scale
    centre = jnp.sum(weights * dots, axis=0, keepdims=True)
    score_grads = (weights * (dots - centre)).astype(bf16)
    value_grad = nn(weights[own].astype(bf16), upstream)
    key_grad = nn(score_grads[own], query)
    stacked = nn(key.astype(f32).T.astype(bf16), score_grads).T
    parts = [stacked[first : first + count] for first in range(0, stacked.shape[0], count)]
    lanes = lax.broadcasted_iota(jnp.int32, (1, width), 1) // HEAD_DIM
    query_grad = parts[0]
    for head in range(1, len(parts)):
        query_grad = jnp.where(lanes == head, parts[head], query_grad)
    return query_grad * (HEAD_DIM ** (-0.5)), key_grad, value_grad


def middle_kernel(
    extent, row, col, kv, qg, points, gather, spread, left_query, right_query, left_pair,
    right_pair, left_bias, right_bias
):
    count, width = 2 * left_query.shape[0], left_query.shape[1]
    spot = (row[0], col[0])
    keys, queries = points[...].T, points[2:4]
    qg_mid = nn(part_of(gather, GATHERS["middle"]), qg[...]).astype(bf16)
    first_key, first_query = kv.shape[0], MID_QUERIES * width // HEAD_DIM
    bias = window_bias(spot, extent, keys[:first_key], queries[:, :first_query])
    own = slice(KV_ROWS, KV_ROWS + count)
    query_grad, key_grad, value_grad = attention(bias, kv[...], qg_mid, own)
    scattered = nn(part_of(spread, SPREADS["middle"]), query_grad.astype(bf16))
    key_grad = key_grad.reshape(SIDE, 2, HALF, width)
    value_grad = value_grad.reshape(SIDE, 2, HALF, width)
    for half, (query_out, pair_out) in enumerate(
        ((left_query, left_pair), (right_query, right_pair))
    ):
        query_out[...] = scattered[half * HALF_TOKENS : (half + 1) * HALF_TOKENS].astype(bf16)
        pair_out[:, :width] = key_grad[:, half].reshape(HALF_TOKENS, width)
        pair_out[:, width:] = value_grad[:, half].reshape(HALF_TOKENS, width)
    for side in (left_bias, right_bias):
        last_key, last_query = first_key + side.shape[0], first_query + side.shape[1]
        side[...] = window_bias(
            spot, extent, keys[first_key:last_key], queries[:, first_query:last_query]
        )
        first_key, first_query = last_key, last_query


def side_kernel(
    half, place, mine, theirs, query_mid, pair_mid, bias, spread, weight, sent, kept, stacked
):
    width = query_mid.shape[1]
    own = slice(OWN_FROM, OWN_FROM + OWN_EDGE)
    kv = jnp.concatenate([mine[:KV_EDGE], theirs[:KV_EDGE]], axis=0)
    qg = jnp.concatenate([mine[KV_EDGE:], theirs[KV_EDGE:]], axis=0)
    query_grad, key_grad, value_grad = attention(bias[...], kv, qg, own)
    query_side = query_grad[:QG_EDGE].astype(bf16)
    pair_side = jnp.concatenate([key_grad, value_grad], axis=1)
    coarse = pair_side.astype(bf16)
    fine = (pair_side - coarse.astype(f32)).astype(bf16)
    key_spread = part_of(spread, SPREADS["keys"][half])
    query_spread = part_of(spread, SPREADS["queries"][half])
    pair = pair_mid[...] + (nn(key_spread, coarse) + nn(key_spread, fine))
    query_grad = query_mid[...].astype(f32) + nn(query_spread, query_side)
    stacked[:, :width] = query_grad.astype(bf16)
    stacked[:, width:] = pair.astype(bf16)
    block = sent.shape[0] // 2
    ordered = []
    for other in (1, 3, 0, 2):
        first = pl.multiple_of(jnp.bitwise_xor(place[0], other) * block, block)
        ordered.append(stacked[pl.ds(first, block), :])
    ordered = jnp.concatenate(ordered, axis=0)
    total = nt(ordered[:, :width], weight[0])
    total += nt(ordered[:, width : 2 * width], weight[1])
    total += nt(ordered[:, 2 * width :], weight[2])
    sent[...] = total[: 2 * block].astype(bf16)
    kept[...] = total[2 * block :]


def fold_kernel(kept, received, sent, still):
    block = sent.shape[0]
    still[...] = kept[:block] + received[:block].astype(f32)
    sent[...] = (kept[block:] + received[block:].astype(f32)).astype(bf16)


def finish_kernel(
    place, left_kept, left_received, right_kept, right_received, latent, gain, cotangent, result
):
    lines, cols, width = result.shape
    count = lines * cols
    first = pl.multiple_of(place[0] * count, count)
    tokens = latent[pl.ds(first, count), :].astype(f32)
    upstream = cotangent[pl.ds(first, count), :].astype(f32)
    halves = [
        (kept[...] + received[...].astype(f32)).reshape(lines, cols // 2, width)
        for kept, received in ((left_kept, left_received), (right_kept, right_received))
    ]
    summed = jnp.concatenate(halves, axis=1).reshape(count, width)
    inverse = lax.rsqrt(jnp.mean(tokens * tokens, axis=-1, keepdims=True) + 1e-06)
    unit = tokens * inverse
    scaled = summed * gain[...]
    stat = jnp.mean(scaled * unit, axis=-1, keepdims=True)
    outcome = upstream + inverse * (scaled - unit * stat)
    result[...] = outcome.reshape(lines, cols, width)


def paired(block, axis, first):
    count = lax.axis_size(axis)
    route = []
    for low in range(first, count - 1, 2):
        route += [(low, low + 1), (low + 1, low)]
    return lax.ppermute(block, axis, route)


def moved(block, axis, distance):
    count = lax.axis_size(axis)
    route = [(i, i + distance) for i in range(count) if 0 <= i + distance < count]
    return lax.ppermute(block, axis, route)


def per_device(latent, norm_gain, qkv_weight, out_weight, cotangent):
    tile_rows, tile_cols, model_width = latent.shape
    head_cols = out_weight.shape[0]
    count = tile_rows * tile_cols
    tp = lax.axis_size("tp")
    flat_latent = latent.reshape(count, model_width)
    flat_cotangent = cotangent.reshape(count, model_width)
    gain = norm_gain.reshape(1, model_width)
    weight = qkv_weight.transpose(1, 0, 2)
    shape = pltpu.VMEM
    heads = head_cols // HEAD_DIM
    row = lax.axis_index("row").astype(jnp.int32).reshape(1)
    col = lax.axis_index("col").astype(jnp.int32).reshape(1)
    place = lax.axis_index("tp").astype(jnp.int32).reshape(1)
    extent = (lax.axis_size("row"), lax.axis_size("col"))
    edge = shape((KV_ROWS + QG_ROWS, 2 * head_cols), bf16)
    kv, qg, far, near = pl.pallas_call(
        project_kernel,
        out_shape=[shape((count, 2 * head_cols), bf16)] * 2 + [edge] * 2,
        in_specs=[SMEM, SMEM, SMEM, FAR_SPACE, HERE, FAR_SPACE, FAR_SPACE, FAR_SPACE],
        out_specs=[HERE] * 4,
        scratch_shapes=[
            pltpu.VMEM(flat_latent.shape, bf16),
            pltpu.VMEM(weight.shape, bf16),
            pltpu.VMEM(out_weight.shape, bf16),
            pltpu.VMEM(flat_cotangent.shape, bf16),
            pltpu.SemaphoreType.DMA((6,)),
        ],
        compiler_params=PARAMS,
        name="project",
    )(
        row,
        col,
        place,
        in_hbm(flat_latent),
        in_hbm(gain),
        in_hbm(weight),
        in_hbm(out_weight),
        in_hbm(flat_cotangent),
    )
    far = paired(far, "row", 1)
    near = paired(near, "row", 0)
    side = shape((KV_EDGE + QG_EDGE, 2 * head_cols), bf16)
    gather, spread = gathers(), spreads()
    tall = [shape((lines * SIDE, 2 * head_cols), bf16) for lines in (WIDE, TALL)]
    leftward, rightward, kv_tall, qg_tall = near_call(
        edges_kernel,
        "edges",
        [side] * 2 + tall,
        [SMEM] + [VMEM] * 5,
        row, kv, qg, far, near, gather,
    )
    from_left = moved(rightward, "col", 1)
    from_right = moved(leftward, "col", -1)
    bias = shape((2 * KV_EDGE, 2 * QG_EDGE * heads), f32)
    queries, pairs = shape((count // 2, head_cols), bf16), shape((count // 2, 2 * head_cols), f32)
    left_query, right_query, left_pair, right_pair, left_bias, right_bias = near_call(
        functools.partial(middle_kernel, extent),
        "middle",
        [queries, queries, pairs, pairs, bias, bias],
        [SMEM] * 2 + [VMEM] * 5,
        row, col, kv_tall, qg_tall, places(heads), gather, spread,
    )
    own = count // tp
    reduced = []
    for half, operands in enumerate(
        (
            (leftward, from_left, left_query, left_pair, left_bias),
            (rightward, from_right, right_query, right_pair, right_bias),
        )
    ):
        sent, kept = near_call(
            functools.partial(side_kernel, half),
            ("left_side", "right_side")[half],
            [shape((own, model_width), bf16), shape((own, model_width), f32)],
            [SMEM] + [VMEM] * 7,
            place, *operands, spread, weight,
            scratch=[pltpu.VMEM((count // 2, 3 * head_cols), bf16)],
        )
        received = lax.ppermute(sent, "tp", [(i, i ^ 1) for i in range(tp)])
        sent, kept = near_call(
            fold_kernel,
            ("left_fold", "right_fold")[half],
            [shape((own // 2, model_width), bf16), shape((own // 2, model_width), f32)],
            [VMEM] * 2,
            kept, received,
        )
        reduced += [kept, lax.ppermute(sent, "tp", [(i, i ^ 2) for i in range(tp)])]
    return near_call(
        finish_kernel,
        "finish",
        jax.ShapeDtypeStruct((own // tile_cols, tile_cols, model_width), f32),
        [SMEM] + [VMEM] * 7,
        place, *reduced, flat_latent, gain, flat_cotangent,
    )


def solution(mesh):
    placed = (P("row", "col", None), P(), P(None, None, "tp"), P("tp", None), P("row", "col", None))
    return jax.shard_map(
        per_device,
        mesh=mesh,
        in_specs=placed,
        out_specs=P(("row", "tp"), "col", None),
        check_vma=False,
    )
```

```python
import functools

import jax
import jax.numpy as jnp
import numpy as np
from jax import lax
from jax.experimental import pallas as pl
from jax.experimental.pallas import tpu as pltpu
from jax.sharding import PartitionSpec as P

HEAD_DIM = 64
RADIUS = 3
REACH = 2 * RADIUS
SIDE = 16
WIDE = SIDE + 2 * REACH
TALL = SIDE + 2 * RADIUS
KV_ROWS = REACH * SIDE
QG_ROWS = RADIUS * SIDE
KV_EDGE = 176
QG_EDGE = 80
MIDDLE = SIDE - 2 * RADIUS
MID_QUERIES = 224
OWN_FROM = 32
OWN_EDGE = 112
FAR = 1000.0
FOLD_COST = 40_000_000_000
bf16 = jnp.bfloat16
f32 = jnp.float32
VMEM = pl.BlockSpec(memory_space=pltpu.VMEM)
HERE = pl.BlockSpec(memory_space=pltpu.VMEM)
SMEM = pl.BlockSpec(memory_space=pltpu.SMEM)
FAR_SPACE = pl.BlockSpec(memory_space=pltpu.HBM)
PARAMS = pltpu.CompilerParams(vmem_limit_bytes=32 * 1024 * 1024)


def in_hbm(block):
    return pltpu.with_memory_space_constraint(block, pltpu.HBM)


def near_call(kernel, name, outs, specs, *operands, scratch=(), cost=None):
    fixed = [
        pltpu.with_memory_space_constraint(x, pltpu.VMEM) if spec is VMEM else x
        for x, spec in zip(operands, specs)
    ]
    places = [VMEM if spec is HERE else spec for spec in specs]
    return pl.pallas_call(
        kernel,
        out_shape=outs,
        in_specs=places,
        out_specs=jax.tree.map(lambda _: VMEM, outs),
        scratch_shapes=scratch,
        cost_estimate=cost,
        compiler_params=PARAMS,
        name=name,
    )(*fixed)


def nt(a, b):
    return lax.dot_general(a, b, (((1,), (1,)), ((), ())), preferred_element_type=f32)


def nn(a, b):
    return jnp.dot(a, b, preferred_element_type=f32)


def table(out_rows, in_rows, pairs):
    filled = np.zeros((out_rows, in_rows), np.float32)
    for target, source in pairs:
        filled[target, source] = 1.0
    return jnp.asarray(filled, bf16)


def strip_pairs(lines, count, first):
    return [
        (line * count + step, line * SIDE + first + step)
        for line in range(lines)
        for step in range(count)
    ]


GATHERS = {
    "kv_edges": (0, 2 * KV_EDGE, WIDE * SIDE),
    "qg_edges": (2 * KV_EDGE, 2 * QG_EDGE, TALL * SIDE),
    "middle": (2 * KV_EDGE + 2 * QG_EDGE, MID_QUERIES, TALL * SIDE),
}
HALF = SIDE // 2
HALF_TOKENS = SIDE * HALF
SPREADS = {
    "middle": (0, 2 * HALF_TOKENS, MID_QUERIES),
    "keys": ((2 * HALF_TOKENS, HALF_TOKENS, OWN_EDGE), (3 * HALF_TOKENS, HALF_TOKENS, OWN_EDGE)),
    "queries": ((4 * HALF_TOKENS, HALF_TOKENS, QG_EDGE), (5 * HALF_TOKENS, HALF_TOKENS, QG_EDGE)),
}


def part_of(ref, spot):
    first, rows, cols = spot
    return ref[first : first + rows, :cols]


def gathers():
    pairs = []
    for part, first in enumerate((0, SIDE - REACH)):
        pairs += [(part * KV_EDGE + t, f) for t, f in strip_pairs(WIDE, REACH, first)]
    begin = GATHERS["qg_edges"][0]
    for part, first in enumerate((0, SIDE - RADIUS)):
        pairs += [(begin + part * QG_EDGE + t, f) for t, f in strip_pairs(TALL, RADIUS, first)]
    begin = GATHERS["middle"][0]
    pairs += [(begin + t, f) for t, f in strip_pairs(TALL, MIDDLE, RADIUS)]
    return table(begin + MID_QUERIES, WIDE * SIDE, pairs)


def spreads():
    pairs = []

    def add(first, halo, column, target):
        token = target - halo * SIDE
        if 0 <= token < SIDE * SIDE:
            y, x = divmod(token, SIDE)
            pairs.append((first + x // HALF * HALF_TOKENS + y * HALF + x % HALF, column))

    for t, f in strip_pairs(TALL, MIDDLE, RADIUS):
        add(0, RADIUS, t, f)
    for first in (0, SIDE - REACH):
        for t, f in strip_pairs(WIDE, REACH, first):
            add(SPREADS["keys"][0][0], REACH, t - OWN_FROM, f)
    for first in (0, SIDE - RADIUS):
        for t, f in strip_pairs(TALL, RADIUS, first):
            add(SPREADS["queries"][0][0], RADIUS, t, f)
    return table(6 * HALF_TOKENS, SIDE * SIDE, pairs)


def coords(lines, reach, first, count, total, pad):
    ys = [float(line - reach) for line in range(lines) for _ in range(count)]
    xs = [float(first + step) for _ in range(lines) for step in range(count)]
    spare = [pad] * (total - len(ys))
    return np.asarray([ys + spare, xs + spare], np.float32)


def places(heads):
    keys = [coords(WIDE, REACH, 0, SIDE, WIDE * SIDE, FAR)]
    queries = [np.tile(coords(TALL, RADIUS, RADIUS, MIDDLE, MID_QUERIES, -FAR), (1, heads))]
    for key_firsts, query_firsts in (
        ((0, -REACH), (0, -RADIUS)),
        ((SIDE - REACH, SIDE), (SIDE - RADIUS, SIDE)),
    ):
        keys += [coords(WIDE, REACH, f, REACH, KV_EDGE, FAR) for f in key_firsts]
        both = [coords(TALL, RADIUS, f, RADIUS, QG_EDGE, -FAR) for f in query_firsts]
        queries.append(np.tile(np.concatenate(both, axis=1), (1, heads)))
    keys, queries = np.concatenate(keys, axis=1), np.concatenate(queries, axis=1)
    joined = np.full((8, queries.shape[1]), FAR, np.float32)
    joined[:2, : keys.shape[1]] = keys
    joined[2:4] = queries
    return jnp.asarray(joined)


def project_kernel(
    row, col, place, latent_any, gain, weight_any, out_weight_any, cotangent_any, kv, qg, far, near,
    latent, weight, out_weight, cotangent, sems
):
    copies = [
        pltpu.make_async_copy(source, target, sems.at[i])
        for i, (source, target) in enumerate(
            (
                (latent_any, latent),
                (weight_any.at[1], weight.at[1]),
                (weight_any.at[2], weight.at[2]),
                (weight_any.at[0], weight.at[0]),
                (cotangent_any, cotangent),
                (out_weight_any, out_weight),
            )
        )
    ]
    for copy in copies:
        copy.start()
    width = out_weight.shape[0]
    copies[0].wait()
    tokens = latent[...].astype(f32)
    inverse = lax.rsqrt(jnp.mean(tokens * tokens, axis=-1, keepdims=True) + 1e-06)
    normed = (tokens * inverse * gain[...]).astype(bf16)
    copies[1].wait()
    copies[2].wait()
    kv[:, :width] = nn(normed, weight[1]).astype(bf16)
    kv[:, width:] = nn(normed, weight[2]).astype(bf16)
    for copy in copies[3:]:
        copy.wait()
    query = nn(normed, weight[0]).astype(bf16)
    qg[:, :width] = query * jnp.asarray(HEAD_DIM ** (-0.5), bf16)
    qg[:, width:] = nt(cotangent[...], out_weight[...]).astype(bf16)
    count = latent.shape[0]
    odd = lax.rem(row[0], 2)
    for strip, at_end in ((far, odd), (near, 1 - odd)):
        first = pl.multiple_of(at_end * (count - KV_ROWS), SIDE)
        strip[:KV_ROWS] = kv[pl.ds(first, KV_ROWS), :]
        first = pl.multiple_of(at_end * (count - QG_ROWS), SIDE)
        strip[KV_ROWS:] = qg[pl.ds(first, QG_ROWS), :]


def tall_blocks(row, kv, qg, far, near):
    odd = lax.rem(row[0], 2) == 1
    above = jnp.where(odd, near[...], far[...])
    below = jnp.where(odd, far[...], near[...])
    kv_all = jnp.concatenate([above[:KV_ROWS], kv[...], below[:KV_ROWS]], axis=0)
    qg_all = jnp.concatenate([above[KV_ROWS:], qg[...], below[KV_ROWS:]], axis=0)
    return kv_all, qg_all


def edges_kernel(row, kv, qg, far, near, gather, left, right, kv_tall, qg_tall):
    kv_all, qg_all = tall_blocks(row, kv, qg, far, near)
    kv_tall[...] = kv_all
    qg_tall[...] = qg_all
    kv_edges = nn(part_of(gather, GATHERS["kv_edges"]), kv_all).astype(bf16)
    qg_edges = nn(part_of(gather, GATHERS["qg_edges"]), qg_all).astype(bf16)
    left[:KV_EDGE] = kv_edges[:KV_EDGE]
    left[KV_EDGE:] = qg_edges[:QG_EDGE]
    right[:KV_EDGE] = kv_edges[KV_EDGE:]
    right[KV_EDGE:] = qg_edges[QG_EDGE:]


def window_bias(spot, extent, keys, queries):
    key_y, key_x = keys[:, 0:1], keys[:, 1:2]
    top, left = (-(at * SIDE).astype(f32) for at in spot)
    bottom, right = ((((n - at) * SIDE) - 1).astype(f32) for at, n in zip(spot, extent))
    inside = (key_y >= top) & (key_y <= bottom) & (key_x >= left) & (key_x <= right)
    key_y = jnp.where(inside, key_y, FAR)
    apart = jnp.maximum(jnp.abs(key_y - queries[0:1, :]), jnp.abs(key_x - queries[1:2, :]))
    return jnp.where(apart <= RADIUS, 0.0, -1e30)


def by_head(block):
    width = block.shape[1]
    lanes = lax.broadcasted_iota(jnp.int32, (1, width), 1) // HEAD_DIM
    return [jnp.where(lanes == head, block, jnp.zeros_like(block)) for head in range(width // HEAD_DIM)]


def attention(bias, kv, qg, own):
    width = kv.shape[1] // 2
    count = qg.shape[0]
    key, value = kv[:, :width], kv[:, width:]
    query = jnp.concatenate(by_head(qg[:, :width]), axis=0)
    upstream = jnp.concatenate(by_head(qg[:, width:]), axis=0)
    scores = nt(key, query) + bias
    dots = nt(value, upstream)
    exponent = jnp.exp(scores - jnp.max(scores, axis=0, keepdims=True))
    scale = 1.0 / jnp.sum(exponent, axis=0, keepdims=True)
    weights = exponent * scale
    centre = jnp.sum(weights * dots, axis=0, keepdims=True)
    score_grads = (weights * (dots - centre)).astype(bf16)
    value_grad = nn(weights[own].astype(bf16), upstream)
    key_grad = nn(score_grads[own], query)
    stacked = nn(key.astype(f32).T.astype(bf16), score_grads).T
    parts = [stacked[first : first + count] for first in range(0, stacked.shape[0], count)]
    lanes = lax.broadcasted_iota(jnp.int32, (1, width), 1) // HEAD_DIM
    query_grad = parts[0]
    for head in range(1, len(parts)):
        query_grad = jnp.where(lanes == head, parts[head], query_grad)
    return query_grad * (HEAD_DIM ** (-0.5)), key_grad, value_grad


def middle_kernel(
    extent, row, col, kv, qg, points, gather, spread, left_query, right_query, left_pair,
    right_pair, left_bias, right_bias
):
    count, width = 2 * left_query.shape[0], left_query.shape[1]
    spot = (row[0], col[0])
    keys, queries = points[...].T, points[2:4]
    qg_mid = nn(part_of(gather, GATHERS["middle"]), qg[...]).astype(bf16)
    first_key, first_query = kv.shape[0], MID_QUERIES * width // HEAD_DIM
    bias = window_bias(spot, extent, keys[:first_key], queries[:, :first_query])
    own = slice(KV_ROWS, KV_ROWS + count)
    query_grad, key_grad, value_grad = attention(bias, kv[...], qg_mid, own)
    scattered = nn(part_of(spread, SPREADS["middle"]), query_grad.astype(bf16))
    key_grad = key_grad.reshape(SIDE, 2, HALF, width)
    value_grad = value_grad.reshape(SIDE, 2, HALF, width)
    for half, (query_out, pair_out) in enumerate(
        ((left_query, left_pair), (right_query, right_pair))
    ):
        query_out[...] = scattered[half * HALF_TOKENS : (half + 1) * HALF_TOKENS].astype(bf16)
        pair_out[:, :width] = key_grad[:, half].reshape(HALF_TOKENS, width)
        pair_out[:, width:] = value_grad[:, half].reshape(HALF_TOKENS, width)
    for side in (left_bias, right_bias):
        last_key, last_query = first_key + side.shape[0], first_query + side.shape[1]
        side[...] = window_bias(
            spot, extent, keys[first_key:last_key], queries[:, first_query:last_query]
        )
        first_key, first_query = last_key, last_query


def side_grads(half, mine, theirs, query_mid, pair_mid, bias, spread):
    own = slice(OWN_FROM, OWN_FROM + OWN_EDGE)
    kv = jnp.concatenate([mine[:KV_EDGE], theirs[:KV_EDGE]], axis=0)
    qg = jnp.concatenate([mine[KV_EDGE:], theirs[KV_EDGE:]], axis=0)
    query_grad, key_grad, value_grad = attention(bias[...], kv, qg, own)
    query_side = query_grad[:QG_EDGE].astype(bf16)
    pair_side = jnp.concatenate([key_grad, value_grad], axis=1)
    coarse = pair_side.astype(bf16)
    fine = (pair_side - coarse.astype(f32)).astype(bf16)
    key_spread = part_of(spread, SPREADS["keys"][half])
    query_spread = part_of(spread, SPREADS["queries"][half])
    pair = pair_mid[...] + (nn(key_spread, coarse) + nn(key_spread, fine))
    query_grad = query_mid[...].astype(f32) + nn(query_spread, query_side)
    return query_grad.astype(bf16), pair.astype(bf16)


def back_projected(stacked, weight):
    width = weight.shape[2]
    total = nt(stacked[:, :width], weight[0])
    total += nt(stacked[:, width : 2 * width], weight[1])
    total += nt(stacked[:, 2 * width :], weight[2])
    return total


def left_kernel(after, mine, theirs, query_mid, pair_mid, bias, spread, weight, partial):
    grads = side_grads(0, mine, theirs, query_mid, pair_mid, bias, spread)
    partial[...] = back_projected(jnp.concatenate(grads, axis=1), weight).astype(bf16)


def right_kernel(
    place, mine, theirs, query_mid, pair_mid, bias, spread, weight, sent, kept, stacked
):
    width = query_mid.shape[1]
    query_grad, pair = side_grads(1, mine, theirs, query_mid, pair_mid, bias, spread)
    stacked[:, :width] = query_grad
    stacked[:, width:] = pair
    block = sent.shape[0] // 2
    ordered = []
    for other in (1, 3, 0, 2):
        first = pl.multiple_of(jnp.bitwise_xor(place[0], other) * block, block)
        ordered.append(stacked[pl.ds(first, block), :])
    total = back_projected(jnp.concatenate(ordered, axis=0), weight)
    sent[...] = total[: 2 * block].astype(bf16)
    kept[...] = total[2 * block :]


def fold_kernel(kept, received, sent, still):
    block = sent.shape[0]
    still[...] = kept[:block] + received[:block].astype(f32)
    sent[...] = (kept[block:] + received[block:].astype(f32)).astype(bf16)


def finish_kernel(
    place, left_received, right_kept, right_received, latent, gain, cotangent, result
):
    lines, cols, width = result.shape
    count = lines * cols
    first = pl.multiple_of(place[0] * count, count)
    tokens = latent[pl.ds(first, count), :].astype(f32)
    upstream = cotangent[pl.ds(first, count), :].astype(f32)
    left = left_received[0].astype(f32)
    for part in range(1, left_received.shape[0]):
        left += left_received[part].astype(f32)
    right = right_kept[...] + right_received[...].astype(f32)
    halves = [half.reshape(lines, cols // 2, width) for half in (left, right)]
    summed = jnp.concatenate(halves, axis=1).reshape(count, width)
    inverse = lax.rsqrt(jnp.mean(tokens * tokens, axis=-1, keepdims=True) + 1e-06)
    unit = tokens * inverse
    scaled = summed * gain[...]
    stat = jnp.mean(scaled * unit, axis=-1, keepdims=True)
    outcome = upstream + inverse * (scaled - unit * stat)
    result[...] = outcome.reshape(lines, cols, width)


def paired(block, axis, first):
    count = lax.axis_size(axis)
    route = []
    for low in range(first, count - 1, 2):
        route += [(low, low + 1), (low + 1, low)]
    return lax.ppermute(block, axis, route)


def moved(block, axis, distance):
    count = lax.axis_size(axis)
    route = [(i, i + distance) for i in range(count) if 0 <= i + distance < count]
    return lax.ppermute(block, axis, route)


def per_device(latent, norm_gain, qkv_weight, out_weight, cotangent):
    tile_rows, tile_cols, model_width = latent.shape
    head_cols = out_weight.shape[0]
    count = tile_rows * tile_cols
    tp = lax.axis_size("tp")
    flat_latent = latent.reshape(count, model_width)
    flat_cotangent = cotangent.reshape(count, model_width)
    gain = norm_gain.reshape(1, model_width)
    weight = qkv_weight.transpose(1, 0, 2)
    shape = pltpu.VMEM
    heads = head_cols // HEAD_DIM
    row = lax.axis_index("row").astype(jnp.int32).reshape(1)
    col = lax.axis_index("col").astype(jnp.int32).reshape(1)
    place = lax.axis_index("tp").astype(jnp.int32).reshape(1)
    extent = (lax.axis_size("row"), lax.axis_size("col"))
    edge = shape((KV_ROWS + QG_ROWS, 2 * head_cols), bf16)
    kv, qg, far, near = pl.pallas_call(
        project_kernel,
        out_shape=[shape((count, 2 * head_cols), bf16)] * 2 + [edge] * 2,
        in_specs=[SMEM, SMEM, SMEM, FAR_SPACE, HERE, FAR_SPACE, FAR_SPACE, FAR_SPACE],
        out_specs=[HERE] * 4,
        scratch_shapes=[
            pltpu.VMEM(flat_latent.shape, bf16),
            pltpu.VMEM(weight.shape, bf16),
            pltpu.VMEM(out_weight.shape, bf16),
            pltpu.VMEM(flat_cotangent.shape, bf16),
            pltpu.SemaphoreType.DMA((6,)),
        ],
        compiler_params=PARAMS,
        name="project",
    )(
        row,
        col,
        place,
        in_hbm(flat_latent),
        in_hbm(gain),
        in_hbm(weight),
        in_hbm(out_weight),
        in_hbm(flat_cotangent),
    )
    far = paired(far, "row", 1)
    near = paired(near, "row", 0)
    side = shape((KV_EDGE + QG_EDGE, 2 * head_cols), bf16)
    gather, spread = gathers(), spreads()
    tall = [shape((lines * SIDE, 2 * head_cols), bf16) for lines in (WIDE, TALL)]
    leftward, rightward, kv_tall, qg_tall = near_call(
        edges_kernel,
        "edges",
        [side] * 2 + tall,
        [SMEM] + [VMEM] * 5,
        row, kv, qg, far, near, gather,
    )
    from_left = moved(rightward, "col", 1)
    from_right = moved(leftward, "col", -1)
    bias = shape((2 * KV_EDGE, 2 * QG_EDGE * heads), f32)
    queries, pairs = shape((count // 2, head_cols), bf16), shape((count // 2, 2 * head_cols), f32)
    left_query, right_query, left_pair, right_pair, left_bias, right_bias = near_call(
        functools.partial(middle_kernel, extent),
        "middle",
        [queries, queries, pairs, pairs, bias, bias],
        [SMEM] * 2 + [VMEM] * 5,
        row, col, kv_tall, qg_tall, places(heads), gather, spread,
    )
    own = count // tp
    sent, kept = near_call(
        right_kernel,
        "right_side",
        [shape((own, model_width), bf16), shape((own, model_width), f32)],
        [SMEM] + [VMEM] * 7,
        place, rightward, from_right, right_query, right_pair, right_bias, spread, weight,
        scratch=[pltpu.VMEM((count // 2, 3 * head_cols), bf16)],
    )
    received = lax.ppermute(sent, "tp", [(i, i ^ 1) for i in range(tp)])
    partial = near_call(
        left_kernel,
        "left_side",
        shape((count // 2, model_width), bf16),
        [VMEM] * 8,
        kept, leftward, from_left, left_query, left_pair, left_bias, spread, weight,
    )
    sent, right_kept = near_call(
        fold_kernel,
        "right_fold",
        [shape((own // 2, model_width), bf16), shape((own // 2, model_width), f32)],
        [VMEM] * 2,
        kept, received,
        cost=pl.CostEstimate(flops=FOLD_COST, transcendentals=0, bytes_accessed=1 << 18),
    )
    right_received = lax.ppermute(sent, "tp", [(i, i ^ 2) for i in range(tp)])
    left_received = lax.all_to_all(partial.reshape(tp, own // 2, model_width), "tp", 0, 0)
    return near_call(
        finish_kernel,
        "finish",
        jax.ShapeDtypeStruct((own // tile_cols, tile_cols, model_width), f32),
        [SMEM] + [VMEM] * 6,
        place, left_received, right_kept, right_received, flat_latent, gain, flat_cotangent,
    )


def solution(mesh):
    placed = (P("row", "col", None), P(), P(None, None, "tp"), P("tp", None), P("row", "col", None))
    return jax.shard_map(
        per_device,
        mesh=mesh,
        in_specs=placed,
        out_specs=P(("row", "tp"), "col", None),
        check_vma=False,
    )
```

```python
import functools

import jax
import jax.numpy as jnp
import numpy as np
from jax import lax
from jax.experimental import pallas as pl
from jax.experimental.pallas import tpu as pltpu
from jax.sharding import PartitionSpec as P

HEAD_DIM = 64
RADIUS = 3
REACH = 2 * RADIUS
SIDE = 16
WIDE = SIDE + 2 * REACH
TALL = SIDE + 2 * RADIUS
KV_ROWS = REACH * SIDE
QG_ROWS = RADIUS * SIDE
KV_EDGE = 176
QG_EDGE = 80
INNER = range(RADIUS, SIDE - RADIUS)
ALONG = range(SIDE)
TOP = range(-RADIUS, RADIUS)
BOTTOM = range(SIDE - RADIUS, SIDE + RADIUS)
TOP_KEYS = range(-REACH, REACH)
BOTTOM_KEYS = range(SIDE - REACH, SIDE + REACH)
CORE_QUERIES = 128
RIM_QUERIES = 64
RIM_KEYS = 2 * REACH * SIDE
OWN_FROM = 32
OWN_EDGE = 112
FAR = 1000.0
bf16 = jnp.bfloat16
f32 = jnp.float32
VMEM = pl.BlockSpec(memory_space=pltpu.VMEM)
HERE = pl.BlockSpec(memory_space=pltpu.VMEM)
SMEM = pl.BlockSpec(memory_space=pltpu.SMEM)
FAR_SPACE = pl.BlockSpec(memory_space=pltpu.HBM)
PARAMS = pltpu.CompilerParams(vmem_limit_bytes=32 * 1024 * 1024)


def in_hbm(block):
    return pltpu.with_memory_space_constraint(block, pltpu.HBM)


def near_call(kernel, name, outs, specs, *operands, scratch=()):
    fixed = [
        pltpu.with_memory_space_constraint(x, pltpu.VMEM) if spec is VMEM else x
        for x, spec in zip(operands, specs)
    ]
    places = [VMEM if spec is HERE else spec for spec in specs]
    return pl.pallas_call(
        kernel,
        out_shape=outs,
        in_specs=places,
        out_specs=jax.tree.map(lambda _: VMEM, outs),
        scratch_shapes=scratch,
        compiler_params=PARAMS,
        name=name,
    )(*fixed)


def nt(a, b):
    return lax.dot_general(a, b, (((1,), (1,)), ((), ())), preferred_element_type=f32)


def nn(a, b):
    return jnp.dot(a, b, preferred_element_type=f32)


def table(out_rows, in_rows, pairs):
    filled = np.zeros((out_rows, in_rows), np.float32)
    for target, source in pairs:
        filled[target, source] = 1.0
    return jnp.asarray(filled, bf16)


def strip_pairs(lines, count, first):
    return [
        (line * count + step, line * SIDE + first + step)
        for line in range(lines)
        for step in range(count)
    ]


def cells(rows, cols):
    return [(y, x) for y in rows for x in cols]


GATHERS = {
    "kv_edges": (0, 2 * KV_EDGE, WIDE * SIDE),
    "qg_edges": (2 * KV_EDGE, 2 * QG_EDGE, TALL * SIDE),
    "core": (2 * KV_EDGE + 2 * QG_EDGE, CORE_QUERIES, SIDE * SIDE),
    "rim": (2 * KV_EDGE + 2 * QG_EDGE + CORE_QUERIES, 2 * RIM_QUERIES, TALL * SIDE),
}
HALF = SIDE // 2
HALF_TOKENS = SIDE * HALF
SPREADS = {
    "core": (0, 2 * HALF_TOKENS, CORE_QUERIES),
    "rim": (0, 2 * HALF_TOKENS, 2 * RIM_QUERIES, CORE_QUERIES),
    "keys": ((2 * HALF_TOKENS, HALF_TOKENS, OWN_EDGE), (3 * HALF_TOKENS, HALF_TOKENS, OWN_EDGE)),
    "queries": ((4 * HALF_TOKENS, HALF_TOKENS, QG_EDGE), (5 * HALF_TOKENS, HALF_TOKENS, QG_EDGE)),
}


def part_of(ref, spot):
    first, rows, cols, begin = (*spot, 0)[:4]
    return ref[first : first + rows, begin : begin + cols]


def gathers():
    pairs = []
    for part, first in enumerate((0, SIDE - REACH)):
        pairs += [(part * KV_EDGE + t, f) for t, f in strip_pairs(WIDE, REACH, first)]
    begin = GATHERS["qg_edges"][0]
    for part, first in enumerate((0, SIDE - RADIUS)):
        pairs += [(begin + part * QG_EDGE + t, f) for t, f in strip_pairs(TALL, RADIUS, first)]
    begin = GATHERS["core"][0]
    pairs += [(begin + t, y * SIDE + x) for t, (y, x) in enumerate(cells(INNER, INNER))]
    begin = GATHERS["rim"][0]
    for part, rows in enumerate((TOP, BOTTOM)):
        for t, (y, x) in enumerate(cells(rows, INNER)):
            pairs.append((begin + part * RIM_QUERIES + t, (y + RADIUS) * SIDE + x))
    return table(begin + 2 * RIM_QUERIES, WIDE * SIDE, pairs)


def spreads():
    pairs = []

    def add(first, halo, column, target):
        token = target - halo * SIDE
        if 0 <= token < SIDE * SIDE:
            y, x = divmod(token, SIDE)
            pairs.append((first + x // HALF * HALF_TOKENS + y * HALF + x % HALF, column))

    for t, (y, x) in enumerate(cells(INNER, INNER)):
        add(0, 0, t, y * SIDE + x)
    for part, rows in enumerate((TOP, BOTTOM)):
        for t, (y, x) in enumerate(cells(rows, INNER)):
            add(0, 0, CORE_QUERIES + part * RIM_QUERIES + t, y * SIDE + x)
    for first in (0, SIDE - REACH):
        for t, f in strip_pairs(WIDE, REACH, first):
            add(SPREADS["keys"][0][0], REACH, t - OWN_FROM, f)
    for first in (0, SIDE - RADIUS):
        for t, f in strip_pairs(TALL, RADIUS, first):
            add(SPREADS["queries"][0][0], RADIUS, t, f)
    return table(6 * HALF_TOKENS, SIDE * SIDE, pairs)


def coords(rows, cols, total, pad):
    spots = cells(rows, cols)
    spots += [(pad, pad)] * (total - len(spots))
    return np.asarray(spots, np.float32).T


def places(heads):
    keys = [coords(ALONG, ALONG, SIDE * SIDE, FAR)]
    queries = [np.tile(coords(INNER, INNER, CORE_QUERIES, -FAR), (1, heads))]
    for rows, key_rows in ((TOP, TOP_KEYS), (BOTTOM, BOTTOM_KEYS)):
        keys.append(coords(key_rows, ALONG, RIM_KEYS, FAR))
        queries.append(np.tile(coords(rows, INNER, RIM_QUERIES, -FAR), (1, heads)))
    wide, tall = range(-REACH, SIDE + REACH), range(-RADIUS, SIDE + RADIUS)
    for key_firsts, query_firsts in (
        ((0, -REACH), (0, -RADIUS)),
        ((SIDE - REACH, SIDE), (SIDE - RADIUS, SIDE)),
    ):
        keys += [coords(wide, range(f, f + REACH), KV_EDGE, FAR) for f in key_firsts]
        both = [coords(tall, range(f, f + RADIUS), QG_EDGE, -FAR) for f in query_firsts]
        queries.append(np.tile(np.concatenate(both, axis=1), (1, heads)))
    keys, queries = np.concatenate(keys, axis=1), np.concatenate(queries, axis=1)
    joined = np.full((8, queries.shape[1]), FAR, np.float32)
    joined[:2, : keys.shape[1]] = keys
    joined[2:4] = queries
    return jnp.asarray(joined)


def project_kernel(
    row, col, place, latent_any, gain, weight_any, out_weight_any, cotangent_any, kv, qg, far, near,
    latent, weight, out_weight, cotangent, sems
):
    copies = [
        pltpu.make_async_copy(source, target, sems.at[i])
        for i, (source, target) in enumerate(
            (
                (latent_any, latent),
                (weight_any.at[1], weight.at[1]),
                (weight_any.at[2], weight.at[2]),
                (weight_any.at[0], weight.at[0]),
                (cotangent_any, cotangent),
                (out_weight_any, out_weight),
            )
        )
    ]
    for copy in copies:
        copy.start()
    width = out_weight.shape[0]
    copies[0].wait()
    tokens = latent[...].astype(f32)
    inverse = lax.rsqrt(jnp.mean(tokens * tokens, axis=-1, keepdims=True) + 1e-06)
    normed = (tokens * inverse * gain[...]).astype(bf16)
    copies[1].wait()
    copies[2].wait()
    kv[:, :width] = nn(normed, weight[1]).astype(bf16)
    kv[:, width:] = nn(normed, weight[2]).astype(bf16)
    for copy in copies[3:]:
        copy.wait()
    query = nn(normed, weight[0]).astype(bf16)
    qg[:, :width] = query * jnp.asarray(HEAD_DIM ** (-0.5), bf16)
    qg[:, width:] = nt(cotangent[...], out_weight[...]).astype(bf16)
    count = latent.shape[0]
    odd = lax.rem(row[0], 2)
    for strip, at_end in ((far, odd), (near, 1 - odd)):
        first = pl.multiple_of(at_end * (count - KV_ROWS), SIDE)
        strip[:KV_ROWS] = kv[pl.ds(first, KV_ROWS), :]
        first = pl.multiple_of(at_end * (count - QG_ROWS), SIDE)
        strip[KV_ROWS:] = qg[pl.ds(first, QG_ROWS), :]


def tall_blocks(row, kv, qg, far, near):
    odd = lax.rem(row[0], 2) == 1
    above = jnp.where(odd, near[...], far[...])
    below = jnp.where(odd, far[...], near[...])
    kv_all = jnp.concatenate([above[:KV_ROWS], kv[...], below[:KV_ROWS]], axis=0)
    qg_all = jnp.concatenate([above[KV_ROWS:], qg[...], below[KV_ROWS:]], axis=0)
    return kv_all, qg_all


def edges_kernel(row, kv, qg, far, near, gather, after, left, right, kv_tall, qg_tall):
    kv_all, qg_all = tall_blocks(row, kv, qg, far, near)
    kv_tall[...] = kv_all
    qg_tall[...] = qg_all
    kv_edges = nn(part_of(gather, GATHERS["kv_edges"]), kv_all).astype(bf16)
    qg_edges = nn(part_of(gather, GATHERS["qg_edges"]), qg_all).astype(bf16)
    left[:KV_EDGE] = kv_edges[:KV_EDGE]
    left[KV_EDGE:] = qg_edges[:QG_EDGE]
    right[:KV_EDGE] = kv_edges[KV_EDGE:]
    right[KV_EDGE:] = qg_edges[QG_EDGE:]


def window_bias(spot, extent, keys, queries):
    key_y, key_x = keys[:, 0:1], keys[:, 1:2]
    top, left = (-(at * SIDE).astype(f32) for at in spot)
    bottom, right = ((((n - at) * SIDE) - 1).astype(f32) for at, n in zip(spot, extent))
    inside = (key_y >= top) & (key_y <= bottom) & (key_x >= left) & (key_x <= right)
    key_y = jnp.where(inside, key_y, FAR)
    apart = jnp.maximum(jnp.abs(key_y - queries[0:1, :]), jnp.abs(key_x - queries[1:2, :]))
    return jnp.where(apart <= RADIUS, 0.0, -1e30)


def by_head(block):
    width = block.shape[1]
    lanes = lax.broadcasted_iota(jnp.int32, (1, width), 1) // HEAD_DIM
    return [jnp.where(lanes == head, block, jnp.zeros_like(block)) for head in range(width // HEAD_DIM)]


def attention(bias, kv, qg, own):
    width = kv.shape[1] // 2
    count = qg.shape[0]
    key, value = kv[:, :width], kv[:, width:]
    query = jnp.concatenate(by_head(qg[:, :width]), axis=0)
    upstream = jnp.concatenate(by_head(qg[:, width:]), axis=0)
    scores = nt(key, query) + bias
    dots = nt(value, upstream)
    exponent = jnp.exp(scores - jnp.max(scores, axis=0, keepdims=True))
    scale = 1.0 / jnp.sum(exponent, axis=0, keepdims=True)
    weights = exponent * scale
    centre = jnp.sum(weights * dots, axis=0, keepdims=True)
    score_grads = (weights * (dots - centre)).astype(bf16)
    value_grad = nn(weights[own].astype(bf16), upstream)
    key_grad = nn(score_grads[own], query)
    stacked = nn(key.astype(f32).T.astype(bf16), score_grads).T
    parts = [stacked[first : first + count] for first in range(0, stacked.shape[0], count)]
    lanes = lax.broadcasted_iota(jnp.int32, (1, width), 1) // HEAD_DIM
    query_grad = parts[0]
    for head in range(1, len(parts)):
        query_grad = jnp.where(lanes == head, parts[head], query_grad)
    return query_grad * (HEAD_DIM ** (-0.5)), key_grad, value_grad


def core_kernel(
    extent, row, col, kv, qg, points, gather, spread, query_out, pair_out, *biases
):
    count = kv.shape[0]
    width = kv.shape[1] // 2
    spot = (row[0], col[0])
    keys, queries = points[...].T, points[2:4]

    def mask(first_key, key_count, first_query, query_count):
        at_keys = keys[first_key : first_key + key_count]
        at_queries = queries[:, first_query : first_query + query_count]
        return window_bias(spot, extent, at_keys, at_queries)

    lanes = CORE_QUERIES * width // HEAD_DIM
    bias = mask(0, count, 0, lanes)
    inner = nn(part_of(gather, GATHERS["core"]), qg[...]).astype(bf16)
    query_grad, key_grad, value_grad = attention(bias, kv[...], inner, slice(0, count))
    query_out[...] = nn(part_of(spread, SPREADS["core"]), query_grad.astype(bf16)).astype(bf16)
    pair_out[:, :width] = key_grad
    pair_out[:, width:] = value_grad
    first_key, first_query = count, lanes
    for side in biases:
        side[...] = mask(first_key, side.shape[0], first_query, side.shape[1])
        first_key, first_query = first_key + side.shape[0], first_query + side.shape[1]


def middle_kernel(
    kv, qg, top_bias, bottom_bias, gather, spread, core_query, core_pair, left_query,
    right_query, left_pair, right_pair
):
    width = left_query.shape[1]
    rim = nn(part_of(gather, GATHERS["rim"]), qg[...]).astype(bf16)
    near_rows = REACH * SIDE
    last = kv.shape[0] - RIM_KEYS
    top = attention(
        top_bias[...], kv[:RIM_KEYS], rim[:RIM_QUERIES], slice(near_rows, 2 * near_rows)
    )
    bottom = attention(bottom_bias[...], kv[last:], rim[RIM_QUERIES:], slice(0, near_rows))
    query_grad = jnp.concatenate([top[0], bottom[0]], axis=0).astype(bf16)
    scattered = nn(part_of(spread, SPREADS["rim"]), query_grad)
    scattered = (scattered + core_query[...].astype(f32)).astype(bf16)
    between = jnp.zeros((SIDE * SIDE - 2 * near_rows, width), f32)
    for which, first in ((1, 0), (2, width)):
        grad = jnp.concatenate([top[which], between, bottom[which]], axis=0)
        grad += core_pair[:, first : first + width]
        grad = grad.reshape(SIDE, 2, HALF, width)
        for half, pair_out in enumerate((left_pair, right_pair)):
            pair_out[:, first : first + width] = grad[:, half].reshape(HALF_TOKENS, width)
    left_query[...] = scattered[:HALF_TOKENS]
    right_query[...] = scattered[HALF_TOKENS:]


def side_kernel(
    half, place, mine, theirs, query_mid, pair_mid, bias, spread, weight, sent, kept, stacked
):
    width = query_mid.shape[1]
    own = slice(OWN_FROM, OWN_FROM + OWN_EDGE)
    kv = jnp.concatenate([mine[:KV_EDGE], theirs[:KV_EDGE]], axis=0)
    qg = jnp.concatenate([mine[KV_EDGE:], theirs[KV_EDGE:]], axis=0)
    query_grad, key_grad, value_grad = attention(bias[...], kv, qg, own)
    query_side = query_grad[:QG_EDGE].astype(bf16)
    pair_side = jnp.concatenate([key_grad, value_grad], axis=1)
    coarse = pair_side.astype(bf16)
    fine = (pair_side - coarse.astype(f32)).astype(bf16)
    key_spread = part_of(spread, SPREADS["keys"][half])
    query_spread = part_of(spread, SPREADS["queries"][half])
    pair = pair_mid[...] + (nn(key_spread, coarse) + nn(key_spread, fine))
    query_grad = query_mid[...].astype(f32) + nn(query_spread, query_side)
    stacked[:, :width] = query_grad.astype(bf16)
    stacked[:, width:] = pair.astype(bf16)
    block = sent.shape[0] // 2
    ordered = []
    for other in (1, 3, 0, 2):
        first = pl.multiple_of(jnp.bitwise_xor(place[0], other) * block, block)
        ordered.append(stacked[pl.ds(first, block), :])
    ordered = jnp.concatenate(ordered, axis=0)
    total = nt(ordered[:, :width], weight[0])
    total += nt(ordered[:, width : 2 * width], weight[1])
    total += nt(ordered[:, 2 * width :], weight[2])
    sent[...] = total[: 2 * block].astype(bf16)
    kept[...] = total[2 * block :]


def fold_kernel(kept, received, sent, still):
    block = sent.shape[0]
    still[...] = kept[:block] + received[:block].astype(f32)
    sent[...] = (kept[block:] + received[block:].astype(f32)).astype(bf16)


def finish_kernel(
    place, left_kept, left_received, right_kept, right_received, latent, gain, cotangent, result
):
    lines, cols, width = result.shape
    count = lines * cols
    first = pl.multiple_of(place[0] * count, count)
    tokens = latent[pl.ds(first, count), :].astype(f32)
    upstream = cotangent[pl.ds(first, count), :].astype(f32)
    halves = [
        (kept[...] + received[...].astype(f32)).reshape(lines, cols // 2, width)
        for kept, received in ((left_kept, left_received), (right_kept, right_received))
    ]
    summed = jnp.concatenate(halves, axis=1).reshape(count, width)
    inverse = lax.rsqrt(jnp.mean(tokens * tokens, axis=-1, keepdims=True) + 1e-06)
    unit = tokens * inverse
    scaled = summed * gain[...]
    stat = jnp.mean(scaled * unit, axis=-1, keepdims=True)
    outcome = upstream + inverse * (scaled - unit * stat)
    result[...] = outcome.reshape(lines, cols, width)


def paired(block, axis, first):
    count = lax.axis_size(axis)
    route = []
    for low in range(first, count - 1, 2):
        route += [(low, low + 1), (low + 1, low)]
    return lax.ppermute(block, axis, route)


def moved(block, axis, distance):
    count = lax.axis_size(axis)
    route = [(i, i + distance) for i in range(count) if 0 <= i + distance < count]
    return lax.ppermute(block, axis, route)


def per_device(latent, norm_gain, qkv_weight, out_weight, cotangent):
    tile_rows, tile_cols, model_width = latent.shape
    head_cols = out_weight.shape[0]
    count = tile_rows * tile_cols
    tp = lax.axis_size("tp")
    flat_latent = latent.reshape(count, model_width)
    flat_cotangent = cotangent.reshape(count, model_width)
    gain = norm_gain.reshape(1, model_width)
    weight = qkv_weight.transpose(1, 0, 2)
    shape = pltpu.VMEM
    heads = head_cols // HEAD_DIM
    row = lax.axis_index("row").astype(jnp.int32).reshape(1)
    col = lax.axis_index("col").astype(jnp.int32).reshape(1)
    place = lax.axis_index("tp").astype(jnp.int32).reshape(1)
    extent = (lax.axis_size("row"), lax.axis_size("col"))
    edge = shape((KV_ROWS + QG_ROWS, 2 * head_cols), bf16)
    kv, qg, far, near = pl.pallas_call(
        project_kernel,
        out_shape=[shape((count, 2 * head_cols), bf16)] * 2 + [edge] * 2,
        in_specs=[SMEM, SMEM, SMEM, FAR_SPACE, HERE, FAR_SPACE, FAR_SPACE, FAR_SPACE],
        out_specs=[HERE] * 4,
        scratch_shapes=[
            pltpu.VMEM(flat_latent.shape, bf16),
            pltpu.VMEM(weight.shape, bf16),
            pltpu.VMEM(out_weight.shape, bf16),
            pltpu.VMEM(flat_cotangent.shape, bf16),
            pltpu.SemaphoreType.DMA((6,)),
        ],
        compiler_params=PARAMS,
        name="project",
    )(
        row,
        col,
        place,
        in_hbm(flat_latent),
        in_hbm(gain),
        in_hbm(weight),
        in_hbm(out_weight),
        in_hbm(flat_cotangent),
    )
    far = paired(far, "row", 1)
    near = paired(near, "row", 0)
    bias = shape((2 * KV_EDGE, 2 * QG_EDGE * heads), f32)
    rim = shape((RIM_KEYS, RIM_QUERIES * heads), f32)
    gather, spread = gathers(), spreads()
    core_query, core_pair, top_bias, bottom_bias, left_bias, right_bias = near_call(
        functools.partial(core_kernel, extent),
        "core",
        [shape((count, head_cols), bf16), shape((count, 2 * head_cols), f32), rim, rim, bias, bias],
        [SMEM] * 2 + [VMEM] * 5,
        row, col, kv, qg, places(heads), gather, spread,
    )
    side = shape((KV_EDGE + QG_EDGE, 2 * head_cols), bf16)
    tall = [shape((lines * SIDE, 2 * head_cols), bf16) for lines in (WIDE, TALL)]
    leftward, rightward, kv_tall, qg_tall = near_call(
        edges_kernel,
        "edges",
        [side] * 2 + tall,
        [SMEM] + [VMEM] * 6,
        row, kv, qg, far, near, gather, core_query,
    )
    from_left = moved(rightward, "col", 1)
    from_right = moved(leftward, "col", -1)
    queries, pairs = shape((count // 2, head_cols), bf16), shape((count // 2, 2 * head_cols), f32)
    left_query, right_query, left_pair, right_pair = near_call(
        middle_kernel,
        "middle",
        [queries, queries, pairs, pairs],
        [VMEM] * 8,
        kv_tall, qg_tall, top_bias, bottom_bias, gather, spread, core_query, core_pair,
    )
    own = count // tp
    reduced = []
    for half, operands in enumerate(
        (
            (leftward, from_left, left_query, left_pair, left_bias),
            (rightward, from_right, right_query, right_pair, right_bias),
        )
    ):
        sent, kept = near_call(
            functools.partial(side_kernel, half),
            ("left_side", "right_side")[half],
            [shape((own, model_width), bf16), shape((own, model_width), f32)],
            [SMEM] + [VMEM] * 7,
            place, *operands, spread, weight,
            scratch=[pltpu.VMEM((count // 2, 3 * head_cols), bf16)],
        )
        received = lax.ppermute(sent, "tp", [(i, i ^ 1) for i in range(tp)])
        sent, kept = near_call(
            fold_kernel,
            ("left_fold", "right_fold")[half],
            [shape((own // 2, model_width), bf16), shape((own // 2, model_width), f32)],
            [VMEM] * 2,
            kept, received,
        )
        reduced += [kept, lax.ppermute(sent, "tp", [(i, i ^ 2) for i in range(tp)])]
    return near_call(
        finish_kernel,
        "finish",
        jax.ShapeDtypeStruct((own // tile_cols, tile_cols, model_width), f32),
        [SMEM] + [VMEM] * 7,
        place, *reduced, flat_latent, gain, flat_cotangent,
    )


def solution(mesh):
    placed = (P("row", "col", None), P(), P(None, None, "tp"), P("tp", None), P("row", "col", None))
    return jax.shard_map(
        per_device,
        mesh=mesh,
        in_specs=placed,
        out_specs=P(("row", "tp"), "col", None),
        check_vma=False,
    )
```

```python
import functools

import jax
import jax.numpy as jnp
import numpy as np
from jax import lax
from jax.experimental import pallas as pl
from jax.experimental.pallas import tpu as pltpu
from jax.sharding import PartitionSpec as P

HEAD_DIM = 64
RADIUS = 3
REACH = 2 * RADIUS
SIDE = 16
WIDE = SIDE + 2 * REACH
TALL = SIDE + 2 * RADIUS
KV_ROWS = REACH * SIDE
QG_ROWS = RADIUS * SIDE
KV_EDGE = 176
QG_EDGE = 80
INNER = range(RADIUS, SIDE - RADIUS)
ALONG = range(SIDE)
TOP = range(-RADIUS, RADIUS)
BOTTOM = range(SIDE - RADIUS, SIDE + RADIUS)
TOP_KEYS = range(-REACH, REACH)
BOTTOM_KEYS = range(SIDE - REACH, SIDE + REACH)
CORE_QUERIES = 128
RIM_QUERIES = 64
RIM_KEYS = 2 * REACH * SIDE
OWN_FROM = 32
OWN_EDGE = 112
FAR = 1000.0
LANES = 128
bf16 = jnp.bfloat16
f32 = jnp.float32
VMEM = pl.BlockSpec(memory_space=pltpu.VMEM)
HERE = pl.BlockSpec(memory_space=pltpu.VMEM)
SMEM = pl.BlockSpec(memory_space=pltpu.SMEM)
FAR_SPACE = pl.BlockSpec(memory_space=pltpu.HBM)
PARAMS = pltpu.CompilerParams(vmem_limit_bytes=32 * 1024 * 1024)


def in_hbm(block):
    return pltpu.with_memory_space_constraint(block, pltpu.HBM)


def near_call(kernel, name, outs, specs, *operands, scratch=()):
    fixed = [
        pltpu.with_memory_space_constraint(x, pltpu.VMEM) if spec is VMEM else x
        for x, spec in zip(operands, specs)
    ]
    places = [VMEM if spec is HERE else spec for spec in specs]
    return pl.pallas_call(
        kernel,
        out_shape=outs,
        in_specs=places,
        out_specs=jax.tree.map(lambda _: VMEM, outs),
        scratch_shapes=scratch,
        compiler_params=PARAMS,
        name=name,
    )(*fixed)


def nt(a, b):
    return lax.dot_general(a, b, (((1,), (1,)), ((), ())), preferred_element_type=f32)


def nn(a, b):
    return jnp.dot(a, b, preferred_element_type=f32)


def table(out_rows, in_rows, pairs):
    filled = np.zeros((out_rows, in_rows), np.float32)
    for target, source in pairs:
        filled[target, source] = 1.0
    return jnp.asarray(filled, bf16)


def strip_pairs(lines, count, first):
    return [
        (line * count + step, line * SIDE + first + step)
        for line in range(lines)
        for step in range(count)
    ]


def cells(rows, cols):
    return [(y, x) for y in rows for x in cols]


GATHERS = {
    "kv_edges": (0, 2 * KV_EDGE, WIDE * SIDE),
    "qg_edges": (2 * KV_EDGE, 2 * QG_EDGE, TALL * SIDE),
    "core": (2 * KV_EDGE + 2 * QG_EDGE, CORE_QUERIES, SIDE * SIDE),
    "rim": (2 * KV_EDGE + 2 * QG_EDGE + CORE_QUERIES, 2 * RIM_QUERIES, TALL * SIDE),
}
SPREADS = {
    "core": (0, SIDE * SIDE, CORE_QUERIES),
    "rim": (0, SIDE * SIDE, 2 * RIM_QUERIES, CORE_QUERIES),
    "keys": (SIDE * SIDE, SIDE * SIDE, 2 * OWN_EDGE),
    "queries": (2 * SIDE * SIDE, SIDE * SIDE, 2 * QG_EDGE),
}


def part_of(ref, spot):
    first, rows, cols, begin = (*spot, 0)[:4]
    return ref[first : first + rows, begin : begin + cols]


def gathers():
    pairs = []
    for part, first in enumerate((0, SIDE - REACH)):
        pairs += [(part * KV_EDGE + t, f) for t, f in strip_pairs(WIDE, REACH, first)]
    begin = GATHERS["qg_edges"][0]
    for part, first in enumerate((0, SIDE - RADIUS)):
        pairs += [(begin + part * QG_EDGE + t, f) for t, f in strip_pairs(TALL, RADIUS, first)]
    begin = GATHERS["core"][0]
    pairs += [(begin + t, y * SIDE + x) for t, (y, x) in enumerate(cells(INNER, INNER))]
    begin = GATHERS["rim"][0]
    for part, rows in enumerate((TOP, BOTTOM)):
        for t, (y, x) in enumerate(cells(rows, INNER)):
            pairs.append((begin + part * RIM_QUERIES + t, (y + RADIUS) * SIDE + x))
    return table(begin + 2 * RIM_QUERIES, WIDE * SIDE, pairs)


def spreads():
    pairs = []

    def add(name, column, token):
        if 0 <= token < SIDE * SIDE:
            pairs.append((SPREADS[name][0] + token, column))

    for t, (y, x) in enumerate(cells(INNER, INNER)):
        add("core", t, y * SIDE + x)
    for part, rows in enumerate((TOP, BOTTOM)):
        for t, (y, x) in enumerate(cells(rows, INNER)):
            add("rim", CORE_QUERIES + part * RIM_QUERIES + t, y * SIDE + x)
    for part, first in enumerate((0, SIDE - REACH)):
        for t, f in strip_pairs(WIDE, REACH, first):
            add("keys", part * OWN_EDGE + t - OWN_FROM, f - KV_ROWS)
    for part, first in enumerate((0, SIDE - RADIUS)):
        for t, f in strip_pairs(TALL, RADIUS, first):
            add("queries", part * QG_EDGE + t, f - QG_ROWS)
    return table(3 * SIDE * SIDE, SIDE * SIDE, pairs)


def coords(rows, cols, total, pad):
    spots = cells(rows, cols)
    spots += [(pad, pad)] * (total - len(spots))
    return np.asarray(spots, np.float32).T


def places(heads):
    keys = [coords(ALONG, ALONG, SIDE * SIDE, FAR)]
    queries = [np.tile(coords(INNER, INNER, CORE_QUERIES, -FAR), (1, heads))]
    for rows, key_rows in ((TOP, TOP_KEYS), (BOTTOM, BOTTOM_KEYS)):
        keys.append(coords(key_rows, ALONG, RIM_KEYS, FAR))
        queries.append(np.tile(coords(rows, INNER, RIM_QUERIES, -FAR), (1, heads)))
    wide, tall = range(-REACH, SIDE + REACH), range(-RADIUS, SIDE + RADIUS)
    for key_firsts, query_firsts in (
        ((0, -REACH), (0, -RADIUS)),
        ((SIDE - REACH, SIDE), (SIDE - RADIUS, SIDE)),
    ):
        keys += [coords(wide, range(f, f + REACH), KV_EDGE, FAR) for f in key_firsts]
        both = [coords(tall, range(f, f + RADIUS), QG_EDGE, -FAR) for f in query_firsts]
        queries += [np.tile(part, (1, heads)) for part in both]
    keys, queries = np.concatenate(keys, axis=1), np.concatenate(queries, axis=1)
    joined = np.full((8, queries.shape[1]), FAR, np.float32)
    joined[:2, : keys.shape[1]] = keys
    joined[2:4] = queries
    return jnp.asarray(joined)


def project_kernel(
    row, col, place, latent_any, gain, weight_any, out_weight_any, cotangent_any, kv, qg, far, near,
    latent, weight, out_weight, cotangent, sems
):
    copies = [
        pltpu.make_async_copy(source, target, sems.at[i])
        for i, (source, target) in enumerate(
            (
                (latent_any, latent),
                (weight_any.at[1], weight.at[1]),
                (weight_any.at[2], weight.at[2]),
                (weight_any.at[0], weight.at[0]),
                (cotangent_any, cotangent),
                (out_weight_any, out_weight),
            )
        )
    ]
    for copy in copies:
        copy.start()
    width = out_weight.shape[0]
    copies[0].wait()
    tokens = latent[...].astype(f32)
    inverse = lax.rsqrt(jnp.mean(tokens * tokens, axis=-1, keepdims=True) + 1e-06)
    normed = (tokens * inverse * gain[...]).astype(bf16)
    copies[1].wait()
    copies[2].wait()
    kv[:, :width] = nn(normed, weight[1]).astype(bf16)
    kv[:, width:] = nn(normed, weight[2]).astype(bf16)
    for copy in copies[3:]:
        copy.wait()
    query = nn(normed, weight[0]).astype(bf16)
    qg[:, :width] = query * jnp.asarray(HEAD_DIM ** (-0.5), bf16)
    qg[:, width:] = nt(cotangent[...], out_weight[...]).astype(bf16)
    count = latent.shape[0]
    odd = lax.rem(row[0], 2)
    for strip, at_end in ((far, odd), (near, 1 - odd)):
        first = pl.multiple_of(at_end * (count - KV_ROWS), SIDE)
        strip[:KV_ROWS] = kv[pl.ds(first, KV_ROWS), :]
        first = pl.multiple_of(at_end * (count - QG_ROWS), SIDE)
        strip[KV_ROWS:] = qg[pl.ds(first, QG_ROWS), :]


def tall_blocks(row, kv, qg, far, near):
    odd = lax.rem(row[0], 2) == 1
    above = jnp.where(odd, near[...], far[...])
    below = jnp.where(odd, far[...], near[...])
    kv_all = jnp.concatenate([above[:KV_ROWS], kv[...], below[:KV_ROWS]], axis=0)
    qg_all = jnp.concatenate([above[KV_ROWS:], qg[...], below[KV_ROWS:]], axis=0)
    return kv_all, qg_all


def edges_kernel(row, kv, qg, far, near, gather, after, left, right, kv_tall, qg_tall):
    kv_all, qg_all = tall_blocks(row, kv, qg, far, near)
    kv_tall[...] = kv_all
    qg_tall[...] = qg_all
    kv_edges = nn(part_of(gather, GATHERS["kv_edges"]), kv_all).astype(bf16)
    qg_edges = nn(part_of(gather, GATHERS["qg_edges"]), qg_all).astype(bf16)
    left[:KV_EDGE] = kv_edges[:KV_EDGE]
    left[KV_EDGE:] = qg_edges[:QG_EDGE]
    right[:KV_EDGE] = kv_edges[KV_EDGE:]
    right[KV_EDGE:] = qg_edges[QG_EDGE:]


def window_bias(spot, extent, keys, queries):
    key_y, key_x = keys[:, 0:1], keys[:, 1:2]
    top, left = (-(at * SIDE).astype(f32) for at in spot)
    bottom, right = ((((n - at) * SIDE) - 1).astype(f32) for at, n in zip(spot, extent))
    inside = (key_y >= top) & (key_y <= bottom) & (key_x >= left) & (key_x <= right)
    key_y = jnp.where(inside, key_y, FAR)
    apart = jnp.maximum(jnp.abs(key_y - queries[0:1, :]), jnp.abs(key_x - queries[1:2, :]))
    return jnp.where(apart <= RADIUS, 0.0, -1e30)


def by_head(block):
    width = block.shape[1]
    lanes = lax.broadcasted_iota(jnp.int32, (1, width), 1) // HEAD_DIM
    return [jnp.where(lanes == head, block, jnp.zeros_like(block)) for head in range(width // HEAD_DIM)]


def attention(bias, kv, groups, own):
    width = kv.shape[1] // 2
    key, value = kv[:, :width], kv[:, width:]
    query = jnp.concatenate([part for qg in groups for part in by_head(qg[:, :width])], axis=0)
    upstream = jnp.concatenate([part for qg in groups for part in by_head(qg[:, width:])], axis=0)
    scores = nt(key, query) + bias
    dots = nt(value, upstream)
    exponent = jnp.exp(scores - jnp.max(scores, axis=0, keepdims=True))
    scale = 1.0 / jnp.sum(exponent, axis=0, keepdims=True)
    weights = exponent * scale
    centre = jnp.sum(weights * dots, axis=0, keepdims=True)
    score_grads = (weights * (dots - centre)).astype(bf16)
    value_grad = nn(weights[own].astype(bf16), upstream)
    key_grad = nn(score_grads[own], query)
    count = groups[0].shape[0]
    heads = width // HEAD_DIM
    used = -(-count * heads // LANES) * LANES
    stacked = nn(key.astype(f32).T.astype(bf16), score_grads[:, :used]).T
    lanes = lax.broadcasted_iota(jnp.int32, (1, width), 1) // HEAD_DIM
    query_grad = stacked[:count]
    for head in range(1, heads):
        part = stacked[head * count : (head + 1) * count]
        query_grad = jnp.where(lanes == head, part, query_grad)
    return query_grad * (HEAD_DIM ** (-0.5)), key_grad, value_grad


def core_kernel(
    extent, row, col, kv, qg, points, gather, spread, query_out, pair_out, *biases
):
    count = kv.shape[0]
    width = kv.shape[1] // 2
    spot = (row[0], col[0])
    keys, queries = points[...].T, points[2:4]

    def mask(first_key, key_count, first_query, query_count):
        at_keys = keys[first_key : first_key + key_count]
        at_queries = queries[:, first_query : first_query + query_count]
        return window_bias(spot, extent, at_keys, at_queries)

    lanes = CORE_QUERIES * width // HEAD_DIM
    bias = mask(0, count, 0, lanes)
    inner = nn(part_of(gather, GATHERS["core"]), qg[...]).astype(bf16)
    query_grad, key_grad, value_grad = attention(bias, kv[...], [inner], slice(0, count))
    query_out[...] = nn(part_of(spread, SPREADS["core"]), query_grad.astype(bf16)).astype(bf16)
    pair_out[:, :width] = key_grad
    pair_out[:, width:] = value_grad
    first_key, first_query = count, lanes
    for side in biases:
        side[...] = mask(first_key, side.shape[0], first_query, side.shape[1])
        first_key, first_query = first_key + side.shape[0], first_query + side.shape[1]


def middle_kernel(
    kv, qg, top_bias, bottom_bias, gather, spread, core_query, core_pair, query_out, pair_out
):
    width = query_out.shape[1]
    rim = nn(part_of(gather, GATHERS["rim"]), qg[...]).astype(bf16)
    near_rows = REACH * SIDE
    last = kv.shape[0] - RIM_KEYS
    top = attention(
        top_bias[...], kv[:RIM_KEYS], [rim[:RIM_QUERIES]], slice(near_rows, 2 * near_rows)
    )
    bottom = attention(bottom_bias[...], kv[last:], [rim[RIM_QUERIES:]], slice(0, near_rows))
    query_grad = jnp.concatenate([top[0], bottom[0]], axis=0).astype(bf16)
    scattered = nn(part_of(spread, SPREADS["rim"]), query_grad)
    query_out[...] = (scattered + core_query[...].astype(f32)).astype(bf16)
    between = jnp.zeros((SIDE * SIDE - 2 * near_rows, width), f32)
    for which, first in ((1, 0), (2, width)):
        grad = jnp.concatenate([top[which], between, bottom[which]], axis=0)
        pair_out[:, first : first + width] = grad + core_pair[:, first : first + width]


def back_projected(place, others, stacked, weight):
    width = weight.shape[2]
    block = stacked.shape[0] // 4
    parts = []
    for other in others:
        first = pl.multiple_of(jnp.bitwise_xor(place[0], other) * block, block)
        parts.append(stacked[pl.ds(first, block), :])
    rows = jnp.concatenate(parts, axis=0)
    total = nt(rows[:, :width], weight[0])
    total += nt(rows[:, width : 2 * width], weight[1])
    return total + nt(rows[:, 2 * width :], weight[2])


def sides_kernel(
    place, leftward, from_left, rightward, from_right, query_mid, pair_mid, left_bias, right_bias,
    spread, weight, sent, stacked
):
    width = query_mid.shape[1]
    own = slice(OWN_FROM, OWN_FROM + OWN_EDGE)
    query_parts, pair_parts = [], []
    for mine, theirs, bias in (
        (leftward, from_left, left_bias),
        (rightward, from_right, right_bias),
    ):
        kv = jnp.concatenate([mine[:KV_EDGE], theirs[:KV_EDGE]], axis=0)
        groups = [mine[KV_EDGE:], theirs[KV_EDGE:]]
        query_grad, key_grad, value_grad = attention(bias[...], kv, groups, own)
        query_parts.append(query_grad)
        pair_parts.append(jnp.concatenate([key_grad, value_grad], axis=1))
    query_side = jnp.concatenate(query_parts, axis=0).astype(bf16)
    pair_side = jnp.concatenate(pair_parts, axis=0)
    coarse = pair_side.astype(bf16)
    fine = (pair_side - coarse.astype(f32)).astype(bf16)
    key_spread, query_spread = (part_of(spread, SPREADS[name]) for name in ("keys", "queries"))
    pair = pair_mid[...] + (nn(key_spread, coarse) + nn(key_spread, fine))
    query_grad = query_mid[...].astype(f32) + nn(query_spread, query_side)
    stacked[:, :width] = query_grad.astype(bf16)
    stacked[:, width:] = pair.astype(bf16)
    sent[...] = back_projected(place, (1, 3), stacked, weight).astype(bf16)


def keep_kernel(place, stacked, weight, kept):
    kept[...] = back_projected(place, (0, 2), stacked, weight)


def fold_kernel(kept, received, sent, still):
    block = sent.shape[0]
    still[...] = kept[:block] + received[:block].astype(f32)
    sent[...] = (kept[block:] + received[block:].astype(f32)).astype(bf16)


def finish_kernel(place, kept, received, latent, gain, cotangent, result):
    count = kept.shape[0]
    first = pl.multiple_of(place[0] * count, count)
    tokens = latent[pl.ds(first, count), :].astype(f32)
    upstream = cotangent[pl.ds(first, count), :].astype(f32)
    summed = kept[...] + received[...].astype(f32)
    inverse = lax.rsqrt(jnp.mean(tokens * tokens, axis=-1, keepdims=True) + 1e-06)
    unit = tokens * inverse
    scaled = summed * gain[...]
    stat = jnp.mean(scaled * unit, axis=-1, keepdims=True)
    result[...] = upstream + inverse * (scaled - unit * stat)


def paired(block, axis, first):
    count = lax.axis_size(axis)
    route = []
    for low in range(first, count - 1, 2):
        route += [(low, low + 1), (low + 1, low)]
    return lax.ppermute(block, axis, route)


def moved(block, axis, distance):
    count = lax.axis_size(axis)
    route = [(i, i + distance) for i in range(count) if 0 <= i + distance < count]
    return lax.ppermute(block, axis, route)


def per_device(latent, norm_gain, qkv_weight, out_weight, cotangent):
    tile_rows, tile_cols, model_width = latent.shape
    head_cols = out_weight.shape[0]
    count = tile_rows * tile_cols
    tp = lax.axis_size("tp")
    flat_latent = latent.reshape(count, model_width)
    flat_cotangent = cotangent.reshape(count, model_width)
    gain = norm_gain.reshape(1, model_width)
    weight = qkv_weight.transpose(1, 0, 2)
    shape = pltpu.VMEM
    heads = head_cols // HEAD_DIM
    row = lax.axis_index("row").astype(jnp.int32).reshape(1)
    col = lax.axis_index("col").astype(jnp.int32).reshape(1)
    place = lax.axis_index("tp").astype(jnp.int32).reshape(1)
    extent = (lax.axis_size("row"), lax.axis_size("col"))
    edge = shape((KV_ROWS + QG_ROWS, 2 * head_cols), bf16)
    kv, qg, far, near = pl.pallas_call(
        project_kernel,
        out_shape=[shape((count, 2 * head_cols), bf16)] * 2 + [edge] * 2,
        in_specs=[SMEM, SMEM, SMEM, FAR_SPACE, HERE, FAR_SPACE, FAR_SPACE, FAR_SPACE],
        out_specs=[HERE] * 4,
        scratch_shapes=[
            pltpu.VMEM(flat_latent.shape, bf16),
            pltpu.VMEM(weight.shape, bf16),
            pltpu.VMEM(out_weight.shape, bf16),
            pltpu.VMEM(flat_cotangent.shape, bf16),
            pltpu.SemaphoreType.DMA((6,)),
        ],
        compiler_params=PARAMS,
        name="project",
    )(
        row,
        col,
        place,
        in_hbm(flat_latent),
        in_hbm(gain),
        in_hbm(weight),
        in_hbm(out_weight),
        in_hbm(flat_cotangent),
    )
    far = paired(far, "row", 1)
    near = paired(near, "row", 0)
    bias = shape((2 * KV_EDGE, 2 * QG_EDGE * heads), f32)
    rim = shape((RIM_KEYS, RIM_QUERIES * heads), f32)
    gather, spread = gathers(), spreads()
    core_query, core_pair, top_bias, bottom_bias, left_bias, right_bias = near_call(
        functools.partial(core_kernel, extent),
        "core",
        [shape((count, head_cols), bf16), shape((count, 2 * head_cols), f32), rim, rim, bias, bias],
        [SMEM] * 2 + [VMEM] * 5,
        row, col, kv, qg, places(heads), gather, spread,
    )
    side = shape((KV_EDGE + QG_EDGE, 2 * head_cols), bf16)
    tall = [shape((lines * SIDE, 2 * head_cols), bf16) for lines in (WIDE, TALL)]
    leftward, rightward, kv_tall, qg_tall = near_call(
        edges_kernel,
        "edges",
        [side] * 2 + tall,
        [SMEM] + [VMEM] * 6,
        row, kv, qg, far, near, gather, core_query,
    )
    from_left = moved(rightward, "col", 1)
    from_right = moved(leftward, "col", -1)
    query_mid, pair_mid = near_call(
        middle_kernel,
        "middle",
        [shape((count, head_cols), bf16), shape((count, 2 * head_cols), f32)],
        [VMEM] * 8,
        kv_tall, qg_tall, top_bias, bottom_bias, gather, spread, core_query, core_pair,
    )
    own = count // tp
    sent, stacked = near_call(
        sides_kernel,
        "sides",
        [shape((2 * own, model_width), bf16), shape((count, 3 * head_cols), bf16)],
        [SMEM] + [VMEM] * 10,
        place, leftward, from_left, rightward, from_right, query_mid, pair_mid, left_bias,
        right_bias, spread, weight,
    )
    received = lax.ppermute(sent, "tp", [(i, i ^ 1) for i in range(tp)])
    kept = near_call(
        keep_kernel,
        "keep",
        shape((2 * own, model_width), f32),
        [SMEM] + [VMEM] * 2,
        place, stacked, weight,
    )
    sent, kept = near_call(
        fold_kernel,
        "fold",
        [shape((own, model_width), bf16), shape((own, model_width), f32)],
        [VMEM] * 2,
        kept, received,
    )
    received = lax.ppermute(sent, "tp", [(i, i ^ 2) for i in range(tp)])
    result = near_call(
        finish_kernel,
        "finish",
        jax.ShapeDtypeStruct((own, model_width), f32),
        [SMEM] + [VMEM] * 5,
        place, kept, received, flat_latent, gain, flat_cotangent,
    )
    return result.reshape(own // tile_cols, tile_cols, model_width)


def solution(mesh):
    placed = (P("row", "col", None), P(), P(None, None, "tp"), P("tp", None), P("row", "col", None))
    return jax.shard_map(
        per_device,
        mesh=mesh,
        in_specs=placed,
        out_specs=P(("row", "tp"), "col", None),
        check_vma=False,
    )
```

```python
import functools

import jax
import jax.numpy as jnp
import numpy as np
from jax import lax
from jax.experimental import pallas as pl
from jax.experimental.pallas import tpu as pltpu
from jax.sharding import PartitionSpec as P

HEAD_DIM = 64
RADIUS = 3
REACH = 2 * RADIUS
SIDE = 16
WIDE = SIDE + 2 * REACH
TALL = SIDE + 2 * RADIUS
KV_ROWS = REACH * SIDE
QG_ROWS = RADIUS * SIDE
KV_EDGE = 176
QG_EDGE = 80
INNER = range(RADIUS, SIDE - RADIUS)
ALONG = range(SIDE)
TOP = range(-RADIUS, RADIUS)
BOTTOM = range(SIDE - RADIUS, SIDE + RADIUS)
TOP_KEYS = range(-REACH, REACH)
BOTTOM_KEYS = range(SIDE - REACH, SIDE + REACH)
CORE_QUERIES = 128
RIM_QUERIES = 64
RIM_KEYS = 2 * REACH * SIDE
OWN_FROM = 32
OWN_EDGE = 112
FAR = 1000.0
LANES = 128
bf16 = jnp.bfloat16
f32 = jnp.float32
VMEM = pl.BlockSpec(memory_space=pltpu.VMEM)
HERE = pl.BlockSpec(memory_space=pltpu.VMEM)
SMEM = pl.BlockSpec(memory_space=pltpu.SMEM)
FAR_SPACE = pl.BlockSpec(memory_space=pltpu.HBM)
PARAMS = pltpu.CompilerParams(vmem_limit_bytes=32 * 1024 * 1024)


def in_hbm(block):
    return pltpu.with_memory_space_constraint(block, pltpu.HBM)


def near_call(kernel, name, outs, specs, *operands, scratch=()):
    fixed = [
        pltpu.with_memory_space_constraint(x, pltpu.VMEM) if spec is VMEM else x
        for x, spec in zip(operands, specs)
    ]
    places = [VMEM if spec is HERE else spec for spec in specs]
    return pl.pallas_call(
        kernel,
        out_shape=outs,
        in_specs=places,
        out_specs=jax.tree.map(lambda _: VMEM, outs),
        scratch_shapes=scratch,
        compiler_params=PARAMS,
        name=name,
    )(*fixed)


def nt(a, b):
    return lax.dot_general(a, b, (((1,), (1,)), ((), ())), preferred_element_type=f32)


def nn(a, b):
    return jnp.dot(a, b, preferred_element_type=f32)


def table(out_rows, in_rows, pairs):
    filled = np.zeros((out_rows, in_rows), np.float32)
    for target, source in pairs:
        filled[target, source] = 1.0
    return jnp.asarray(filled, bf16)


def strip_pairs(lines, count, first):
    return [
        (line * count + step, line * SIDE + first + step)
        for line in range(lines)
        for step in range(count)
    ]


def cells(rows, cols):
    return [(y, x) for y in rows for x in cols]


GATHERS = {
    "kv_edges": (0, 2 * KV_EDGE, WIDE * SIDE),
    "qg_edges": (2 * KV_EDGE, 2 * QG_EDGE, TALL * SIDE),
    "core": (2 * KV_EDGE + 2 * QG_EDGE, CORE_QUERIES, SIDE * SIDE),
    "rim": (2 * KV_EDGE + 2 * QG_EDGE + CORE_QUERIES, 2 * RIM_QUERIES, TALL * SIDE),
}
SPREADS = {
    "core": (0, SIDE * SIDE, CORE_QUERIES),
    "rim": (0, SIDE * SIDE, 2 * RIM_QUERIES, CORE_QUERIES),
    "keys": (SIDE * SIDE, SIDE * SIDE, 2 * OWN_EDGE),
    "queries": (2 * SIDE * SIDE, SIDE * SIDE, 2 * QG_EDGE),
}


def part_of(ref, spot):
    first, rows, cols, begin = (*spot, 0)[:4]
    return ref[first : first + rows, begin : begin + cols]


def gathers():
    pairs = []
    for part, first in enumerate((0, SIDE - REACH)):
        pairs += [(part * KV_EDGE + t, f) for t, f in strip_pairs(WIDE, REACH, first)]
    begin = GATHERS["qg_edges"][0]
    for part, first in enumerate((0, SIDE - RADIUS)):
        pairs += [(begin + part * QG_EDGE + t, f) for t, f in strip_pairs(TALL, RADIUS, first)]
    begin = GATHERS["core"][0]
    pairs += [(begin + t, y * SIDE + x) for t, (y, x) in enumerate(cells(INNER, INNER))]
    begin = GATHERS["rim"][0]
    for part, rows in enumerate((TOP, BOTTOM)):
        for t, (y, x) in enumerate(cells(rows, INNER)):
            pairs.append((begin + part * RIM_QUERIES + t, (y + RADIUS) * SIDE + x))
    return table(begin + 2 * RIM_QUERIES, WIDE * SIDE, pairs)


def spreads():
    pairs = []

    def add(name, column, token):
        if 0 <= token < SIDE * SIDE:
            pairs.append((SPREADS[name][0] + token, column))

    for t, (y, x) in enumerate(cells(INNER, INNER)):
        add("core", t, y * SIDE + x)
    for part, rows in enumerate((TOP, BOTTOM)):
        for t, (y, x) in enumerate(cells(rows, INNER)):
            add("rim", CORE_QUERIES + part * RIM_QUERIES + t, y * SIDE + x)
    for part, first in enumerate((0, SIDE - REACH)):
        for t, f in strip_pairs(WIDE, REACH, first):
            add("keys", part * OWN_EDGE + t - OWN_FROM, f - KV_ROWS)
    for part, first in enumerate((0, SIDE - RADIUS)):
        for t, f in strip_pairs(TALL, RADIUS, first):
            add("queries", part * QG_EDGE + t, f - QG_ROWS)
    return table(3 * SIDE * SIDE, SIDE * SIDE, pairs)


def coords(rows, cols, total, pad):
    spots = cells(rows, cols)
    spots += [(pad, pad)] * (total - len(spots))
    return np.asarray(spots, np.float32).T


def places(heads):
    keys = [coords(ALONG, ALONG, SIDE * SIDE, FAR)]
    queries = [np.tile(coords(INNER, INNER, CORE_QUERIES, -FAR), (1, heads))]
    for rows, key_rows in ((TOP, TOP_KEYS), (BOTTOM, BOTTOM_KEYS)):
        keys.append(coords(key_rows, ALONG, RIM_KEYS, FAR))
        queries.append(np.tile(coords(rows, INNER, RIM_QUERIES, -FAR), (1, heads)))
    wide, tall = range(-REACH, SIDE + REACH), range(-RADIUS, SIDE + RADIUS)
    for key_firsts, query_firsts in (
        ((0, -REACH), (0, -RADIUS)),
        ((SIDE - REACH, SIDE), (SIDE - RADIUS, SIDE)),
    ):
        keys += [coords(wide, range(f, f + REACH), KV_EDGE, FAR) for f in key_firsts]
        both = [coords(tall, range(f, f + RADIUS), QG_EDGE, -FAR) for f in query_firsts]
        queries += [np.tile(part, (1, heads)) for part in both]
    keys, queries = np.concatenate(keys, axis=1), np.concatenate(queries, axis=1)
    joined = np.full((8, queries.shape[1]), FAR, np.float32)
    joined[:2, : keys.shape[1]] = keys
    joined[2:4] = queries
    return jnp.asarray(joined)


def project_kernel(
    row, col, place, latent_any, gain, weight_any, out_weight_any, cotangent_any, kv, qg, far, near,
    latent, weight, out_weight, cotangent, sems
):
    copies = [
        pltpu.make_async_copy(source, target, sems.at[i])
        for i, (source, target) in enumerate(
            (
                (latent_any, latent),
                (weight_any.at[1], weight.at[1]),
                (weight_any.at[2], weight.at[2]),
                (weight_any.at[0], weight.at[0]),
                (cotangent_any, cotangent),
                (out_weight_any, out_weight),
            )
        )
    ]
    for copy in copies:
        copy.start()
    width = out_weight.shape[0]
    copies[0].wait()
    tokens = latent[...].astype(f32)
    inverse = lax.rsqrt(jnp.mean(tokens * tokens, axis=-1, keepdims=True) + 1e-06)
    normed = (tokens * inverse * gain[...]).astype(bf16)
    copies[1].wait()
    copies[2].wait()
    kv[:, :width] = nn(normed, weight[1]).astype(bf16)
    kv[:, width:] = nn(normed, weight[2]).astype(bf16)
    for copy in copies[3:]:
        copy.wait()
    query = nn(normed, weight[0]).astype(bf16)
    qg[:, :width] = query * jnp.asarray(HEAD_DIM ** (-0.5), bf16)
    qg[:, width:] = nt(cotangent[...], out_weight[...]).astype(bf16)
    count = latent.shape[0]
    odd = lax.rem(row[0], 2)
    for strip, at_end in ((far, odd), (near, 1 - odd)):
        first = pl.multiple_of(at_end * (count - KV_ROWS), SIDE)
        strip[:KV_ROWS] = kv[pl.ds(first, KV_ROWS), :]
        first = pl.multiple_of(at_end * (count - QG_ROWS), SIDE)
        strip[KV_ROWS:] = qg[pl.ds(first, QG_ROWS), :]


def tall_blocks(row, kv, qg, far, near):
    odd = lax.rem(row[0], 2) == 1
    above = jnp.where(odd, near[...], far[...])
    below = jnp.where(odd, far[...], near[...])
    kv_all = jnp.concatenate([above[:KV_ROWS], kv[...], below[:KV_ROWS]], axis=0)
    qg_all = jnp.concatenate([above[KV_ROWS:], qg[...], below[KV_ROWS:]], axis=0)
    return kv_all, qg_all


def edges_kernel(row, kv, qg, far, near, gather, after, left, right, kv_tall, qg_tall):
    kv_all, qg_all = tall_blocks(row, kv, qg, far, near)
    kv_tall[...] = kv_all
    qg_tall[...] = qg_all
    kv_edges = nn(part_of(gather, GATHERS["kv_edges"]), kv_all).astype(bf16)
    qg_edges = nn(part_of(gather, GATHERS["qg_edges"]), qg_all).astype(bf16)
    left[:KV_EDGE] = kv_edges[:KV_EDGE]
    left[KV_EDGE:] = qg_edges[:QG_EDGE]
    right[:KV_EDGE] = kv_edges[KV_EDGE:]
    right[KV_EDGE:] = qg_edges[QG_EDGE:]


def window_bias(spot, extent, keys, queries):
    key_y, key_x = keys[:, 0:1], keys[:, 1:2]
    top, left = (-(at * SIDE).astype(f32) for at in spot)
    bottom, right = ((((n - at) * SIDE) - 1).astype(f32) for at, n in zip(spot, extent))
    inside = (key_y >= top) & (key_y <= bottom) & (key_x >= left) & (key_x <= right)
    key_y = jnp.where(inside, key_y, FAR)
    apart = jnp.maximum(jnp.abs(key_y - queries[0:1, :]), jnp.abs(key_x - queries[1:2, :]))
    return jnp.where(apart <= RADIUS, 0.0, -1e30)


def by_head(block):
    width = block.shape[1]
    lanes = lax.broadcasted_iota(jnp.int32, (1, width), 1) // HEAD_DIM
    return [jnp.where(lanes == head, block, jnp.zeros_like(block)) for head in range(width // HEAD_DIM)]


def attention(bias, kv, groups, own):
    width = kv.shape[1] // 2
    key, value = kv[:, :width], kv[:, width:]
    query = jnp.concatenate([part for qg in groups for part in by_head(qg[:, :width])], axis=0)
    upstream = jnp.concatenate([part for qg in groups for part in by_head(qg[:, width:])], axis=0)
    scores = nt(key, query) + bias
    dots = nt(value, upstream)
    exponent = jnp.exp(scores - jnp.max(scores, axis=0, keepdims=True))
    scale = 1.0 / jnp.sum(exponent, axis=0, keepdims=True)
    weights = exponent * scale
    centre = jnp.sum(weights * dots, axis=0, keepdims=True)
    score_grads = (weights * (dots - centre)).astype(bf16)
    value_grad = nn(weights[own].astype(bf16), upstream)
    key_grad = nn(score_grads[own], query)
    count = groups[0].shape[0]
    heads = width // HEAD_DIM
    used = -(-count * heads // LANES) * LANES
    stacked = nn(key.astype(f32).T.astype(bf16), score_grads[:, :used]).T
    lanes = lax.broadcasted_iota(jnp.int32, (1, width), 1) // HEAD_DIM
    query_grad = stacked[:count]
    for head in range(1, heads):
        part = stacked[head * count : (head + 1) * count]
        query_grad = jnp.where(lanes == head, part, query_grad)
    return query_grad * (HEAD_DIM ** (-0.5)), key_grad, value_grad


def core_kernel(
    extent, row, col, kv, qg, points, gather, spread, query_out, pair_out, *biases
):
    count = kv.shape[0]
    width = kv.shape[1] // 2
    spot = (row[0], col[0])
    keys, queries = points[...].T, points[2:4]

    def mask(first_key, key_count, first_query, query_count):
        at_keys = keys[first_key : first_key + key_count]
        at_queries = queries[:, first_query : first_query + query_count]
        return window_bias(spot, extent, at_keys, at_queries)

    lanes = CORE_QUERIES * width // HEAD_DIM
    bias = mask(0, count, 0, lanes)
    inner = nn(part_of(gather, GATHERS["core"]), qg[...]).astype(bf16)
    query_grad, key_grad, value_grad = attention(bias, kv[...], [inner], slice(0, count))
    query_out[...] = nn(part_of(spread, SPREADS["core"]), query_grad.astype(bf16)).astype(bf16)
    pair_out[:, :width] = key_grad
    pair_out[:, width:] = value_grad
    first_key, first_query = count, lanes
    for side in biases:
        side[...] = mask(first_key, side.shape[0], first_query, side.shape[1])
        first_key, first_query = first_key + side.shape[0], first_query + side.shape[1]


def middle_kernel(
    kv, qg, top_bias, bottom_bias, gather, spread, core_query, core_pair, query_out, pair_out
):
    width = query_out.shape[1]
    rim = nn(part_of(gather, GATHERS["rim"]), qg[...]).astype(bf16)
    near_rows = REACH * SIDE
    last = kv.shape[0] - RIM_KEYS
    top = attention(
        top_bias[...], kv[:RIM_KEYS], [rim[:RIM_QUERIES]], slice(near_rows, 2 * near_rows)
    )
    bottom = attention(bottom_bias[...], kv[last:], [rim[RIM_QUERIES:]], slice(0, near_rows))
    query_grad = jnp.concatenate([top[0], bottom[0]], axis=0).astype(bf16)
    scattered = nn(part_of(spread, SPREADS["rim"]), query_grad)
    query_out[...] = (scattered + core_query[...].astype(f32)).astype(bf16)
    between = jnp.zeros((SIDE * SIDE - 2 * near_rows, width), f32)
    for which, first in ((1, 0), (2, width)):
        grad = jnp.concatenate([top[which], between, bottom[which]], axis=0)
        pair_out[:, first : first + width] = grad + core_pair[:, first : first + width]


def sides_kernel(
    leftward, from_left, rightward, from_right, query_mid, pair_mid, left_bias, right_bias,
    spread, weight, partial
):
    width = query_mid.shape[1]
    own = slice(OWN_FROM, OWN_FROM + OWN_EDGE)
    query_parts, pair_parts = [], []
    for mine, theirs, bias in (
        (leftward, from_left, left_bias),
        (rightward, from_right, right_bias),
    ):
        kv = jnp.concatenate([mine[:KV_EDGE], theirs[:KV_EDGE]], axis=0)
        groups = [mine[KV_EDGE:], theirs[KV_EDGE:]]
        query_grad, key_grad, value_grad = attention(bias[...], kv, groups, own)
        query_parts.append(query_grad)
        pair_parts.append(jnp.concatenate([key_grad, value_grad], axis=1))
    query_side = jnp.concatenate(query_parts, axis=0).astype(bf16)
    pair_side = jnp.concatenate(pair_parts, axis=0)
    coarse = pair_side.astype(bf16)
    fine = (pair_side - coarse.astype(f32)).astype(bf16)
    key_spread, query_spread = (part_of(spread, SPREADS[name]) for name in ("keys", "queries"))
    pair = pair_mid[...] + (nn(key_spread, coarse) + nn(key_spread, fine))
    query_grad = query_mid[...].astype(f32) + nn(query_spread, query_side)
    pair = pair.astype(bf16)
    total = nt(query_grad.astype(bf16), weight[0])
    total += nt(pair[:, :width], weight[1])
    total += nt(pair[:, width:], weight[2])
    partial[...] = total.astype(bf16)


def finish_kernel(place, received, latent, gain, cotangent, result):
    count = received.shape[1]
    first = pl.multiple_of(place[0] * count, count)
    tokens = latent[pl.ds(first, count), :].astype(f32)
    upstream = cotangent[pl.ds(first, count), :].astype(f32)
    summed = received[0].astype(f32)
    for part in range(1, received.shape[0]):
        summed += received[part].astype(f32)
    inverse = lax.rsqrt(jnp.mean(tokens * tokens, axis=-1, keepdims=True) + 1e-06)
    unit = tokens * inverse
    scaled = summed * gain[...]
    stat = jnp.mean(scaled * unit, axis=-1, keepdims=True)
    result[...] = upstream + inverse * (scaled - unit * stat)


def paired(block, axis, first):
    count = lax.axis_size(axis)
    route = []
    for low in range(first, count - 1, 2):
        route += [(low, low + 1), (low + 1, low)]
    return lax.ppermute(block, axis, route)


def moved(block, axis, distance):
    count = lax.axis_size(axis)
    route = [(i, i + distance) for i in range(count) if 0 <= i + distance < count]
    return lax.ppermute(block, axis, route)


def per_device(latent, norm_gain, qkv_weight, out_weight, cotangent):
    tile_rows, tile_cols, model_width = latent.shape
    head_cols = out_weight.shape[0]
    count = tile_rows * tile_cols
    tp = lax.axis_size("tp")
    flat_latent = latent.reshape(count, model_width)
    flat_cotangent = cotangent.reshape(count, model_width)
    gain = norm_gain.reshape(1, model_width)
    weight = qkv_weight.transpose(1, 0, 2)
    shape = pltpu.VMEM
    heads = head_cols // HEAD_DIM
    row = lax.axis_index("row").astype(jnp.int32).reshape(1)
    col = lax.axis_index("col").astype(jnp.int32).reshape(1)
    place = lax.axis_index("tp").astype(jnp.int32).reshape(1)
    extent = (lax.axis_size("row"), lax.axis_size("col"))
    edge = shape((KV_ROWS + QG_ROWS, 2 * head_cols), bf16)
    kv, qg, far, near = pl.pallas_call(
        project_kernel,
        out_shape=[shape((count, 2 * head_cols), bf16)] * 2 + [edge] * 2,
        in_specs=[SMEM, SMEM, SMEM, FAR_SPACE, HERE, FAR_SPACE, FAR_SPACE, FAR_SPACE],
        out_specs=[HERE] * 4,
        scratch_shapes=[
            pltpu.VMEM(flat_latent.shape, bf16),
            pltpu.VMEM(weight.shape, bf16),
            pltpu.VMEM(out_weight.shape, bf16),
            pltpu.VMEM(flat_cotangent.shape, bf16),
            pltpu.SemaphoreType.DMA((6,)),
        ],
        compiler_params=PARAMS,
        name="project",
    )(
        row,
        col,
        place,
        in_hbm(flat_latent),
        in_hbm(gain),
        in_hbm(weight),
        in_hbm(out_weight),
        in_hbm(flat_cotangent),
    )
    far = paired(far, "row", 1)
    near = paired(near, "row", 0)
    bias = shape((2 * KV_EDGE, 2 * QG_EDGE * heads), f32)
    rim = shape((RIM_KEYS, RIM_QUERIES * heads), f32)
    gather, spread = gathers(), spreads()
    core_query, core_pair, top_bias, bottom_bias, left_bias, right_bias = near_call(
        functools.partial(core_kernel, extent),
        "core",
        [shape((count, head_cols), bf16), shape((count, 2 * head_cols), f32), rim, rim, bias, bias],
        [SMEM] * 2 + [VMEM] * 5,
        row, col, kv, qg, places(heads), gather, spread,
    )
    side = shape((KV_EDGE + QG_EDGE, 2 * head_cols), bf16)
    tall = [shape((lines * SIDE, 2 * head_cols), bf16) for lines in (WIDE, TALL)]
    leftward, rightward, kv_tall, qg_tall = near_call(
        edges_kernel,
        "edges",
        [side] * 2 + tall,
        [SMEM] + [VMEM] * 6,
        row, kv, qg, far, near, gather, core_query,
    )
    from_left = moved(rightward, "col", 1)
    from_right = moved(leftward, "col", -1)
    query_mid, pair_mid = near_call(
        middle_kernel,
        "middle",
        [shape((count, head_cols), bf16), shape((count, 2 * head_cols), f32)],
        [VMEM] * 8,
        kv_tall, qg_tall, top_bias, bottom_bias, gather, spread, core_query, core_pair,
    )
    own = count // tp
    partial = near_call(
        sides_kernel,
        "sides",
        shape((count, model_width), bf16),
        [VMEM] * 10,
        leftward, from_left, rightward, from_right, query_mid, pair_mid, left_bias, right_bias,
        spread, weight,
    )
    received = lax.all_to_all(partial.reshape(tp, own, model_width), "tp", 0, 0)
    result = near_call(
        finish_kernel,
        "finish",
        jax.ShapeDtypeStruct((own, model_width), f32),
        [SMEM] + [VMEM] * 4,
        place, received, flat_latent, gain, flat_cotangent,
    )
    return result.reshape(own // tile_cols, tile_cols, model_width)


def solution(mesh):
    placed = (P("row", "col", None), P(), P(None, None, "tp"), P("tp", None), P("row", "col", None))
    return jax.shard_map(
        per_device,
        mesh=mesh,
        in_specs=placed,
        out_specs=P(("row", "tp"), "col", None),
        check_vma=False,
    )
```

```python
import functools

import jax
import jax.numpy as jnp
import numpy as np
from jax import lax
from jax.experimental import pallas as pl
from jax.experimental.pallas import tpu as pltpu
from jax.sharding import PartitionSpec as P

HEAD_DIM = 64
RADIUS = 3
REACH = 2 * RADIUS
SIDE = 16
WIDE = SIDE + 2 * REACH
TALL = SIDE + 2 * RADIUS
KV_ROWS = REACH * SIDE
QG_ROWS = RADIUS * SIDE
KV_EDGE = 168
QG_EDGE = 72
INNER = range(RADIUS, SIDE - RADIUS)
ALONG = range(SIDE)
TOP = range(-RADIUS, RADIUS)
BOTTOM = range(SIDE - RADIUS, SIDE + RADIUS)
TOP_KEYS = range(-REACH, REACH)
BOTTOM_KEYS = range(SIDE - REACH, SIDE + REACH)
CORE_QUERIES = 128
RIM_QUERIES = 64
RIM_KEYS = 2 * REACH * SIDE
OWN_FROM = 32
OWN_EDGE = 112
FAR = 1000.0
LANES = 128
bf16 = jnp.bfloat16
f32 = jnp.float32
VMEM = pl.BlockSpec(memory_space=pltpu.VMEM)
HERE = pl.BlockSpec(memory_space=pltpu.VMEM)
SMEM = pl.BlockSpec(memory_space=pltpu.SMEM)
FAR_SPACE = pl.BlockSpec(memory_space=pltpu.HBM)
PARAMS = pltpu.CompilerParams(vmem_limit_bytes=32 * 1024 * 1024)


def in_hbm(block):
    return pltpu.with_memory_space_constraint(block, pltpu.HBM)


def near_call(kernel, name, outs, specs, *operands, scratch=()):
    fixed = [
        pltpu.with_memory_space_constraint(x, pltpu.VMEM) if spec is VMEM else x
        for x, spec in zip(operands, specs)
    ]
    places = [VMEM if spec is HERE else spec for spec in specs]
    return pl.pallas_call(
        kernel,
        out_shape=outs,
        in_specs=places,
        out_specs=jax.tree.map(lambda _: VMEM, outs),
        scratch_shapes=scratch,
        compiler_params=PARAMS,
        name=name,
    )(*fixed)


def nt(a, b):
    return lax.dot_general(a, b, (((1,), (1,)), ((), ())), preferred_element_type=f32)


def tn(a, b):
    return lax.dot_general(a, b, (((0,), (0,)), ((), ())), preferred_element_type=f32)


def nn(a, b):
    return jnp.dot(a, b, preferred_element_type=f32)


def table(out_rows, in_rows, pairs):
    filled = np.zeros((out_rows, in_rows), np.float32)
    for target, source in pairs:
        filled[target, source] = 1.0
    return jnp.asarray(filled, bf16)


def strip_pairs(lines, count, first):
    return [
        (line * count + step, line * SIDE + first + step)
        for line in range(lines)
        for step in range(count)
    ]


def cells(rows, cols):
    return [(y, x) for y in rows for x in cols]


GATHERS = {
    "kv_edges": (0, 2 * KV_EDGE, WIDE * SIDE),
    "qg_edges": (2 * KV_EDGE, 2 * QG_EDGE, TALL * SIDE),
    "core": (2 * KV_EDGE + 2 * QG_EDGE, CORE_QUERIES, SIDE * SIDE),
    "rim": (2 * KV_EDGE + 2 * QG_EDGE + CORE_QUERIES, 2 * RIM_QUERIES, TALL * SIDE),
}
SPREADS = {
    "core": (0, SIDE * SIDE, CORE_QUERIES),
    "rim": (0, SIDE * SIDE, 2 * RIM_QUERIES, CORE_QUERIES),
    "keys": (SIDE * SIDE, SIDE * SIDE, 2 * OWN_EDGE),
    "queries": (2 * SIDE * SIDE, SIDE * SIDE, 2 * QG_EDGE),
}


def part_of(ref, spot):
    first, rows, cols, begin = (*spot, 0)[:4]
    return ref[first : first + rows, begin : begin + cols]


def gathers():
    pairs = []
    for part, first in enumerate((0, SIDE - REACH)):
        pairs += [(part * KV_EDGE + t, f) for t, f in strip_pairs(WIDE, REACH, first)]
    begin = GATHERS["qg_edges"][0]
    for part, first in enumerate((0, SIDE - RADIUS)):
        pairs += [(begin + part * QG_EDGE + t, f) for t, f in strip_pairs(TALL, RADIUS, first)]
    begin = GATHERS["core"][0]
    pairs += [(begin + t, y * SIDE + x) for t, (y, x) in enumerate(cells(INNER, INNER))]
    begin = GATHERS["rim"][0]
    for part, rows in enumerate((TOP, BOTTOM)):
        for t, (y, x) in enumerate(cells(rows, INNER)):
            pairs.append((begin + part * RIM_QUERIES + t, (y + RADIUS) * SIDE + x))
    return table(begin + 2 * RIM_QUERIES, WIDE * SIDE, pairs)


def spreads():
    pairs = []

    def add(name, column, token):
        if 0 <= token < SIDE * SIDE:
            pairs.append((SPREADS[name][0] + token, column))

    for t, (y, x) in enumerate(cells(INNER, INNER)):
        add("core", t, y * SIDE + x)
    for part, rows in enumerate((TOP, BOTTOM)):
        for t, (y, x) in enumerate(cells(rows, INNER)):
            add("rim", CORE_QUERIES + part * RIM_QUERIES + t, y * SIDE + x)
    for part, first in enumerate((0, SIDE - REACH)):
        for t, f in strip_pairs(WIDE, REACH, first):
            add("keys", part * OWN_EDGE + t - OWN_FROM, f - KV_ROWS)
    for part, first in enumerate((0, SIDE - RADIUS)):
        for t, f in strip_pairs(TALL, RADIUS, first):
            add("queries", part * QG_EDGE + t, f - QG_ROWS)
    return table(3 * SIDE * SIDE, SIDE * SIDE, pairs)


def coords(rows, cols, total, pad):
    spots = cells(rows, cols)
    spots += [(pad, pad)] * (total - len(spots))
    return np.asarray(spots, np.float32).T


def places(heads):
    keys = [coords(ALONG, ALONG, SIDE * SIDE, FAR)]
    queries = [np.tile(coords(INNER, INNER, CORE_QUERIES, -FAR), (1, heads))]
    for rows, key_rows in ((TOP, TOP_KEYS), (BOTTOM, BOTTOM_KEYS)):
        keys.append(coords(key_rows, ALONG, RIM_KEYS, FAR))
        queries.append(np.tile(coords(rows, INNER, RIM_QUERIES, -FAR), (1, heads)))
    wide, tall = range(-REACH, SIDE + REACH), range(-RADIUS, SIDE + RADIUS)
    for key_firsts, query_firsts in (
        ((0, -REACH), (0, -RADIUS)),
        ((SIDE - REACH, SIDE), (SIDE - RADIUS, SIDE)),
    ):
        keys += [coords(wide, range(f, f + REACH), KV_EDGE, FAR) for f in key_firsts]
        both = [coords(tall, range(f, f + RADIUS), QG_EDGE, -FAR) for f in query_firsts]
        queries += [np.tile(part, (1, heads)) for part in both]
    keys, queries = np.concatenate(keys, axis=1), np.concatenate(queries, axis=1)
    joined = np.full((8, queries.shape[1]), FAR, np.float32)
    joined[:2, : keys.shape[1]] = keys
    joined[2:4] = queries
    return jnp.asarray(joined)


def project_kernel(
    row, col, place, latent_any, gain, weight_any, out_weight_any, cotangent_any, kv, qg, far, near,
    latent, weight, out_weight, cotangent, sems
):
    copies = [
        pltpu.make_async_copy(source, target, sems.at[i])
        for i, (source, target) in enumerate(
            (
                (latent_any, latent),
                (weight_any.at[1], weight.at[1]),
                (weight_any.at[2], weight.at[2]),
                (weight_any.at[0], weight.at[0]),
                (cotangent_any, cotangent),
                (out_weight_any, out_weight),
            )
        )
    ]
    for copy in copies:
        copy.start()
    width = out_weight.shape[0]
    copies[0].wait()
    tokens = latent[...].astype(f32)
    inverse = lax.rsqrt(jnp.mean(tokens * tokens, axis=-1, keepdims=True) + 1e-06)
    normed = (tokens * inverse * gain[...]).astype(bf16)
    copies[1].wait()
    copies[2].wait()
    kv[:, :width] = nn(normed, weight[1]).astype(bf16)
    kv[:, width:] = nn(normed, weight[2]).astype(bf16)
    for copy in copies[3:]:
        copy.wait()
    query = nn(normed, weight[0]).astype(bf16)
    qg[:, :width] = query * jnp.asarray(HEAD_DIM ** (-0.5), bf16)
    qg[:, width:] = nt(cotangent[...], out_weight[...]).astype(bf16)
    count = latent.shape[0]
    odd = lax.rem(row[0], 2)
    for strip, at_end in ((far, odd), (near, 1 - odd)):
        first = pl.multiple_of(at_end * (count - KV_ROWS), SIDE)
        strip[:KV_ROWS] = kv[pl.ds(first, KV_ROWS), :]
        first = pl.multiple_of(at_end * (count - QG_ROWS), SIDE)
        strip[KV_ROWS:] = qg[pl.ds(first, QG_ROWS), :]


def tall_blocks(row, kv, qg, far, near):
    odd = lax.rem(row[0], 2) == 1
    above = jnp.where(odd, near[...], far[...])
    below = jnp.where(odd, far[...], near[...])
    kv_all = jnp.concatenate([above[:KV_ROWS], kv[...], below[:KV_ROWS]], axis=0)
    qg_all = jnp.concatenate([above[KV_ROWS:], qg[...], below[KV_ROWS:]], axis=0)
    return kv_all, qg_all


def edges_kernel(row, kv, qg, far, near, gather, after, left, right, kv_tall, qg_tall):
    kv_all, qg_all = tall_blocks(row, kv, qg, far, near)
    kv_tall[...] = kv_all
    qg_tall[...] = qg_all
    kv_edges = nn(part_of(gather, GATHERS["kv_edges"]), kv_all).astype(bf16)
    qg_edges = nn(part_of(gather, GATHERS["qg_edges"]), qg_all).astype(bf16)
    left[:KV_EDGE] = kv_edges[:KV_EDGE]
    left[KV_EDGE:] = qg_edges[:QG_EDGE]
    right[:KV_EDGE] = kv_edges[KV_EDGE:]
    right[KV_EDGE:] = qg_edges[QG_EDGE:]


def window_bias(spot, extent, keys, queries):
    key_y, key_x = keys[:, 0:1], keys[:, 1:2]
    top, left = (-(at * SIDE).astype(f32) for at in spot)
    bottom, right = ((((n - at) * SIDE) - 1).astype(f32) for at, n in zip(spot, extent))
    inside = (key_y >= top) & (key_y <= bottom) & (key_x >= left) & (key_x <= right)
    key_y = jnp.where(inside, key_y, FAR)
    apart = jnp.maximum(jnp.abs(key_y - queries[0:1, :]), jnp.abs(key_x - queries[1:2, :]))
    return jnp.where(apart <= RADIUS, 0.0, -1e30)


def by_head(block):
    width = block.shape[1]
    lanes = lax.broadcasted_iota(jnp.int32, (1, width), 1) // HEAD_DIM
    return [jnp.where(lanes == head, block, jnp.zeros_like(block)) for head in range(width // HEAD_DIM)]


def attention(bias, kv, groups, own):
    width = kv.shape[1] // 2
    key, value = kv[:, :width], kv[:, width:]
    query = jnp.concatenate([part for qg in groups for part in by_head(qg[:, :width])], axis=0)
    upstream = jnp.concatenate([part for qg in groups for part in by_head(qg[:, width:])], axis=0)
    scores = nt(key, query) + bias
    dots = nt(value, upstream)
    exponent = jnp.exp(scores - jnp.max(scores, axis=0, keepdims=True))
    scale = 1.0 / jnp.sum(exponent, axis=0, keepdims=True)
    weights = exponent * scale
    centre = jnp.sum(weights * dots, axis=0, keepdims=True)
    score_grads = (weights * (dots - centre)).astype(bf16)
    value_grad = nn(weights[own].astype(bf16), upstream)
    key_grad = nn(score_grads[own], query)
    count = groups[0].shape[0]
    heads = width // HEAD_DIM
    used = -(-count * heads // LANES) * LANES
    stacked = tn(score_grads[:, :used], key)
    lanes = lax.broadcasted_iota(jnp.int32, (1, width), 1) // HEAD_DIM
    query_grad = stacked[:count]
    for head in range(1, heads):
        part = stacked[head * count : (head + 1) * count]
        query_grad = jnp.where(lanes == head, part, query_grad)
    return query_grad * (HEAD_DIM ** (-0.5)), key_grad, value_grad


def core_kernel(
    extent, row, col, kv, qg, points, gather, spread, query_out, pair_out, *biases
):
    count = kv.shape[0]
    width = kv.shape[1] // 2
    spot = (row[0], col[0])
    keys, queries = points[...].T, points[2:4]

    def mask(first_key, key_count, first_query, query_count):
        at_keys = keys[first_key : first_key + key_count]
        at_queries = queries[:, first_query : first_query + query_count]
        return window_bias(spot, extent, at_keys, at_queries)

    lanes = CORE_QUERIES * width // HEAD_DIM
    bias = mask(0, count, 0, lanes)
    inner = nn(part_of(gather, GATHERS["core"]), qg[...]).astype(bf16)
    query_grad, key_grad, value_grad = attention(bias, kv[...], [inner], slice(0, count))
    query_out[...] = nn(part_of(spread, SPREADS["core"]), query_grad.astype(bf16)).astype(bf16)
    pair_out[:, :width] = key_grad
    pair_out[:, width:] = value_grad
    first_key, first_query = count, lanes
    for side in biases:
        side[...] = mask(first_key, side.shape[0], first_query, side.shape[1])
        first_key, first_query = first_key + side.shape[0], first_query + side.shape[1]


def middle_kernel(
    kv, qg, top_bias, bottom_bias, gather, spread, core_query, core_pair, query_out, pair_out
):
    width = query_out.shape[1]
    rim = nn(part_of(gather, GATHERS["rim"]), qg[...]).astype(bf16)
    near_rows = REACH * SIDE
    last = kv.shape[0] - RIM_KEYS
    top = attention(
        top_bias[...], kv[:RIM_KEYS], [rim[:RIM_QUERIES]], slice(near_rows, 2 * near_rows)
    )
    bottom = attention(bottom_bias[...], kv[last:], [rim[RIM_QUERIES:]], slice(0, near_rows))
    query_grad = jnp.concatenate([top[0], bottom[0]], axis=0).astype(bf16)
    scattered = nn(part_of(spread, SPREADS["rim"]), query_grad)
    query_out[...] = (scattered + core_query[...].astype(f32)).astype(bf16)
    between = jnp.zeros((SIDE * SIDE - 2 * near_rows, width), f32)
    for which, first in ((1, 0), (2, width)):
        grad = jnp.concatenate([top[which], between, bottom[which]], axis=0)
        pair_out[:, first : first + width] = grad + core_pair[:, first : first + width]


def side_grads(mine, theirs, bias):
    own = slice(OWN_FROM, OWN_FROM + OWN_EDGE)
    kv = jnp.concatenate([mine[:KV_EDGE], theirs[:KV_EDGE]], axis=0)
    groups = [mine[KV_EDGE:], theirs[KV_EDGE:]]
    query_grad, key_grad, value_grad = attention(bias[...], kv, groups, own)
    return query_grad.astype(bf16), jnp.concatenate([key_grad, value_grad], axis=1)


def right_kernel(rightward, from_right, right_bias, query_out, pair_out):
    query_out[...], pair_out[...] = side_grads(rightward, from_right, right_bias)


def sides_kernel(
    leftward, from_left, left_bias, right_query, right_pair, query_mid, pair_mid, spread, weight,
    partial
):
    width = query_mid.shape[1]
    left_query, left_pair = side_grads(leftward, from_left, left_bias)
    query_side = jnp.concatenate([left_query, right_query[...]], axis=0)
    pair_side = jnp.concatenate([left_pair, right_pair[...]], axis=0)
    coarse = pair_side.astype(bf16)
    fine = (pair_side - coarse.astype(f32)).astype(bf16)
    key_spread, query_spread = (part_of(spread, SPREADS[name]) for name in ("keys", "queries"))
    pair = pair_mid[...] + (nn(key_spread, coarse) + nn(key_spread, fine))
    query_grad = query_mid[...].astype(f32) + nn(query_spread, query_side)
    pair = pair.astype(bf16)
    total = nt(query_grad.astype(bf16), weight[0])
    total += nt(pair[:, :width], weight[1])
    total += nt(pair[:, width:], weight[2])
    partial[...] = total.astype(bf16)


def finish_kernel(place, received, latent, gain, cotangent, result):
    count = received.shape[1]
    first = pl.multiple_of(place[0] * count, count)
    tokens = latent[pl.ds(first, count), :].astype(f32)
    upstream = cotangent[pl.ds(first, count), :].astype(f32)
    summed = received[0].astype(f32)
    for part in range(1, received.shape[0]):
        summed += received[part].astype(f32)
    inverse = lax.rsqrt(jnp.mean(tokens * tokens, axis=-1, keepdims=True) + 1e-06)
    unit = tokens * inverse
    scaled = summed * gain[...]
    stat = jnp.mean(scaled * unit, axis=-1, keepdims=True)
    result[...] = upstream + inverse * (scaled - unit * stat)


def paired(block, axis, first):
    count = lax.axis_size(axis)
    route = []
    for low in range(first, count - 1, 2):
        route += [(low, low + 1), (low + 1, low)]
    return lax.ppermute(block, axis, route)


def moved(block, axis, distance):
    count = lax.axis_size(axis)
    route = [(i, i + distance) for i in range(count) if 0 <= i + distance < count]
    return lax.ppermute(block, axis, route)


def per_device(latent, norm_gain, qkv_weight, out_weight, cotangent):
    tile_rows, tile_cols, model_width = latent.shape
    head_cols = out_weight.shape[0]
    count = tile_rows * tile_cols
    tp = lax.axis_size("tp")
    flat_latent = latent.reshape(count, model_width)
    flat_cotangent = cotangent.reshape(count, model_width)
    gain = norm_gain.reshape(1, model_width)
    weight = qkv_weight.transpose(1, 0, 2)
    shape = pltpu.VMEM
    heads = head_cols // HEAD_DIM
    row = lax.axis_index("row").astype(jnp.int32).reshape(1)
    col = lax.axis_index("col").astype(jnp.int32).reshape(1)
    place = lax.axis_index("tp").astype(jnp.int32).reshape(1)
    extent = (lax.axis_size("row"), lax.axis_size("col"))
    edge = shape((KV_ROWS + QG_ROWS, 2 * head_cols), bf16)
    kv, qg, far, near = pl.pallas_call(
        project_kernel,
        out_shape=[shape((count, 2 * head_cols), bf16)] * 2 + [edge] * 2,
        in_specs=[SMEM, SMEM, SMEM, FAR_SPACE, HERE, FAR_SPACE, FAR_SPACE, FAR_SPACE],
        out_specs=[HERE] * 4,
        scratch_shapes=[
            pltpu.VMEM(flat_latent.shape, bf16),
            pltpu.VMEM(weight.shape, bf16),
            pltpu.VMEM(out_weight.shape, bf16),
            pltpu.VMEM(flat_cotangent.shape, bf16),
            pltpu.SemaphoreType.DMA((6,)),
        ],
        compiler_params=PARAMS,
        name="project",
    )(
        row,
        col,
        place,
        in_hbm(flat_latent),
        in_hbm(gain),
        in_hbm(weight),
        in_hbm(out_weight),
        in_hbm(flat_cotangent),
    )
    far = paired(far, "row", 1)
    near = paired(near, "row", 0)
    bias = shape((2 * KV_EDGE, 2 * QG_EDGE * heads), f32)
    rim = shape((RIM_KEYS, RIM_QUERIES * heads), f32)
    gather, spread = gathers(), spreads()
    core_query, core_pair, top_bias, bottom_bias, left_bias, right_bias = near_call(
        functools.partial(core_kernel, extent),
        "core",
        [shape((count, head_cols), bf16), shape((count, 2 * head_cols), f32), rim, rim, bias, bias],
        [SMEM] * 2 + [VMEM] * 5,
        row, col, kv, qg, places(heads), gather, spread,
    )
    side = shape((KV_EDGE + QG_EDGE, 2 * head_cols), bf16)
    tall = [shape((lines * SIDE, 2 * head_cols), bf16) for lines in (WIDE, TALL)]
    leftward, rightward, kv_tall, qg_tall = near_call(
        edges_kernel,
        "edges",
        [side] * 2 + tall,
        [SMEM] + [VMEM] * 6,
        row, kv, qg, far, near, gather, core_query,
    )
    from_left = moved(rightward, "col", 1)
    from_right = moved(leftward, "col", -1)
    query_mid, pair_mid = near_call(
        middle_kernel,
        "middle",
        [shape((count, head_cols), bf16), shape((count, 2 * head_cols), f32)],
        [VMEM] * 8,
        kv_tall, qg_tall, top_bias, bottom_bias, gather, spread, core_query, core_pair,
    )
    own = count // tp
    right_query, right_pair = near_call(
        right_kernel,
        "right_side",
        [shape((QG_EDGE, head_cols), bf16), shape((OWN_EDGE, 2 * head_cols), f32)],
        [VMEM] * 3,
        rightward, from_right, right_bias,
    )
    partial = near_call(
        sides_kernel,
        "sides",
        shape((count, model_width), bf16),
        [VMEM] * 9,
        leftward, from_left, left_bias, right_query, right_pair, query_mid, pair_mid, spread,
        weight,
    )
    received = lax.all_to_all(partial.reshape(tp, own, model_width), "tp", 0, 0)
    result = near_call(
        finish_kernel,
        "finish",
        jax.ShapeDtypeStruct((own, model_width), f32),
        [SMEM] + [VMEM] * 4,
        place, received, flat_latent, gain, flat_cotangent,
    )
    return result.reshape(own // tile_cols, tile_cols, model_width)


def solution(mesh):
    placed = (P("row", "col", None), P(), P(None, None, "tp"), P("tp", None), P("row", "col", None))
    return jax.shard_map(
        per_device,
        mesh=mesh,
        in_specs=placed,
        out_specs=P(("row", "tp"), "col", None),
        check_vma=False,
    )
```

```python
import functools

import jax
import jax.numpy as jnp
import numpy as np
from jax import lax
from jax.experimental import pallas as pl
from jax.experimental.pallas import tpu as pltpu
from jax.sharding import PartitionSpec as P

HEAD_DIM = 64
RADIUS = 3
REACH = 2 * RADIUS
SIDE = 16
WIDE = SIDE + 2 * REACH
TALL = SIDE + 2 * RADIUS
KV_ROWS = REACH * SIDE
QG_ROWS = RADIUS * SIDE
KV_EDGE = 168
QG_EDGE = 72
INNER = range(RADIUS, SIDE - RADIUS)
ALONG = range(SIDE)
TOP = range(-RADIUS, RADIUS)
BOTTOM = range(SIDE - RADIUS, SIDE + RADIUS)
TOP_KEYS = range(-REACH, REACH)
BOTTOM_KEYS = range(SIDE - REACH, SIDE + REACH)
CORE_QUERIES = 128
RIM_QUERIES = 64
RIM_KEYS = 2 * REACH * SIDE
OWN_FROM = 32
OWN_EDGE = 112
FAR = 1000.0
LANES = 128
bf16 = jnp.bfloat16
f32 = jnp.float32
VMEM = pl.BlockSpec(memory_space=pltpu.VMEM)
HERE = pl.BlockSpec(memory_space=pltpu.VMEM)
SMEM = pl.BlockSpec(memory_space=pltpu.SMEM)
FAR_SPACE = pl.BlockSpec(memory_space=pltpu.HBM)
PARAMS = pltpu.CompilerParams(vmem_limit_bytes=32 * 1024 * 1024)


def in_hbm(block):
    return pltpu.with_memory_space_constraint(block, pltpu.HBM)


def near_call(kernel, name, outs, specs, *operands, scratch=()):
    fixed = [
        pltpu.with_memory_space_constraint(x, pltpu.VMEM) if spec is VMEM else x
        for x, spec in zip(operands, specs)
    ]
    places = [VMEM if spec is HERE else spec for spec in specs]
    return pl.pallas_call(
        kernel,
        out_shape=outs,
        in_specs=places,
        out_specs=jax.tree.map(lambda _: VMEM, outs),
        scratch_shapes=scratch,
        compiler_params=PARAMS,
        name=name,
    )(*fixed)


def nt(a, b):
    return lax.dot_general(a, b, (((1,), (1,)), ((), ())), preferred_element_type=f32)


def tn(a, b):
    return lax.dot_general(a, b, (((0,), (0,)), ((), ())), preferred_element_type=f32)


def nn(a, b):
    return jnp.dot(a, b, preferred_element_type=f32)


def strip_pairs(lines, count, first):
    return [
        (line * count + step, line * SIDE + first + step)
        for line in range(lines)
        for step in range(count)
    ]


def cells(rows, cols):
    return [(y, x) for y in rows for x in cols]


GATHERS = {
    "kv_edges": (0, 2 * KV_EDGE, WIDE * SIDE),
    "qg_edges": (2 * KV_EDGE, 2 * QG_EDGE, TALL * SIDE),
    "core": (2 * KV_EDGE + 2 * QG_EDGE, CORE_QUERIES, SIDE * SIDE),
    "rim": (2 * KV_EDGE + 2 * QG_EDGE + CORE_QUERIES, 2 * RIM_QUERIES, TALL * SIDE),
}
SPREADS = {
    "core": (0, SIDE * SIDE, CORE_QUERIES),
    "rim": (0, SIDE * SIDE, 2 * RIM_QUERIES, CORE_QUERIES),
    "keys": (SIDE * SIDE, SIDE * SIDE, 2 * OWN_EDGE),
    "queries": (2 * SIDE * SIDE, SIDE * SIDE, 2 * QG_EDGE),
}


def part_of(ref, spot):
    first, rows, cols, begin = (*spot, 0)[:4]
    return ref[first : first + rows, begin : begin + cols]


def gathers():
    pairs = []
    for part, first in enumerate((0, SIDE - REACH)):
        pairs += [(part * KV_EDGE + t, f) for t, f in strip_pairs(WIDE, REACH, first)]
    begin = GATHERS["qg_edges"][0]
    for part, first in enumerate((0, SIDE - RADIUS)):
        pairs += [(begin + part * QG_EDGE + t, f) for t, f in strip_pairs(TALL, RADIUS, first)]
    begin = GATHERS["core"][0]
    pairs += [(begin + t, y * SIDE + x) for t, (y, x) in enumerate(cells(INNER, INNER))]
    begin = GATHERS["rim"][0]
    for part, rows in enumerate((TOP, BOTTOM)):
        for t, (y, x) in enumerate(cells(rows, INNER)):
            pairs.append((begin + part * RIM_QUERIES + t, (y + RADIUS) * SIDE + x))
    sources = np.full((begin + 2 * RIM_QUERIES,), -1.0, np.float32)
    for target, source in pairs:
        sources[target] = source
    return sources


def spreads():
    pairs = []

    def add(name, column, token):
        if 0 <= token < SIDE * SIDE:
            pairs.append((SPREADS[name][0] + token, column))

    for t, (y, x) in enumerate(cells(INNER, INNER)):
        add("core", t, y * SIDE + x)
    for part, rows in enumerate((TOP, BOTTOM)):
        for t, (y, x) in enumerate(cells(rows, INNER)):
            add("rim", CORE_QUERIES + part * RIM_QUERIES + t, y * SIDE + x)
    for part, first in enumerate((0, SIDE - REACH)):
        for t, f in strip_pairs(WIDE, REACH, first):
            add("keys", part * OWN_EDGE + t - OWN_FROM, f - KV_ROWS)
    for part, first in enumerate((0, SIDE - RADIUS)):
        for t, f in strip_pairs(TALL, RADIUS, first):
            add("queries", part * QG_EDGE + t, f - QG_ROWS)
    targets = np.full((3, SIDE * SIDE), -1.0, np.float32)
    for target, column in pairs:
        targets[target // (SIDE * SIDE), column] = target % (SIDE * SIDE)
    return targets


def coords(rows, cols, total, pad):
    spots = cells(rows, cols)
    spots += [(pad, pad)] * (total - len(spots))
    return np.asarray(spots, np.float32).T


def places(heads):
    keys = [coords(ALONG, ALONG, SIDE * SIDE, FAR)]
    queries = [np.tile(coords(INNER, INNER, CORE_QUERIES, -FAR), (1, heads))]
    for rows, key_rows in ((TOP, TOP_KEYS), (BOTTOM, BOTTOM_KEYS)):
        keys.append(coords(key_rows, ALONG, RIM_KEYS, FAR))
        queries.append(np.tile(coords(rows, INNER, RIM_QUERIES, -FAR), (1, heads)))
    wide, tall = range(-REACH, SIDE + REACH), range(-RADIUS, SIDE + RADIUS)
    for key_firsts, query_firsts in (
        ((0, -REACH), (0, -RADIUS)),
        ((SIDE - REACH, SIDE), (SIDE - RADIUS, SIDE)),
    ):
        keys += [coords(wide, range(f, f + REACH), KV_EDGE, FAR) for f in key_firsts]
        both = [coords(tall, range(f, f + RADIUS), QG_EDGE, -FAR) for f in query_firsts]
        queries += [np.tile(part, (1, heads)) for part in both]
    keys, queries = np.concatenate(keys, axis=1), np.concatenate(queries, axis=1)
    joined = np.full((8, queries.shape[1]), FAR, np.float32)
    joined[:2, : keys.shape[1]] = keys
    joined[2:4] = queries
    sources = gathers()
    joined[4, : sources.shape[0]] = sources
    joined[5:, : SIDE * SIDE] = spreads()
    return jnp.asarray(joined), (sources.shape[0], WIDE * SIDE)


def project_kernel(
    row, col, place, latent_any, gain, weight_any, out_weight_any, cotangent_any, kv, qg, far, near,
    latent, weight, out_weight, cotangent, sems
):
    copies = [
        pltpu.make_async_copy(source, target, sems.at[i])
        for i, (source, target) in enumerate(
            (
                (latent_any, latent),
                (weight_any.at[1], weight.at[1]),
                (weight_any.at[2], weight.at[2]),
                (weight_any.at[0], weight.at[0]),
                (cotangent_any, cotangent),
                (out_weight_any, out_weight),
            )
        )
    ]
    for copy in copies:
        copy.start()
    width = out_weight.shape[0]
    copies[0].wait()
    tokens = latent[...].astype(f32)
    inverse = lax.rsqrt(jnp.mean(tokens * tokens, axis=-1, keepdims=True) + 1e-06)
    normed = (tokens * inverse * gain[...]).astype(bf16)
    copies[1].wait()
    copies[2].wait()
    kv[:, :width] = nn(normed, weight[1]).astype(bf16)
    kv[:, width:] = nn(normed, weight[2]).astype(bf16)
    for copy in copies[3:]:
        copy.wait()
    query = nn(normed, weight[0]).astype(bf16)
    qg[:, :width] = query * jnp.asarray(HEAD_DIM ** (-0.5), bf16)
    qg[:, width:] = nt(cotangent[...], out_weight[...]).astype(bf16)
    count = latent.shape[0]
    odd = lax.rem(row[0], 2)
    for strip, at_end in ((far, odd), (near, 1 - odd)):
        first = pl.multiple_of(at_end * (count - KV_ROWS), SIDE)
        strip[:KV_ROWS] = kv[pl.ds(first, KV_ROWS), :]
        first = pl.multiple_of(at_end * (count - QG_ROWS), SIDE)
        strip[KV_ROWS:] = qg[pl.ds(first, QG_ROWS), :]


def tall_blocks(row, kv, qg, far, near):
    odd = lax.rem(row[0], 2) == 1
    above = jnp.where(odd, near[...], far[...])
    below = jnp.where(odd, far[...], near[...])
    kv_all = jnp.concatenate([above[:KV_ROWS], kv[...], below[:KV_ROWS]], axis=0)
    qg_all = jnp.concatenate([above[KV_ROWS:], qg[...], below[KV_ROWS:]], axis=0)
    return kv_all, qg_all


def edges_kernel(row, kv, qg, far, near, gather, left, right, kv_tall, qg_tall):
    kv_all, qg_all = tall_blocks(row, kv, qg, far, near)
    kv_tall[...] = kv_all
    qg_tall[...] = qg_all
    kv_edges = nn(part_of(gather, GATHERS["kv_edges"]), kv_all).astype(bf16)
    qg_edges = nn(part_of(gather, GATHERS["qg_edges"]), qg_all).astype(bf16)
    left[:KV_EDGE] = kv_edges[:KV_EDGE]
    left[KV_EDGE:] = qg_edges[:QG_EDGE]
    right[:KV_EDGE] = kv_edges[KV_EDGE:]
    right[KV_EDGE:] = qg_edges[QG_EDGE:]


def window_bias(spot, extent, keys, queries):
    key_y, key_x = keys[:, 0:1], keys[:, 1:2]
    top, left = (-(at * SIDE).astype(f32) for at in spot)
    bottom, right = ((((n - at) * SIDE) - 1).astype(f32) for at, n in zip(spot, extent))
    inside = (key_y >= top) & (key_y <= bottom) & (key_x >= left) & (key_x <= right)
    key_y = jnp.where(inside, key_y, FAR)
    apart = jnp.maximum(jnp.abs(key_y - queries[0:1, :]), jnp.abs(key_x - queries[1:2, :]))
    return jnp.where(apart <= RADIUS, 0.0, -1e30)


def by_head(block):
    width = block.shape[1]
    lanes = lax.broadcasted_iota(jnp.int32, (1, width), 1) // HEAD_DIM
    return [jnp.where(lanes == head, block, jnp.zeros_like(block)) for head in range(width // HEAD_DIM)]


def attention(bias, kv, groups, own):
    width = kv.shape[1] // 2
    key, value = kv[:, :width], kv[:, width:]
    query = jnp.concatenate([part for qg in groups for part in by_head(qg[:, :width])], axis=0)
    upstream = jnp.concatenate([part for qg in groups for part in by_head(qg[:, width:])], axis=0)
    scores = nt(key, query) + bias
    dots = nt(value, upstream)
    exponent = jnp.exp(scores - jnp.max(scores, axis=0, keepdims=True))
    scale = 1.0 / jnp.sum(exponent, axis=0, keepdims=True)
    weights = exponent * scale
    centre = jnp.sum(weights * dots, axis=0, keepdims=True)
    score_grads = (weights * (dots - centre)).astype(bf16)
    value_grad = nn(weights[own].astype(bf16), upstream)
    key_grad = nn(score_grads[own], query)
    count = groups[0].shape[0]
    heads = width // HEAD_DIM
    used = -(-count * heads // LANES) * LANES
    stacked = tn(score_grads[:, :used], key)
    lanes = lax.broadcasted_iota(jnp.int32, (1, width), 1) // HEAD_DIM
    query_grad = stacked[:count]
    for head in range(1, heads):
        part = stacked[head * count : (head + 1) * count]
        query_grad = jnp.where(lanes == head, part, query_grad)
    return query_grad * (HEAD_DIM ** (-0.5)), key_grad, value_grad


def core_kernel(
    extent, row, col, kv, qg, points, gather, spread, query_out, pair_out, *biases
):
    count = kv.shape[0]
    width = kv.shape[1] // 2
    spot = (row[0], col[0])
    columns = points[...].T
    keys, queries = columns[:, :2], points[2:4]
    picked = columns[: gather.shape[0], 4:5].astype(jnp.int32)
    sources = lax.broadcasted_iota(jnp.int32, gather.shape, 1)
    gather[...] = jnp.where(sources == picked, 1.0, 0.0).astype(bf16)
    tokens = lax.broadcasted_iota(jnp.int32, (count, count), 0)
    for part in range(3):
        targets = points[5 + part : 6 + part, :count].astype(jnp.int32)
        hits = jnp.where(tokens == targets, 1.0, 0.0).astype(bf16)
        spread[part * count : (part + 1) * count] = hits

    def mask(first_key, key_count, first_query, query_count):
        at_keys = keys[first_key : first_key + key_count]
        at_queries = queries[:, first_query : first_query + query_count]
        return window_bias(spot, extent, at_keys, at_queries)

    lanes = CORE_QUERIES * width // HEAD_DIM
    bias = mask(0, count, 0, lanes)
    inner = nn(part_of(gather, GATHERS["core"]), qg[...]).astype(bf16)
    query_grad, key_grad, value_grad = attention(bias, kv[...], [inner], slice(0, count))
    query_out[...] = nn(part_of(spread, SPREADS["core"]), query_grad.astype(bf16)).astype(bf16)
    pair_out[:, :width] = key_grad
    pair_out[:, width:] = value_grad
    first_key, first_query = count, lanes
    for side in biases:
        side[...] = mask(first_key, side.shape[0], first_query, side.shape[1])
        first_key, first_query = first_key + side.shape[0], first_query + side.shape[1]


def middle_kernel(
    kv, qg, top_bias, bottom_bias, gather, spread, core_query, core_pair, query_out, pair_out
):
    width = query_out.shape[1]
    rim = nn(part_of(gather, GATHERS["rim"]), qg[...]).astype(bf16)
    near_rows = REACH * SIDE
    last = kv.shape[0] - RIM_KEYS
    top = attention(
        top_bias[...], kv[:RIM_KEYS], [rim[:RIM_QUERIES]], slice(near_rows, 2 * near_rows)
    )
    bottom = attention(bottom_bias[...], kv[last:], [rim[RIM_QUERIES:]], slice(0, near_rows))
    query_grad = jnp.concatenate([top[0], bottom[0]], axis=0).astype(bf16)
    scattered = nn(part_of(spread, SPREADS["rim"]), query_grad)
    query_out[...] = (scattered + core_query[...].astype(f32)).astype(bf16)
    between = jnp.zeros((SIDE * SIDE - 2 * near_rows, width), f32)
    for which, first in ((1, 0), (2, width)):
        grad = jnp.concatenate([top[which], between, bottom[which]], axis=0)
        pair_out[:, first : first + width] = grad + core_pair[:, first : first + width]


def side_grads(mine, theirs, bias):
    own = slice(OWN_FROM, OWN_FROM + OWN_EDGE)
    kv = jnp.concatenate([mine[:KV_EDGE], theirs[:KV_EDGE]], axis=0)
    groups = [mine[KV_EDGE:], theirs[KV_EDGE:]]
    query_grad, key_grad, value_grad = attention(bias[...], kv, groups, own)
    return query_grad.astype(bf16), jnp.concatenate([key_grad, value_grad], axis=1)


def right_kernel(rightward, from_right, right_bias, query_out, pair_out):
    query_out[...], pair_out[...] = side_grads(rightward, from_right, right_bias)


def sides_kernel(
    leftward, from_left, left_bias, right_query, right_pair, query_mid, pair_mid, spread, weight,
    partial
):
    width = query_mid.shape[1]
    left_query, left_pair = side_grads(leftward, from_left, left_bias)
    query_side = jnp.concatenate([left_query, right_query[...]], axis=0)
    pair_side = jnp.concatenate([left_pair, right_pair[...]], axis=0)
    coarse = pair_side.astype(bf16)
    fine = (pair_side - coarse.astype(f32)).astype(bf16)
    key_spread, query_spread = (part_of(spread, SPREADS[name]) for name in ("keys", "queries"))
    pair = pair_mid[...] + (nn(key_spread, coarse) + nn(key_spread, fine))
    query_grad = query_mid[...].astype(f32) + nn(query_spread, query_side)
    pair = pair.astype(bf16)
    total = nt(query_grad.astype(bf16), weight[0])
    total += nt(pair[:, :width], weight[1])
    total += nt(pair[:, width:], weight[2])
    partial[...] = total.astype(bf16)


def finish_kernel(place, received, latent, gain, cotangent, result):
    count = received.shape[1]
    first = pl.multiple_of(place[0] * count, count)
    tokens = latent[pl.ds(first, count), :].astype(f32)
    upstream = cotangent[pl.ds(first, count), :].astype(f32)
    summed = received[0].astype(f32)
    for part in range(1, received.shape[0]):
        summed += received[part].astype(f32)
    inverse = lax.rsqrt(jnp.mean(tokens * tokens, axis=-1, keepdims=True) + 1e-06)
    unit = tokens * inverse
    scaled = summed * gain[...]
    stat = jnp.mean(scaled * unit, axis=-1, keepdims=True)
    result[...] = upstream + inverse * (scaled - unit * stat)


def paired(block, axis, first):
    count = lax.axis_size(axis)
    route = []
    for low in range(first, count - 1, 2):
        route += [(low, low + 1), (low + 1, low)]
    return lax.ppermute(block, axis, route)


def moved(block, axis, distance):
    count = lax.axis_size(axis)
    route = [(i, i + distance) for i in range(count) if 0 <= i + distance < count]
    return lax.ppermute(block, axis, route)


def per_device(latent, norm_gain, qkv_weight, out_weight, cotangent):
    tile_rows, tile_cols, model_width = latent.shape
    head_cols = out_weight.shape[0]
    count = tile_rows * tile_cols
    tp = lax.axis_size("tp")
    flat_latent = latent.reshape(count, model_width)
    flat_cotangent = cotangent.reshape(count, model_width)
    gain = norm_gain.reshape(1, model_width)
    weight = qkv_weight.transpose(1, 0, 2)
    shape = pltpu.VMEM
    heads = head_cols // HEAD_DIM
    row = lax.axis_index("row").astype(jnp.int32).reshape(1)
    col = lax.axis_index("col").astype(jnp.int32).reshape(1)
    place = lax.axis_index("tp").astype(jnp.int32).reshape(1)
    extent = (lax.axis_size("row"), lax.axis_size("col"))
    edge = shape((KV_ROWS + QG_ROWS, 2 * head_cols), bf16)
    kv, qg, far, near = pl.pallas_call(
        project_kernel,
        out_shape=[shape((count, 2 * head_cols), bf16)] * 2 + [edge] * 2,
        in_specs=[SMEM, SMEM, SMEM, FAR_SPACE, HERE, FAR_SPACE, FAR_SPACE, FAR_SPACE],
        out_specs=[HERE] * 4,
        scratch_shapes=[
            pltpu.VMEM(flat_latent.shape, bf16),
            pltpu.VMEM(weight.shape, bf16),
            pltpu.VMEM(out_weight.shape, bf16),
            pltpu.VMEM(flat_cotangent.shape, bf16),
            pltpu.SemaphoreType.DMA((6,)),
        ],
        compiler_params=PARAMS,
        name="project",
    )(
        row,
        col,
        place,
        in_hbm(flat_latent),
        in_hbm(gain),
        in_hbm(weight),
        in_hbm(out_weight),
        in_hbm(flat_cotangent),
    )
    far = paired(far, "row", 1)
    near = paired(near, "row", 0)
    bias = shape((2 * KV_EDGE, 2 * QG_EDGE * heads), f32)
    rim = shape((RIM_KEYS, RIM_QUERIES * heads), f32)
    points, gather_shape = places(heads)
    gather, spread, core_query, core_pair, top_bias, bottom_bias, left_bias, right_bias = near_call(
        functools.partial(core_kernel, extent),
        "core",
        [
            shape(gather_shape, bf16),
            shape((3 * count, count), bf16),
            shape((count, head_cols), bf16),
            shape((count, 2 * head_cols), f32),
            rim, rim, bias, bias,
        ],
        [SMEM] * 2 + [VMEM] * 3,
        row, col, kv, qg, points,
    )
    side = shape((KV_EDGE + QG_EDGE, 2 * head_cols), bf16)
    tall = [shape((lines * SIDE, 2 * head_cols), bf16) for lines in (WIDE, TALL)]
    leftward, rightward, kv_tall, qg_tall = near_call(
        edges_kernel,
        "edges",
        [side] * 2 + tall,
        [SMEM] + [VMEM] * 5,
        row, kv, qg, far, near, gather,
    )
    from_left = moved(rightward, "col", 1)
    from_right = moved(leftward, "col", -1)
    query_mid, pair_mid = near_call(
        middle_kernel,
        "middle",
        [shape((count, head_cols), bf16), shape((count, 2 * head_cols), f32)],
        [VMEM] * 8,
        kv_tall, qg_tall, top_bias, bottom_bias, gather, spread, core_query, core_pair,
    )
    own = count // tp
    right_query, right_pair = near_call(
        right_kernel,
        "right_side",
        [shape((QG_EDGE, head_cols), bf16), shape((OWN_EDGE, 2 * head_cols), f32)],
        [VMEM] * 3,
        rightward, from_right, right_bias,
    )
    partial = near_call(
        sides_kernel,
        "sides",
        shape((count, model_width), bf16),
        [VMEM] * 9,
        leftward, from_left, left_bias, right_query, right_pair, query_mid, pair_mid, spread,
        weight,
    )
    received = lax.all_to_all(partial.reshape(tp, own, model_width), "tp", 0, 0)
    result = near_call(
        finish_kernel,
        "finish",
        jax.ShapeDtypeStruct((own, model_width), f32),
        [SMEM] + [VMEM] * 4,
        place, received, flat_latent, gain, flat_cotangent,
    )
    return result.reshape(own // tile_cols, tile_cols, model_width)


def solution(mesh):
    placed = (P("row", "col", None), P(), P(None, None, "tp"), P("tp", None), P("row", "col", None))
    return jax.shard_map(
        per_device,
        mesh=mesh,
        in_specs=placed,
        out_specs=P(("row", "tp"), "col", None),
        check_vma=False,
    )
```

```python
import functools

import jax
import jax.numpy as jnp
import numpy as np
from jax import lax
from jax.experimental import pallas as pl
from jax.experimental.pallas import tpu as pltpu
from jax.sharding import PartitionSpec as P

HEAD_DIM = 64
RADIUS = 3
REACH = 2 * RADIUS
SIDE = 16
WIDE = SIDE + 2 * REACH
TALL = SIDE + 2 * RADIUS
KV_ROWS = REACH * SIDE
QG_ROWS = RADIUS * SIDE
KV_EDGE = 168
QG_EDGE = 72
INNER = range(RADIUS, SIDE - RADIUS)
ALONG = range(SIDE)
TOP = range(-RADIUS, RADIUS)
BOTTOM = range(SIDE - RADIUS, SIDE + RADIUS)
TOP_KEYS = range(-REACH, REACH)
BOTTOM_KEYS = range(SIDE - REACH, SIDE + REACH)
CORE_QUERIES = 128
RIM_QUERIES = 64
RIM_KEYS = 2 * REACH * SIDE
OWN_FROM = 32
OWN_EDGE = 112
FAR = 1000.0
LANES = 128
bf16 = jnp.bfloat16
f32 = jnp.float32
VMEM = pl.BlockSpec(memory_space=pltpu.VMEM)
HERE = pl.BlockSpec(memory_space=pltpu.VMEM)
SMEM = pl.BlockSpec(memory_space=pltpu.SMEM)
FAR_SPACE = pl.BlockSpec(memory_space=pltpu.HBM)
PARAMS = pltpu.CompilerParams(vmem_limit_bytes=32 * 1024 * 1024)


def in_hbm(block):
    return pltpu.with_memory_space_constraint(block, pltpu.HBM)


def near_call(kernel, name, outs, specs, *operands, scratch=()):
    fixed = [
        pltpu.with_memory_space_constraint(x, pltpu.VMEM) if spec is VMEM else x
        for x, spec in zip(operands, specs)
    ]
    places = [VMEM if spec is HERE else spec for spec in specs]
    return pl.pallas_call(
        kernel,
        out_shape=outs,
        in_specs=places,
        out_specs=jax.tree.map(lambda _: VMEM, outs),
        scratch_shapes=scratch,
        compiler_params=PARAMS,
        name=name,
    )(*fixed)


def nt(a, b):
    return lax.dot_general(a, b, (((1,), (1,)), ((), ())), preferred_element_type=f32)


def tn(a, b):
    return lax.dot_general(a, b, (((0,), (0,)), ((), ())), preferred_element_type=f32)


def nn(a, b):
    return jnp.dot(a, b, preferred_element_type=f32)


def strip_pairs(lines, count, first):
    return [
        (line * count + step, line * SIDE + first + step)
        for line in range(lines)
        for step in range(count)
    ]


def cells(rows, cols):
    return [(y, x) for y in rows for x in cols]


GATHERS = {
    "kv_edges": (0, 2 * KV_EDGE, WIDE * SIDE),
    "qg_edges": (2 * KV_EDGE, 2 * QG_EDGE, TALL * SIDE),
    "core": (2 * KV_EDGE + 2 * QG_EDGE, CORE_QUERIES, SIDE * SIDE),
    "rim": (2 * KV_EDGE + 2 * QG_EDGE + CORE_QUERIES, 2 * RIM_QUERIES, TALL * SIDE),
}
SPREADS = {
    "core": (0, SIDE * SIDE, CORE_QUERIES),
    "rim": (0, SIDE * SIDE, 2 * RIM_QUERIES, CORE_QUERIES),
    "keys": (SIDE * SIDE, SIDE * SIDE, 2 * OWN_EDGE),
    "queries": (2 * SIDE * SIDE, SIDE * SIDE, 2 * QG_EDGE),
}


def part_of(ref, spot):
    first, rows, cols, begin = (*spot, 0)[:4]
    return ref[first : first + rows, begin : begin + cols]


def gathers():
    pairs = []
    for part, first in enumerate((0, SIDE - REACH)):
        pairs += [(part * KV_EDGE + t, f) for t, f in strip_pairs(WIDE, REACH, first)]
    begin = GATHERS["qg_edges"][0]
    for part, first in enumerate((0, SIDE - RADIUS)):
        pairs += [(begin + part * QG_EDGE + t, f) for t, f in strip_pairs(TALL, RADIUS, first)]
    begin = GATHERS["core"][0]
    pairs += [(begin + t, y * SIDE + x) for t, (y, x) in enumerate(cells(INNER, INNER))]
    begin = GATHERS["rim"][0]
    for part, rows in enumerate((TOP, BOTTOM)):
        for t, (y, x) in enumerate(cells(rows, INNER)):
            pairs.append((begin + part * RIM_QUERIES + t, (y + RADIUS) * SIDE + x))
    sources = np.full((begin + 2 * RIM_QUERIES,), -1.0, np.float32)
    for target, source in pairs:
        sources[target] = source
    return sources


def spreads():
    pairs = []

    def add(name, column, token):
        if 0 <= token < SIDE * SIDE:
            pairs.append((SPREADS[name][0] + token, column))

    for t, (y, x) in enumerate(cells(INNER, INNER)):
        add("core", t, y * SIDE + x)
    for part, rows in enumerate((TOP, BOTTOM)):
        for t, (y, x) in enumerate(cells(rows, INNER)):
            add("rim", CORE_QUERIES + part * RIM_QUERIES + t, y * SIDE + x)
    for part, first in enumerate((0, SIDE - REACH)):
        for t, f in strip_pairs(WIDE, REACH, first):
            add("keys", part * OWN_EDGE + t - OWN_FROM, f - KV_ROWS)
    for part, first in enumerate((0, SIDE - RADIUS)):
        for t, f in strip_pairs(TALL, RADIUS, first):
            add("queries", part * QG_EDGE + t, f - QG_ROWS)
    targets = np.full((3, SIDE * SIDE), -1.0, np.float32)
    for target, column in pairs:
        targets[target // (SIDE * SIDE), column] = target % (SIDE * SIDE)
    return targets


def coords(rows, cols, total, pad):
    spots = cells(rows, cols)
    spots += [(pad, pad)] * (total - len(spots))
    return np.asarray(spots, np.float32).T


def places(heads):
    keys = [coords(ALONG, ALONG, SIDE * SIDE, FAR)]
    queries = [np.tile(coords(INNER, INNER, CORE_QUERIES, -FAR), (1, heads))]
    for rows, key_rows in ((TOP, TOP_KEYS), (BOTTOM, BOTTOM_KEYS)):
        keys.append(coords(key_rows, ALONG, RIM_KEYS, FAR))
        queries.append(np.tile(coords(rows, INNER, RIM_QUERIES, -FAR), (1, heads)))
    wide, tall = range(-REACH, SIDE + REACH), range(-RADIUS, SIDE + RADIUS)
    for key_firsts, query_firsts in (
        ((0, -REACH), (0, -RADIUS)),
        ((SIDE - REACH, SIDE), (SIDE - RADIUS, SIDE)),
    ):
        keys += [coords(wide, range(f, f + REACH), KV_EDGE, FAR) for f in key_firsts]
        both = [coords(tall, range(f, f + RADIUS), QG_EDGE, -FAR) for f in query_firsts]
        queries += [np.tile(part, (1, heads)) for part in both]
    keys, queries = np.concatenate(keys, axis=1), np.concatenate(queries, axis=1)
    joined = np.full((8, queries.shape[1]), FAR, np.float32)
    joined[:2, : keys.shape[1]] = keys
    joined[2:4] = queries
    sources = gathers()
    joined[4, : sources.shape[0]] = sources
    joined[5:, : SIDE * SIDE] = spreads()
    return jnp.asarray(joined), (sources.shape[0], WIDE * SIDE)


def project_kernel(
    row, col, place, latent_any, gain, weight_any, out_weight_any, cotangent_any, kv, qg, far, near,
    latent, weight, out_weight, cotangent, sems
):
    copies = [
        pltpu.make_async_copy(source, target, sems.at[i])
        for i, (source, target) in enumerate(
            (
                (latent_any, latent),
                (weight_any.at[1], weight.at[1]),
                (weight_any.at[2], weight.at[2]),
                (weight_any.at[0], weight.at[0]),
                (cotangent_any, cotangent),
                (out_weight_any, out_weight),
            )
        )
    ]
    for copy in copies:
        copy.start()
    width = out_weight.shape[0]
    copies[0].wait()
    tokens = latent[...].astype(f32)
    inverse = lax.rsqrt(jnp.mean(tokens * tokens, axis=-1, keepdims=True) + 1e-06)
    normed = (tokens * inverse * gain[...]).astype(bf16)
    copies[1].wait()
    copies[2].wait()
    kv[:, :width] = nn(normed, weight[1]).astype(bf16)
    kv[:, width:] = nn(normed, weight[2]).astype(bf16)
    for copy in copies[3:]:
        copy.wait()
    query = nn(normed, weight[0]).astype(bf16)
    qg[:, :width] = query * jnp.asarray(HEAD_DIM ** (-0.5), bf16)
    qg[:, width:] = nt(cotangent[...], out_weight[...]).astype(bf16)
    count = latent.shape[0]
    odd = lax.rem(row[0], 2)
    for strip, at_end in ((far, odd), (near, 1 - odd)):
        first = pl.multiple_of(at_end * (count - KV_ROWS), SIDE)
        strip[:KV_ROWS] = kv[pl.ds(first, KV_ROWS), :]
        first = pl.multiple_of(at_end * (count - QG_ROWS), SIDE)
        strip[KV_ROWS:] = qg[pl.ds(first, QG_ROWS), :]


def tall_blocks(row, kv, qg, far, near):
    odd = lax.rem(row[0], 2) == 1
    above = jnp.where(odd, near[...], far[...])
    below = jnp.where(odd, far[...], near[...])
    kv_all = jnp.concatenate([above[:KV_ROWS], kv[...], below[:KV_ROWS]], axis=0)
    qg_all = jnp.concatenate([above[KV_ROWS:], qg[...], below[KV_ROWS:]], axis=0)
    return kv_all, qg_all


def edges_kernel(row, col, kv, qg, far, near, gather, first, second, kv_tall, qg_tall):
    kv_all, qg_all = tall_blocks(row, kv, qg, far, near)
    kv_tall[...] = kv_all
    qg_tall[...] = qg_all
    kv_edges = nn(part_of(gather, GATHERS["kv_edges"]), kv_all).astype(bf16)
    qg_edges = nn(part_of(gather, GATHERS["qg_edges"]), qg_all).astype(bf16)
    left = jnp.concatenate([kv_edges[:KV_EDGE], qg_edges[:QG_EDGE]], axis=0)
    right = jnp.concatenate([kv_edges[KV_EDGE:], qg_edges[QG_EDGE:]], axis=0)
    odd = lax.rem(col[0], 2) == 1
    first[...] = jnp.where(odd, left, right)
    second[...] = jnp.where(odd, right, left)


def window_bias(spot, extent, keys, queries):
    key_y, key_x = keys[:, 0:1], keys[:, 1:2]
    top, left = (-(at * SIDE).astype(f32) for at in spot)
    bottom, right = ((((n - at) * SIDE) - 1).astype(f32) for at, n in zip(spot, extent))
    inside = (key_y >= top) & (key_y <= bottom) & (key_x >= left) & (key_x <= right)
    key_y = jnp.where(inside, key_y, FAR)
    apart = jnp.maximum(jnp.abs(key_y - queries[0:1, :]), jnp.abs(key_x - queries[1:2, :]))
    return jnp.where(apart <= RADIUS, 0.0, -1e30)


def by_head(block):
    width = block.shape[1]
    lanes = lax.broadcasted_iota(jnp.int32, (1, width), 1) // HEAD_DIM
    return [jnp.where(lanes == head, block, jnp.zeros_like(block)) for head in range(width // HEAD_DIM)]


def attention(bias, kv, groups, own):
    width = kv.shape[1] // 2
    key, value = kv[:, :width], kv[:, width:]
    query = jnp.concatenate([part for qg in groups for part in by_head(qg[:, :width])], axis=0)
    upstream = jnp.concatenate([part for qg in groups for part in by_head(qg[:, width:])], axis=0)
    scores = nt(key, query) + bias
    dots = nt(value, upstream)
    exponent = jnp.exp(scores - jnp.max(scores, axis=0, keepdims=True))
    scale = 1.0 / jnp.sum(exponent, axis=0, keepdims=True)
    weights = exponent * scale
    centre = jnp.sum(weights * dots, axis=0, keepdims=True)
    score_grads = (weights * (dots - centre)).astype(bf16)
    value_grad = nn(weights[own].astype(bf16), upstream)
    key_grad = nn(score_grads[own], query)
    count = groups[0].shape[0]
    heads = width // HEAD_DIM
    used = -(-count * heads // LANES) * LANES
    stacked = tn(score_grads[:, :used], key)
    lanes = lax.broadcasted_iota(jnp.int32, (1, width), 1) // HEAD_DIM
    query_grad = stacked[:count]
    for head in range(1, heads):
        part = stacked[head * count : (head + 1) * count]
        query_grad = jnp.where(lanes == head, part, query_grad)
    return query_grad * (HEAD_DIM ** (-0.5)), key_grad, value_grad


def core_kernel(
    extent, row, col, kv, qg, points, gather, spread, query_out, pair_out, *biases
):
    count = kv.shape[0]
    width = kv.shape[1] // 2
    spot = (row[0], col[0])
    columns = points[...].T
    keys, queries = columns[:, :2], points[2:4]
    picked = columns[: gather.shape[0], 4:5].astype(jnp.int32)
    sources = lax.broadcasted_iota(jnp.int32, gather.shape, 1)
    gather[...] = jnp.where(sources == picked, 1.0, 0.0).astype(bf16)
    tokens = lax.broadcasted_iota(jnp.int32, (count, count), 0)
    for part in range(3):
        targets = points[5 + part : 6 + part, :count].astype(jnp.int32)
        hits = jnp.where(tokens == targets, 1.0, 0.0).astype(bf16)
        spread[part * count : (part + 1) * count] = hits

    def mask(first_key, key_count, first_query, query_count):
        at_keys = keys[first_key : first_key + key_count]
        at_queries = queries[:, first_query : first_query + query_count]
        return window_bias(spot, extent, at_keys, at_queries)

    lanes = CORE_QUERIES * width // HEAD_DIM
    bias = mask(0, count, 0, lanes)
    inner = nn(part_of(gather, GATHERS["core"]), qg[...]).astype(bf16)
    query_grad, key_grad, value_grad = attention(bias, kv[...], [inner], slice(0, count))
    query_out[...] = nn(part_of(spread, SPREADS["core"]), query_grad.astype(bf16)).astype(bf16)
    pair_out[:, :width] = key_grad
    pair_out[:, width:] = value_grad
    first_key, first_query = count, lanes
    for side in biases[:2]:
        side[...] = mask(first_key, side.shape[0], first_query, side.shape[1])
        first_key, first_query = first_key + side.shape[0], first_query + side.shape[1]
    key_count, query_count = biases[2].shape
    left_keys = keys[first_key : first_key + key_count]
    right_keys = keys[first_key + key_count : first_key + 2 * key_count]
    left_queries = queries[:, first_query : first_query + query_count]
    right_queries = queries[:, first_query + query_count : first_query + 2 * query_count]
    odd = lax.rem(col[0], 2) == 1
    for side, flip in ((biases[2], odd), (biases[3], jnp.logical_not(odd))):
        at_keys = jnp.where(flip, left_keys, right_keys)
        at_queries = jnp.where(flip, left_queries, right_queries)
        side[...] = window_bias(spot, extent, at_keys, at_queries)


def middle_kernel(
    kv, qg, top_bias, bottom_bias, gather, spread, core_query, core_pair, query_out, pair_out
):
    width = query_out.shape[1]
    rim = nn(part_of(gather, GATHERS["rim"]), qg[...]).astype(bf16)
    near_rows = REACH * SIDE
    last = kv.shape[0] - RIM_KEYS
    top = attention(
        top_bias[...], kv[:RIM_KEYS], [rim[:RIM_QUERIES]], slice(near_rows, 2 * near_rows)
    )
    bottom = attention(bottom_bias[...], kv[last:], [rim[RIM_QUERIES:]], slice(0, near_rows))
    query_grad = jnp.concatenate([top[0], bottom[0]], axis=0).astype(bf16)
    scattered = nn(part_of(spread, SPREADS["rim"]), query_grad)
    query_out[...] = (scattered + core_query[...].astype(f32)).astype(bf16)
    between = jnp.zeros((SIDE * SIDE - 2 * near_rows, width), f32)
    for which, first in ((1, 0), (2, width)):
        grad = jnp.concatenate([top[which], between, bottom[which]], axis=0)
        pair_out[:, first : first + width] = grad + core_pair[:, first : first + width]


def side_grads(mine, theirs, bias):
    own = slice(OWN_FROM, OWN_FROM + OWN_EDGE)
    kv = jnp.concatenate([mine[:KV_EDGE], theirs[:KV_EDGE]], axis=0)
    groups = [mine[KV_EDGE:], theirs[KV_EDGE:]]
    query_grad, key_grad, value_grad = attention(bias[...], kv, groups, own)
    return query_grad.astype(bf16), jnp.concatenate([key_grad, value_grad], axis=1)


def first_side_kernel(mine, theirs, bias, query_out, pair_out):
    query_out[...], pair_out[...] = side_grads(mine, theirs, bias)


def sides_kernel(
    col, mine, theirs, bias, first_query, first_pair, query_mid, pair_mid, spread, weight, partial
):
    width = query_mid.shape[1]
    second_query, second_pair = side_grads(mine, theirs, bias)
    odd = lax.rem(col[0], 2) == 1
    queries = jnp.where(odd, first_query[...], second_query), jnp.where(odd, second_query, first_query[...])
    pairs = jnp.where(odd, first_pair[...], second_pair), jnp.where(odd, second_pair, first_pair[...])
    query_side = jnp.concatenate(queries, axis=0)
    pair_side = jnp.concatenate(pairs, axis=0)
    coarse = pair_side.astype(bf16)
    fine = (pair_side - coarse.astype(f32)).astype(bf16)
    key_spread, query_spread = (part_of(spread, SPREADS[name]) for name in ("keys", "queries"))
    pair = pair_mid[...] + (nn(key_spread, coarse) + nn(key_spread, fine))
    query_grad = query_mid[...].astype(f32) + nn(query_spread, query_side)
    pair = pair.astype(bf16)
    total = nt(query_grad.astype(bf16), weight[0])
    total += nt(pair[:, :width], weight[1])
    total += nt(pair[:, width:], weight[2])
    partial[...] = total.astype(bf16)


def finish_kernel(place, received, latent, gain, cotangent, result):
    count = received.shape[1]
    first = pl.multiple_of(place[0] * count, count)
    tokens = latent[pl.ds(first, count), :].astype(f32)
    upstream = cotangent[pl.ds(first, count), :].astype(f32)
    summed = received[0].astype(f32)
    for part in range(1, received.shape[0]):
        summed += received[part].astype(f32)
    inverse = lax.rsqrt(jnp.mean(tokens * tokens, axis=-1, keepdims=True) + 1e-06)
    unit = tokens * inverse
    scaled = summed * gain[...]
    stat = jnp.mean(scaled * unit, axis=-1, keepdims=True)
    result[...] = upstream + inverse * (scaled - unit * stat)


def paired(block, axis, first):
    count = lax.axis_size(axis)
    route = []
    for low in range(first, count - 1, 2):
        route += [(low, low + 1), (low + 1, low)]
    return lax.ppermute(block, axis, route)


def per_device(latent, norm_gain, qkv_weight, out_weight, cotangent):
    tile_rows, tile_cols, model_width = latent.shape
    head_cols = out_weight.shape[0]
    count = tile_rows * tile_cols
    tp = lax.axis_size("tp")
    flat_latent = latent.reshape(count, model_width)
    flat_cotangent = cotangent.reshape(count, model_width)
    gain = norm_gain.reshape(1, model_width)
    weight = qkv_weight.transpose(1, 0, 2)
    shape = pltpu.VMEM
    heads = head_cols // HEAD_DIM
    row = lax.axis_index("row").astype(jnp.int32).reshape(1)
    col = lax.axis_index("col").astype(jnp.int32).reshape(1)
    place = lax.axis_index("tp").astype(jnp.int32).reshape(1)
    extent = (lax.axis_size("row"), lax.axis_size("col"))
    edge = shape((KV_ROWS + QG_ROWS, 2 * head_cols), bf16)
    kv, qg, far, near = pl.pallas_call(
        project_kernel,
        out_shape=[shape((count, 2 * head_cols), bf16)] * 2 + [edge] * 2,
        in_specs=[SMEM, SMEM, SMEM, FAR_SPACE, HERE, FAR_SPACE, FAR_SPACE, FAR_SPACE],
        out_specs=[HERE] * 4,
        scratch_shapes=[
            pltpu.VMEM(flat_latent.shape, bf16),
            pltpu.VMEM(weight.shape, bf16),
            pltpu.VMEM(out_weight.shape, bf16),
            pltpu.VMEM(flat_cotangent.shape, bf16),
            pltpu.SemaphoreType.DMA((6,)),
        ],
        compiler_params=PARAMS,
        name="project",
    )(
        row,
        col,
        place,
        in_hbm(flat_latent),
        in_hbm(gain),
        in_hbm(weight),
        in_hbm(out_weight),
        in_hbm(flat_cotangent),
    )
    far = paired(far, "row", 1)
    near = paired(near, "row", 0)
    bias = shape((2 * KV_EDGE, 2 * QG_EDGE * heads), f32)
    rim = shape((RIM_KEYS, RIM_QUERIES * heads), f32)
    points, gather_shape = places(heads)
    gather, spread, core_query, core_pair, top_bias, bottom_bias, first_bias, second_bias = near_call(
        functools.partial(core_kernel, extent),
        "core",
        [
            shape(gather_shape, bf16),
            shape((3 * count, count), bf16),
            shape((count, head_cols), bf16),
            shape((count, 2 * head_cols), f32),
            rim, rim, bias, bias,
        ],
        [SMEM] * 2 + [VMEM] * 3,
        row, col, kv, qg, points,
    )
    side = shape((KV_EDGE + QG_EDGE, 2 * head_cols), bf16)
    tall = [shape((lines * SIDE, 2 * head_cols), bf16) for lines in (WIDE, TALL)]
    first, second, kv_tall, qg_tall = near_call(
        edges_kernel,
        "edges",
        [side] * 2 + tall,
        [SMEM] * 2 + [VMEM] * 5,
        row, col, kv, qg, far, near, gather,
    )
    first_theirs = paired(first, "col", 0)
    second_theirs = paired(second, "col", 1)
    query_mid, pair_mid = near_call(
        middle_kernel,
        "middle",
        [shape((count, head_cols), bf16), shape((count, 2 * head_cols), f32)],
        [VMEM] * 8,
        kv_tall, qg_tall, top_bias, bottom_bias, gather, spread, core_query, core_pair,
    )
    own = count // tp
    first_query, first_pair = near_call(
        first_side_kernel,
        "first_side",
        [shape((QG_EDGE, head_cols), bf16), shape((OWN_EDGE, 2 * head_cols), f32)],
        [VMEM] * 3,
        first, first_theirs, first_bias,
    )
    partial = near_call(
        sides_kernel,
        "sides",
        shape((count, model_width), bf16),
        [SMEM] + [VMEM] * 9,
        col, second, second_theirs, second_bias, first_query, first_pair, query_mid, pair_mid,
        spread, weight,
    )
    received = lax.all_to_all(partial.reshape(tp, own, model_width), "tp", 0, 0)
    result = near_call(
        finish_kernel,
        "finish",
        jax.ShapeDtypeStruct((own, model_width), f32),
        [SMEM] + [VMEM] * 4,
        place, received, flat_latent, gain, flat_cotangent,
    )
    return result.reshape(own // tile_cols, tile_cols, model_width)


def solution(mesh):
    placed = (P("row", "col", None), P(), P(None, None, "tp"), P("tp", None), P("row", "col", None))
    return jax.shard_map(
        per_device,
        mesh=mesh,
        in_specs=placed,
        out_specs=P(("row", "tp"), "col", None),
        check_vma=False,
    )
```

```python
import functools

import jax
import jax.numpy as jnp
import numpy as np
from jax import lax
from jax.experimental import pallas as pl
from jax.experimental.pallas import tpu as pltpu
from jax.sharding import PartitionSpec as P

HEAD_DIM = 64
RADIUS = 3
REACH = 2 * RADIUS
SIDE = 16
WIDE = SIDE + 2 * REACH
TALL = SIDE + 2 * RADIUS
KV_ROWS = REACH * SIDE
QG_ROWS = RADIUS * SIDE
KV_EDGE = 168
QG_EDGE = 72
INNER = range(RADIUS, SIDE - RADIUS)
ALONG = range(SIDE)
TOP = range(-RADIUS, RADIUS)
BOTTOM = range(SIDE - RADIUS, SIDE + RADIUS)
TOP_KEYS = range(-REACH, REACH)
BOTTOM_KEYS = range(SIDE - REACH, SIDE + REACH)
CORE_QUERIES = 128
RIM_QUERIES = 64
RIM_KEYS = 2 * REACH * SIDE
OWN_FROM = 32
OWN_EDGE = 112
FAR = 1000.0
LANES = 128
bf16 = jnp.bfloat16
f32 = jnp.float32
VMEM = pl.BlockSpec(memory_space=pltpu.VMEM)
HERE = pl.BlockSpec(memory_space=pltpu.VMEM)
SMEM = pl.BlockSpec(memory_space=pltpu.SMEM)
FAR_SPACE = pl.BlockSpec(memory_space=pltpu.HBM)
PARAMS = pltpu.CompilerParams(vmem_limit_bytes=32 * 1024 * 1024)


def in_hbm(block):
    return pltpu.with_memory_space_constraint(block, pltpu.HBM)


def near_call(kernel, name, outs, specs, *operands, scratch=()):
    fixed = [
        pltpu.with_memory_space_constraint(x, pltpu.VMEM) if spec is VMEM else x
        for x, spec in zip(operands, specs)
    ]
    places = [VMEM if spec is HERE else spec for spec in specs]
    return pl.pallas_call(
        kernel,
        out_shape=outs,
        in_specs=places,
        out_specs=jax.tree.map(lambda _: VMEM, outs),
        scratch_shapes=scratch,
        compiler_params=PARAMS,
        name=name,
    )(*fixed)


def nt(a, b):
    return lax.dot_general(a, b, (((1,), (1,)), ((), ())), preferred_element_type=f32)


def tn(a, b):
    return lax.dot_general(a, b, (((0,), (0,)), ((), ())), preferred_element_type=f32)


def nn(a, b):
    return jnp.dot(a, b, preferred_element_type=f32)


def strip_pairs(lines, count, first):
    return [
        (line * count + step, line * SIDE + first + step)
        for line in range(lines)
        for step in range(count)
    ]


def cells(rows, cols):
    return [(y, x) for y in rows for x in cols]


GATHERS = {
    "kv_edges": (0, 2 * KV_EDGE, WIDE * SIDE),
    "qg_edges": (2 * KV_EDGE, 2 * QG_EDGE, TALL * SIDE),
    "core": (2 * KV_EDGE + 2 * QG_EDGE, CORE_QUERIES, SIDE * SIDE),
    "rim": (2 * KV_EDGE + 2 * QG_EDGE + CORE_QUERIES, 2 * RIM_QUERIES, TALL * SIDE),
}
SPREADS = {
    "core": (0, SIDE * SIDE, CORE_QUERIES),
    "rim": (0, SIDE * SIDE, 2 * RIM_QUERIES, CORE_QUERIES),
    "keys": (SIDE * SIDE, SIDE * SIDE, 2 * OWN_EDGE),
    "queries": (2 * SIDE * SIDE, SIDE * SIDE, 2 * QG_EDGE),
}


def part_of(ref, spot):
    first, rows, cols, begin = (*spot, 0)[:4]
    return ref[first : first + rows, begin : begin + cols]


def gathers():
    pairs = []
    for part, first in enumerate((0, SIDE - REACH)):
        pairs += [(part * KV_EDGE + t, f) for t, f in strip_pairs(WIDE, REACH, first)]
    begin = GATHERS["qg_edges"][0]
    for part, first in enumerate((0, SIDE - RADIUS)):
        pairs += [(begin + part * QG_EDGE + t, f) for t, f in strip_pairs(TALL, RADIUS, first)]
    begin = GATHERS["core"][0]
    pairs += [(begin + t, y * SIDE + x) for t, (y, x) in enumerate(cells(INNER, INNER))]
    begin = GATHERS["rim"][0]
    for part, rows in enumerate((TOP, BOTTOM)):
        for t, (y, x) in enumerate(cells(rows, INNER)):
            pairs.append((begin + part * RIM_QUERIES + t, (y + RADIUS) * SIDE + x))
    sources = np.full((begin + 2 * RIM_QUERIES,), -1.0, np.float32)
    for target, source in pairs:
        sources[target] = source
    return sources


def spreads():
    pairs = []

    def add(name, column, token):
        if 0 <= token < SIDE * SIDE:
            pairs.append((SPREADS[name][0] + token, column))

    for t, (y, x) in enumerate(cells(INNER, INNER)):
        add("core", t, y * SIDE + x)
    for part, rows in enumerate((TOP, BOTTOM)):
        for t, (y, x) in enumerate(cells(rows, INNER)):
            add("rim", CORE_QUERIES + part * RIM_QUERIES + t, y * SIDE + x)
    for part, first in enumerate((0, SIDE - REACH)):
        for t, f in strip_pairs(WIDE, REACH, first):
            add("keys", part * OWN_EDGE + t - OWN_FROM, f - KV_ROWS)
    for part, first in enumerate((0, SIDE - RADIUS)):
        for t, f in strip_pairs(TALL, RADIUS, first):
            add("queries", part * QG_EDGE + t, f - QG_ROWS)
    targets = np.full((3, SIDE * SIDE), -1.0, np.float32)
    for target, column in pairs:
        targets[target // (SIDE * SIDE), column] = target % (SIDE * SIDE)
    return targets


def coords(rows, cols, total, pad):
    spots = cells(rows, cols)
    spots += [(pad, pad)] * (total - len(spots))
    return np.asarray(spots, np.float32).T


def places(heads):
    keys = [coords(ALONG, ALONG, SIDE * SIDE, FAR)]
    queries = [np.tile(coords(INNER, INNER, CORE_QUERIES, -FAR), (1, heads))]
    for rows, key_rows in ((TOP, TOP_KEYS), (BOTTOM, BOTTOM_KEYS)):
        keys.append(coords(key_rows, ALONG, RIM_KEYS, FAR))
        queries.append(np.tile(coords(rows, INNER, RIM_QUERIES, -FAR), (1, heads)))
    wide, tall = range(-REACH, SIDE + REACH), range(-RADIUS, SIDE + RADIUS)
    for key_firsts, query_firsts in (
        ((0, -REACH), (0, -RADIUS)),
        ((SIDE - REACH, SIDE), (SIDE - RADIUS, SIDE)),
    ):
        keys += [coords(wide, range(f, f + REACH), KV_EDGE, FAR) for f in key_firsts]
        both = [coords(tall, range(f, f + RADIUS), QG_EDGE, -FAR) for f in query_firsts]
        queries += [np.tile(part, (1, heads)) for part in both]
    keys, queries = np.concatenate(keys, axis=1), np.concatenate(queries, axis=1)
    joined = np.full((8, queries.shape[1]), FAR, np.float32)
    joined[:2, : keys.shape[1]] = keys
    joined[2:4] = queries
    sources = gathers()
    joined[4, : sources.shape[0]] = sources
    joined[5:, : SIDE * SIDE] = spreads()
    return jnp.asarray(joined), (sources.shape[0], WIDE * SIDE)


def project_kernel(
    row, col, place, latent_any, gain, weight_any, out_weight_any, cotangent_any, kv, qg, far, near,
    latent, weight, out_weight, cotangent, sems
):
    copies = [
        pltpu.make_async_copy(source, target, sems.at[i])
        for i, (source, target) in enumerate(
            (
                (latent_any, latent),
                (weight_any.at[1], weight.at[1]),
                (weight_any.at[2], weight.at[2]),
                (weight_any.at[0], weight.at[0]),
                (cotangent_any, cotangent),
                (out_weight_any, out_weight),
            )
        )
    ]
    for copy in copies:
        copy.start()
    width = out_weight.shape[0]
    copies[0].wait()
    tokens = latent[...].astype(f32)
    inverse = lax.rsqrt(jnp.mean(tokens * tokens, axis=-1, keepdims=True) + 1e-06)
    normed = (tokens * inverse * gain[...]).astype(bf16)
    copies[1].wait()
    copies[2].wait()
    kv[:, :width] = nn(normed, weight[1]).astype(bf16)
    kv[:, width:] = nn(normed, weight[2]).astype(bf16)
    for copy in copies[3:]:
        copy.wait()
    query = nn(normed, weight[0]).astype(bf16)
    qg[:, :width] = query * jnp.asarray(HEAD_DIM ** (-0.5), bf16)
    qg[:, width:] = nt(cotangent[...], out_weight[...]).astype(bf16)
    count = latent.shape[0]
    odd = lax.rem(row[0], 2)
    for strip, at_end in ((far, odd), (near, 1 - odd)):
        first = pl.multiple_of(at_end * (count - KV_ROWS), SIDE)
        strip[:KV_ROWS] = kv[pl.ds(first, KV_ROWS), :]
        first = pl.multiple_of(at_end * (count - QG_ROWS), SIDE)
        strip[KV_ROWS:] = qg[pl.ds(first, QG_ROWS), :]


def tall_blocks(row, kv, qg, far, near):
    odd = lax.rem(row[0], 2) == 1
    above = jnp.where(odd, near[...], far[...])
    below = jnp.where(odd, far[...], near[...])
    kv_all = jnp.concatenate([above[:KV_ROWS], kv[...], below[:KV_ROWS]], axis=0)
    qg_all = jnp.concatenate([above[KV_ROWS:], qg[...], below[KV_ROWS:]], axis=0)
    return kv_all, qg_all


def edges_kernel(row, kv, qg, far, near, gather, left, right, kv_tall, qg_tall):
    kv_all, qg_all = tall_blocks(row, kv, qg, far, near)
    kv_tall[...] = kv_all
    qg_tall[...] = qg_all
    kv_edges = nn(part_of(gather, GATHERS["kv_edges"]), kv_all).astype(bf16)
    qg_edges = nn(part_of(gather, GATHERS["qg_edges"]), qg_all).astype(bf16)
    left[:KV_EDGE] = kv_edges[:KV_EDGE]
    left[KV_EDGE:] = qg_edges[:QG_EDGE]
    right[:KV_EDGE] = kv_edges[KV_EDGE:]
    right[KV_EDGE:] = qg_edges[QG_EDGE:]


def window_bias(spot, extent, keys, queries):
    key_y, key_x = keys[:, 0:1], keys[:, 1:2]
    top, left = (-(at * SIDE).astype(f32) for at in spot)
    bottom, right = ((((n - at) * SIDE) - 1).astype(f32) for at, n in zip(spot, extent))
    inside = (key_y >= top) & (key_y <= bottom) & (key_x >= left) & (key_x <= right)
    key_y = jnp.where(inside, key_y, FAR)
    apart = jnp.maximum(jnp.abs(key_y - queries[0:1, :]), jnp.abs(key_x - queries[1:2, :]))
    return jnp.where(apart <= RADIUS, 0.0, -1e30)


def by_head(block):
    width = block.shape[1]
    lanes = lax.broadcasted_iota(jnp.int32, (1, width), 1) // HEAD_DIM
    return [jnp.where(lanes == head, block, jnp.zeros_like(block)) for head in range(width // HEAD_DIM)]


def attention(bias, kv, groups, own):
    width = kv.shape[1] // 2
    key, value = kv[:, :width], kv[:, width:]
    query = jnp.concatenate([part for qg in groups for part in by_head(qg[:, :width])], axis=0)
    upstream = jnp.concatenate([part for qg in groups for part in by_head(qg[:, width:])], axis=0)
    scores = nt(key, query) + bias
    dots = nt(value, upstream)
    exponent = jnp.exp(scores - jnp.max(scores, axis=0, keepdims=True))
    scale = 1.0 / jnp.sum(exponent, axis=0, keepdims=True)
    weights = exponent * scale
    centre = jnp.sum(weights * dots, axis=0, keepdims=True)
    score_grads = (weights * (dots - centre)).astype(bf16)
    value_grad = nn(weights[own].astype(bf16), upstream)
    key_grad = nn(score_grads[own], query)
    count = groups[0].shape[0]
    heads = width // HEAD_DIM
    used = -(-count * heads // LANES) * LANES
    stacked = tn(score_grads[:, :used], key)
    lanes = lax.broadcasted_iota(jnp.int32, (1, width), 1) // HEAD_DIM
    query_grad = stacked[:count]
    for head in range(1, heads):
        part = stacked[head * count : (head + 1) * count]
        query_grad = jnp.where(lanes == head, part, query_grad)
    return query_grad * (HEAD_DIM ** (-0.5)), key_grad, value_grad


def core_kernel(
    extent, row, col, kv, qg, points, gather, spread, query_out, pair_out, *biases
):
    count = kv.shape[0]
    width = kv.shape[1] // 2
    spot = (row[0], col[0])
    columns = points[...].T
    keys, queries = columns[:, :2], points[2:4]
    picked = columns[: gather.shape[0], 4:5].astype(jnp.int32)
    sources = lax.broadcasted_iota(jnp.int32, gather.shape, 1)
    gather[...] = jnp.where(sources == picked, 1.0, 0.0).astype(bf16)
    tokens = lax.broadcasted_iota(jnp.int32, (count, count), 0)
    for part in range(3):
        targets = points[5 + part : 6 + part, :count].astype(jnp.int32)
        hits = jnp.where(tokens == targets, 1.0, 0.0).astype(bf16)
        spread[part * count : (part + 1) * count] = hits

    def mask(first_key, key_count, first_query, query_count):
        at_keys = keys[first_key : first_key + key_count]
        at_queries = queries[:, first_query : first_query + query_count]
        return window_bias(spot, extent, at_keys, at_queries)

    lanes = CORE_QUERIES * width // HEAD_DIM
    bias = mask(0, count, 0, lanes)
    inner = nn(part_of(gather, GATHERS["core"]), qg[...]).astype(bf16)
    query_grad, key_grad, value_grad = attention(bias, kv[...], [inner], slice(0, count))
    query_out[...] = nn(part_of(spread, SPREADS["core"]), query_grad.astype(bf16)).astype(bf16)
    pair_out[:, :width] = key_grad
    pair_out[:, width:] = value_grad
    first_key, first_query = count, lanes
    for side in biases:
        side[...] = mask(first_key, side.shape[0], first_query, side.shape[1])
        first_key, first_query = first_key + side.shape[0], first_query + side.shape[1]


def middle_kernel(
    kv, qg, top_bias, bottom_bias, gather, spread, core_query, core_pair, query_out, pair_out
):
    width = query_out.shape[1]
    rim = nn(part_of(gather, GATHERS["rim"]), qg[...]).astype(bf16)
    near_rows = REACH * SIDE
    last = kv.shape[0] - RIM_KEYS
    top = attention(
        top_bias[...], kv[:RIM_KEYS], [rim[:RIM_QUERIES]], slice(near_rows, 2 * near_rows)
    )
    bottom = attention(bottom_bias[...], kv[last:], [rim[RIM_QUERIES:]], slice(0, near_rows))
    query_grad = jnp.concatenate([top[0], bottom[0]], axis=0).astype(bf16)
    scattered = nn(part_of(spread, SPREADS["rim"]), query_grad)
    query_out[...] = (scattered + core_query[...].astype(f32)).astype(bf16)
    between = jnp.zeros((SIDE * SIDE - 2 * near_rows, width), f32)
    for which, first in ((1, 0), (2, width)):
        grad = jnp.concatenate([top[which], between, bottom[which]], axis=0)
        pair_out[:, first : first + width] = grad + core_pair[:, first : first + width]


def side_grads(mine, theirs, bias):
    own = slice(OWN_FROM, OWN_FROM + OWN_EDGE)
    kv = jnp.concatenate([mine[:KV_EDGE], theirs[:KV_EDGE]], axis=0)
    groups = [mine[KV_EDGE:], theirs[KV_EDGE:]]
    query_grad, key_grad, value_grad = attention(bias[...], kv, groups, own)
    return query_grad.astype(bf16), jnp.concatenate([key_grad, value_grad], axis=1)


def right_kernel(rightward, from_right, right_bias, query_out, pair_out):
    query_out[...], pair_out[...] = side_grads(rightward, from_right, right_bias)


def sides_kernel(
    leftward, from_left, left_bias, right_query, right_pair, query_mid, pair_mid, spread, weight,
    partial
):
    width = query_mid.shape[1]
    left_query, left_pair = side_grads(leftward, from_left, left_bias)
    query_side = jnp.concatenate([left_query, right_query[...]], axis=0)
    pair_side = jnp.concatenate([left_pair, right_pair[...]], axis=0)
    key_spread, query_spread = (part_of(spread, SPREADS[name]) for name in ("keys", "queries"))
    pair = pair_mid[...] + nn(key_spread, pair_side.astype(bf16))
    query_grad = query_mid[...].astype(f32) + nn(query_spread, query_side)
    pair = pair.astype(bf16)
    total = nt(query_grad.astype(bf16), weight[0])
    total += nt(pair[:, :width], weight[1])
    total += nt(pair[:, width:], weight[2])
    partial[...] = total.astype(bf16)


def finish_kernel(place, received, latent, gain, cotangent, result):
    count = received.shape[1]
    first = pl.multiple_of(place[0] * count, count)
    tokens = latent[pl.ds(first, count), :].astype(f32)
    upstream = cotangent[pl.ds(first, count), :].astype(f32)
    summed = received[0].astype(f32)
    for part in range(1, received.shape[0]):
        summed += received[part].astype(f32)
    inverse = lax.rsqrt(jnp.mean(tokens * tokens, axis=-1, keepdims=True) + 1e-06)
    unit = tokens * inverse
    scaled = summed * gain[...]
    stat = jnp.mean(scaled * unit, axis=-1, keepdims=True)
    result[...] = upstream + inverse * (scaled - unit * stat)


def paired(block, axis, first):
    count = lax.axis_size(axis)
    route = []
    for low in range(first, count - 1, 2):
        route += [(low, low + 1), (low + 1, low)]
    return lax.ppermute(block, axis, route)


def moved(block, axis, distance):
    count = lax.axis_size(axis)
    route = [(i, i + distance) for i in range(count) if 0 <= i + distance < count]
    return lax.ppermute(block, axis, route)


def per_device(latent, norm_gain, qkv_weight, out_weight, cotangent):
    tile_rows, tile_cols, model_width = latent.shape
    head_cols = out_weight.shape[0]
    count = tile_rows * tile_cols
    tp = lax.axis_size("tp")
    flat_latent = latent.reshape(count, model_width)
    flat_cotangent = cotangent.reshape(count, model_width)
    gain = norm_gain.reshape(1, model_width)
    weight = qkv_weight.transpose(1, 0, 2)
    shape = pltpu.VMEM
    heads = head_cols // HEAD_DIM
    row = lax.axis_index("row").astype(jnp.int32).reshape(1)
    col = lax.axis_index("col").astype(jnp.int32).reshape(1)
    place = lax.axis_index("tp").astype(jnp.int32).reshape(1)
    extent = (lax.axis_size("row"), lax.axis_size("col"))
    edge = shape((KV_ROWS + QG_ROWS, 2 * head_cols), bf16)
    kv, qg, far, near = pl.pallas_call(
        project_kernel,
        out_shape=[shape((count, 2 * head_cols), bf16)] * 2 + [edge] * 2,
        in_specs=[SMEM, SMEM, SMEM, FAR_SPACE, HERE, FAR_SPACE, FAR_SPACE, FAR_SPACE],
        out_specs=[HERE] * 4,
        scratch_shapes=[
            pltpu.VMEM(flat_latent.shape, bf16),
            pltpu.VMEM(weight.shape, bf16),
            pltpu.VMEM(out_weight.shape, bf16),
            pltpu.VMEM(flat_cotangent.shape, bf16),
            pltpu.SemaphoreType.DMA((6,)),
        ],
        compiler_params=PARAMS,
        name="project",
    )(
        row,
        col,
        place,
        in_hbm(flat_latent),
        in_hbm(gain),
        in_hbm(weight),
        in_hbm(out_weight),
        in_hbm(flat_cotangent),
    )
    far = paired(far, "row", 1)
    near = paired(near, "row", 0)
    bias = shape((2 * KV_EDGE, 2 * QG_EDGE * heads), f32)
    rim = shape((RIM_KEYS, RIM_QUERIES * heads), f32)
    points, gather_shape = places(heads)
    gather, spread, core_query, core_pair, top_bias, bottom_bias, left_bias, right_bias = near_call(
        functools.partial(core_kernel, extent),
        "core",
        [
            shape(gather_shape, bf16),
            shape((3 * count, count), bf16),
            shape((count, head_cols), bf16),
            shape((count, 2 * head_cols), f32),
            rim, rim, bias, bias,
        ],
        [SMEM] * 2 + [VMEM] * 3,
        row, col, kv, qg, points,
    )
    side = shape((KV_EDGE + QG_EDGE, 2 * head_cols), bf16)
    tall = [shape((lines * SIDE, 2 * head_cols), bf16) for lines in (WIDE, TALL)]
    leftward, rightward, kv_tall, qg_tall = near_call(
        edges_kernel,
        "edges",
        [side] * 2 + tall,
        [SMEM] + [VMEM] * 5,
        row, kv, qg, far, near, gather,
    )
    from_left = moved(rightward, "col", 1)
    from_right = moved(leftward, "col", -1)
    query_mid, pair_mid = near_call(
        middle_kernel,
        "middle",
        [shape((count, head_cols), bf16), shape((count, 2 * head_cols), f32)],
        [VMEM] * 8,
        kv_tall, qg_tall, top_bias, bottom_bias, gather, spread, core_query, core_pair,
    )
    own = count // tp
    right_query, right_pair = near_call(
        right_kernel,
        "right_side",
        [shape((QG_EDGE, head_cols), bf16), shape((OWN_EDGE, 2 * head_cols), f32)],
        [VMEM] * 3,
        rightward, from_right, right_bias,
    )
    partial = near_call(
        sides_kernel,
        "sides",
        shape((count, model_width), bf16),
        [VMEM] * 9,
        leftward, from_left, left_bias, right_query, right_pair, query_mid, pair_mid, spread,
        weight,
    )
    received = lax.all_to_all(partial.reshape(tp, own, model_width), "tp", 0, 0)
    result = near_call(
        finish_kernel,
        "finish",
        jax.ShapeDtypeStruct((own, model_width), f32),
        [SMEM] + [VMEM] * 4,
        place, received, flat_latent, gain, flat_cotangent,
    )
    return result.reshape(own // tile_cols, tile_cols, model_width)


def solution(mesh):
    placed = (P("row", "col", None), P(), P(None, None, "tp"), P("tp", None), P("row", "col", None))
    return jax.shard_map(
        per_device,
        mesh=mesh,
        in_specs=placed,
        out_specs=P(("row", "tp"), "col", None),
        check_vma=False,
    )
```
